128 devices in a mesh: dp: 8 (over y, core), queue: 16 (over z, x).
Axes of the slice: x: 4, y: 4, z: 4, core: 2. Of those that a mesh axis runs over, the one named last changes fastest.
Arguments:
- queue_keys: bfloat16 [524288, 768], P(('dp', 'queue')), may hold values from -2.5 to 2.5
- fresh_keys: bfloat16 [1024, 768], P(('dp', 'queue')), may hold values from -4 to 4
- slots: int32 [1024], P(('dp', 'queue')), may hold values from 0 to 524287, as said below
- queries: bfloat16 [1024, 768], P('dp'), may hold values from -40 to 40
- positives: int32 [1024], P('dp'), may hold values from 0 to 1023
Outputs:
- query_grad: float32 [1024, 768], P(('dp', 'queue'))
- mean_loss: float32 [], replicated
- new_queue: bfloat16 [524288, 768], P(('dp', 'queue'))
The draws below stay inside these ranges and needn't reach their ends.
Inputs may be any that keep to these rules, and one draw needn't show every extreme that they name: The 1024 slots are distinct.
All inputs are finite; a program needn't handle non-finite values.
Results may differ from the reference program's by a relative error of at most 0.0035.
Values may be sent and summed in bfloat16 or wider, within the bound.
A program may use at most 128 MiB of HBM per device.

```python
import math
import jax
import jax.numpy as jnp
from jax import lax

D = 768
QUEUE = 524288
NQ = 1024
NEW = 1024


def shared_fresh(key):
    noise = jnp.clip(jax.random.normal(jax.random.fold_in(key, 11), (NEW, D), jnp.float32), -4.0, 4.0)
    fresh_rows = noise * (4.2 / math.sqrt(D))
    return fresh_rows


def draw_fresh_keys(key, part):
    return shared_fresh(key).astype(jnp.bfloat16)


def draw_queries(key, part):
    values = jnp.clip(jax.random.normal(jax.random.fold_in(key, 23), (NQ, D), jnp.float32), -4.0, 4.0)
    return values.astype(jnp.bfloat16)


def draw_queue_keys(key, part):
    position = (jnp.arange(QUEUE, dtype=jnp.float32) / QUEUE)[:, None]
    noise = jnp.clip(jax.random.normal(jax.random.fold_in(key, 37), (QUEUE, D), jnp.float32), -4.0, 4.0)
    return (noise * ((4.0 + 0.35 * position) / math.sqrt(D))).astype(jnp.bfloat16)


def draw_slots(key, part):
    chosen = jax.random.permutation(jax.random.fold_in(key, 41), QUEUE - 2)[:NEW - 2] + 1
    extremes = jnp.array([0, QUEUE - 1], jnp.int32)
    joined = jnp.concatenate([extremes, chosen.astype(jnp.int32)])
    reorder = jax.random.permutation(jax.random.fold_in(key, 43), NEW)
    return joined[reorder]


def touch_ends(values, key, least, top_value):
    longest = values.shape.index(max(values.shape))
    spots = []
    for shift in (0, 1):
        where = [jax.random.randint(jax.random.fold_in(key, axis), (), 0, length) for axis, length in enumerate(values.shape)]
        where[longest] = (where[longest] + shift) % values.shape[longest]
        spots.append(tuple(where))
    return values.at[spots[0]].set(least).at[spots[1]].set(top_value)


def setup_inputs(seed: int = 0) -> dict:
    seeds = jax.random.split(jax.random.key(seed), 6)
    queue_keys = draw_queue_keys(jax.random.fold_in(seeds[5], 71), 0)
    fresh_keys = draw_fresh_keys(jax.random.fold_in(seeds[5], 71), 0)
    slots = draw_slots(jax.random.fold_in(seeds[5], 71), 0)
    queries = draw_queries(jax.random.fold_in(seeds[5], 71), 0)
    positives = touch_ends(jax.random.randint(seeds[4], (NQ,), 0, NEW), jax.random.fold_in(seeds[4], 1), 0, NEW - 1).astype(jnp.int32)
    return {"queue_keys": queue_keys, "fresh_keys": fresh_keys, "slots": slots, "queries": queries, "positives": positives}


def reference(queue_keys, fresh_keys, slots, queries, positives):
    key_rows = jnp.concatenate([queue_keys, fresh_keys], axis=0)
    query_blocks = queries.reshape(NQ // 32, 32, D)

    def one_block(query_block):
        scores = lax.dot_general(query_block, key_rows, (((1,), (1,)), ((), ())), preferred_element_type=jnp.float32)
        row_top = jnp.max(scores, axis=1)
        expsum = jnp.exp(scores - row_top[:, None])
        sum_exp = jnp.sum(expsum, axis=1)
        weights = expsum.astype(jnp.bfloat16)
        pulled = jnp.dot(weights, key_rows, preferred_element_type=jnp.float32)
        return row_top, sum_exp, pulled

    row_tops, sum_exps, pulled = lax.map(one_block, query_blocks)
    row_tops = row_tops.reshape(NQ)
    sum_exps = sum_exps.reshape(NQ)
    pulled = pulled.reshape(NQ, D)
    positive_keys = jnp.take(fresh_keys, positives, axis=0).astype(jnp.float32)
    query_grad = pulled / sum_exps[:, None] - positive_keys
    positive_scores = jnp.sum(queries.astype(jnp.float32) * positive_keys, axis=1)
    mean_loss = jnp.mean(row_tops + jnp.log(sum_exps) - positive_scores)
    new_queue = queue_keys.at[slots].set(fresh_keys)
    return query_grad, mean_loss, new_queue
```

```python
import functools

import jax
import jax.numpy as jnp
from jax import lax
from jax.experimental import pallas as pl
from jax.experimental.pallas import tpu as pltpu
from jax.sharding import PartitionSpec as P

MESH = pl.DeviceIdType.MESH
STAT = 128


def score_rows(query_rows, key_rows):
    return lax.dot_general(
        query_rows, key_rows, (((1,), (1,)), ((), ())), preferred_element_type=jnp.float32
    )


def _device_index():
    return lax.axis_index("dp") * lax.axis_size("queue") + lax.axis_index("queue")


def _greet_all(n, q, me):
    barrier = pltpu.get_barrier_semaphore()

    def signal(k, carry):
        dst = lax.rem(me + k, n)
        pl.semaphore_signal(
            barrier, inc=1, device_id=(dst // q, lax.rem(dst, q)), device_id_type=MESH
        )
        return carry

    lax.fori_loop(1, n, signal, 0)
    pl.semaphore_wait(barrier, n - 1)


def _send_all(n, q, me, src_of, buf, send_sem, recv_sem):
    def send(k, carry):
        dst = lax.rem(me + k, n)
        pltpu.make_async_remote_copy(
            src_ref=src_of(dst),
            dst_ref=buf.at[me],
            send_sem=send_sem,
            recv_sem=recv_sem,
            device_id=(dst // q, lax.rem(dst, q)),
            device_id_type=MESH,
        ).start()
        return carry

    lax.fori_loop(1, n, send, 0)


def _wait_all(n, q, me, src_all, buf, send_sem, recv_sem):
    total = pltpu.make_async_remote_copy(
        src_ref=src_all.at[pl.ds(0, n - 1)],
        dst_ref=buf.at[pl.ds(0, n - 1)],
        send_sem=send_sem,
        recv_sem=recv_sem,
        device_id=(lax.rem(me + 1, n) // q, lax.rem(lax.rem(me + 1, n), q)),
        device_id_type=MESH,
    )
    total.wait_send()
    total.wait_recv()


def combine_kernel(n, q, d, x_ref, o_ref, buf, send_sem, recv_sem, local_sem):
    me = _device_index()
    _greet_all(n, q, me)
    _send_all(n, q, me, lambda dst: x_ref.at[dst], buf, send_sem, recv_sem)
    mine = pltpu.make_async_copy(x_ref.at[me], buf.at[me], local_sem)
    mine.start()
    mine.wait()
    _wait_all(n, q, me, x_ref, buf, send_sem, recv_sem)

    def top(j, m):
        return jnp.maximum(m, buf[j][:, d:d + 1])

    row_top = lax.fori_loop(0, n, top, jnp.full((o_ref.shape[0], 1), -jnp.inf, jnp.float32))

    def add(j, acc):
        b = buf[j]
        scale = jnp.exp(b[:, d:d + 1] - row_top)
        return acc + b * scale

    acc = lax.fori_loop(0, n, add, jnp.zeros(o_ref.shape, jnp.float32))
    col = lax.broadcasted_iota(jnp.int32, o_ref.shape, 1)
    o_ref[...] = jnp.where(col == d, row_top, acc)


def combine(x, n, q, d):
    rows = x.shape[1]
    width = x.shape[2]
    return pl.pallas_call(
        functools.partial(combine_kernel, n, q, d),
        out_shape=jax.ShapeDtypeStruct((rows, width), jnp.float32),
        in_specs=[pl.BlockSpec(memory_space=pl.ANY)],
        out_specs=pl.BlockSpec(memory_space=pltpu.VMEM),
        scratch_shapes=[
            pltpu.VMEM((n, rows, width), jnp.float32),
            pltpu.SemaphoreType.DMA,
            pltpu.SemaphoreType.DMA,
            pltpu.SemaphoreType.DMA,
        ],
        compiler_params=pltpu.CompilerParams(collective_id=0, has_side_effects=True),
    )(x)


def total_kernel(n, q, x_ref, o_ref, buf, send_sem, recv_sem):
    me = _device_index()
    _greet_all(n, q, me)
    _send_all(n, q, me, lambda dst: x_ref, buf, send_sem, recv_sem)
    _wait_all(n, q, me, buf, buf, send_sem, recv_sem)
    buf[me] = x_ref[...]

    def add(j, acc):
        return acc + buf[j]

    o_ref[...] = lax.fori_loop(0, n, add, jnp.zeros(o_ref.shape, jnp.float32))


def device_total(x, n, q):
    return pl.pallas_call(
        functools.partial(total_kernel, n, q),
        out_shape=jax.ShapeDtypeStruct(x.shape, jnp.float32),
        in_specs=[pl.BlockSpec(memory_space=pltpu.VMEM)],
        out_specs=pl.BlockSpec(memory_space=pltpu.VMEM),
        scratch_shapes=[
            pltpu.VMEM((n,) + x.shape, jnp.float32),
            pltpu.SemaphoreType.DMA,
            pltpu.SemaphoreType.DMA,
        ],
        compiler_params=pltpu.CompilerParams(collective_id=1, has_side_effects=True),
    )(x)


def shards(queue_keys, fresh_keys, slots, queries, positives):
    dp_size = lax.axis_size("dp")
    queue_size = lax.axis_size("queue")
    n = dp_size * queue_size
    d = queries.shape[1]
    all_queries = lax.all_gather(queries, "dp", axis=0, tiled=True)
    fresh_all, slots_all = (
        lax.all_gather(fresh_keys, ("dp", "queue"), axis=0, tiled=True),
        lax.all_gather(slots, ("dp", "queue"), axis=0, tiled=True),
    )
    queue_scores = score_rows(all_queries, queue_keys)
    fresh_scores = score_rows(all_queries, fresh_keys)
    local_top = jnp.maximum(jnp.max(queue_scores, axis=1), jnp.max(fresh_scores, axis=1))
    queue_exp = jnp.exp(queue_scores - local_top[:, None])
    fresh_exp = jnp.exp(fresh_scores - local_top[:, None])
    local_sum = jnp.sum(queue_exp, axis=1) + jnp.sum(fresh_exp, axis=1)
    local_pulled = jnp.dot(
        queue_exp.astype(jnp.bfloat16), queue_keys, preferred_element_type=jnp.float32
    ) + jnp.dot(fresh_exp.astype(jnp.bfloat16), fresh_keys, preferred_element_type=jnp.float32)
    total_rows = all_queries.shape[0]
    own_rows = total_rows // n
    stats = jnp.zeros((total_rows, STAT), jnp.float32)
    stats = stats.at[:, 0].set(local_top).at[:, 1].set(local_sum)
    packed = jnp.concatenate([local_pulled, stats], axis=1).reshape(n, own_rows, d + STAT)
    combined = combine(packed, n, queue_size, d)
    top_rows = combined[:, d]
    sum_rows = combined[:, d + 1]
    pulled = combined[:, :d]

    queue_index = lax.axis_index("queue")
    device_index = _device_index()
    local_start = queue_index * own_rows
    positive_rows = lax.dynamic_slice_in_dim(positives, local_start, own_rows, 0)
    query_rows = lax.dynamic_slice_in_dim(queries, local_start, own_rows, 0)
    positive_keys = jnp.take(fresh_all, positive_rows, axis=0).astype(jnp.float32)
    query_grad = pulled / sum_rows[:, None] - positive_keys
    positive_scores = jnp.sum(query_rows.astype(jnp.float32) * positive_keys, axis=1)
    loss_part = jnp.sum(top_rows + jnp.log(sum_rows) - positive_scores)
    loss_sum = device_total(jnp.full((8, 128), loss_part, jnp.float32), n, queue_size)[0, 0]
    mean_loss = loss_sum / total_rows
    held_rows = queue_keys.shape[0]
    local_slot = slots_all - device_index * held_rows
    inside = (local_slot >= 0) & (local_slot < held_rows)
    target = jnp.where(inside, local_slot, held_rows)
    new_queue = queue_keys.at[target].set(fresh_all, mode="drop")
    return (query_grad, mean_loss, new_queue)


def solution(mesh):
    placed = (
        P(("dp", "queue"), None),
        P(("dp", "queue"), None),
        P(("dp", "queue")),
        P("dp", None),
        P("dp"),
    )
    return jax.shard_map(
        shards,
        mesh=mesh,
        in_specs=placed,
        out_specs=(P(("dp", "queue"), None), P(), P(("dp", "queue"), None)),
        check_vma=False,
    )
```

```python
import functools

import jax
import jax.numpy as jnp
from jax import lax
from jax.experimental import pallas as pl
from jax.experimental.pallas import tpu as pltpu
from jax.sharding import PartitionSpec as P

MESH = pl.DeviceIdType.MESH
STAT = 128


def score_rows(query_rows, key_rows):
    return lax.dot_general(
        query_rows, key_rows, (((1,), (1,)), ((), ())), preferred_element_type=jnp.float32
    )


def _device_index():
    return lax.axis_index("dp") * lax.axis_size("queue") + lax.axis_index("queue")


def _wait_bytes(src, dst, send_sem, recv_sem, device_id):
    total = pltpu.make_async_remote_copy(
        src_ref=src, dst_ref=dst, send_sem=send_sem, recv_sem=recv_sem,
        device_id=device_id, device_id_type=MESH,
    )
    total.wait_send()
    total.wait_recv()


def _merge(blocks, d):
    tops = blocks[:, :, d:d + 1]
    top = jnp.max(tops, axis=0)
    return top, jnp.sum(blocks * jnp.exp(tops - top[None]), axis=0)


def combine_kernel(d, x_ref, pos_ref, o_ref, loss_ref, own, pair, merged, gathered,
                   loss_in, loss_pair, sems):
    q = lax.axis_size("queue")
    g = x_ref.shape[1]
    dp = lax.axis_index("dp")
    y, c = dp // 2, lax.rem(dp, 2)
    qi = lax.axis_index("queue")
    me = y * q + qi
    partner = (dp + 1 - 2 * c, qi)

    def peer(k):
        return ((k // q) * 2 + c, lax.rem(k, q))

    barrier = pltpu.get_barrier_semaphore()
    pl.semaphore_signal(barrier, inc=1, device_id=partner, device_id_type=MESH)

    def greet(k, carry):
        pl.semaphore_signal(barrier, inc=1, device_id=peer(lax.rem(me + k, g)), device_id_type=MESH)
        return carry

    lax.fori_loop(1, g, greet, 0)
    pl.semaphore_wait(barrier, g)

    to_pair = pltpu.make_async_remote_copy(
        src_ref=x_ref.at[1 - c], dst_ref=pair, send_sem=sems.at[0], recv_sem=sems.at[1],
        device_id=partner, device_id_type=MESH,
    )
    to_pair.start()
    mine = pltpu.make_async_copy(x_ref.at[c], own, sems.at[2])
    mine.start()
    mine.wait()
    to_pair.wait()

    def merge_pair(k, carry):
        top, acc = _merge(jnp.stack([own[k], pair[k]]), d)
        col = lax.broadcasted_iota(jnp.int32, acc.shape, 1)
        merged[k] = jnp.where(col == d, top, acc)
        return carry

    lax.fori_loop(0, g, merge_pair, 0)

    def send(k, carry):
        dst = lax.rem(me + k, g)
        pltpu.make_async_remote_copy(
            src_ref=merged.at[dst], dst_ref=gathered.at[me], send_sem=sems.at[3],
            recv_sem=sems.at[4], device_id=peer(dst), device_id_type=MESH,
        ).start()
        return carry

    lax.fori_loop(1, g, send, 0)
    gathered[me] = merged[me]
    _wait_bytes(merged.at[pl.ds(0, g - 1)], gathered.at[pl.ds(0, g - 1)], sems.at[3], sems.at[4],
                peer(lax.rem(me + 1, g)))
    def top_of(k, m):
        return jnp.maximum(m, gathered[k][:, d:d + 1])

    top = lax.fori_loop(0, g, top_of, jnp.full((o_ref.shape[0], 1), -jnp.inf, jnp.float32))

    def add_block(k, acc):
        b = gathered[k]
        return acc + b * jnp.exp(b[:, d:d + 1] - top)

    acc = lax.fori_loop(0, g, add_block, jnp.zeros(o_ref.shape, jnp.float32))
    col = lax.broadcasted_iota(jnp.int32, acc.shape, 1)
    o_ref[...] = jnp.where(col == d, top, acc)

    sums = acc[:, d + 1:d + 2]
    part = jnp.sum(top + jnp.log(sums) - pos_ref[:, 0:1])
    tile = jnp.full(loss_ref.shape, part, jnp.float32)
    loss_in[me] = tile

    def send_loss(k, carry):
        dst = lax.rem(me + k, g)
        pltpu.make_async_remote_copy(
            src_ref=loss_in.at[me], dst_ref=loss_in.at[me], send_sem=sems.at[5],
            recv_sem=sems.at[6], device_id=peer(dst), device_id_type=MESH,
        ).start()
        return carry

    lax.fori_loop(1, g, send_loss, 0)
    _wait_bytes(loss_in.at[pl.ds(0, g - 1)], loss_in.at[pl.ds(0, g - 1)], sems.at[5], sems.at[6],
                peer(lax.rem(me + 1, g)))

    def add(k, total):
        return total + loss_in[k]

    core_total = lax.fori_loop(0, g, add, jnp.zeros(loss_ref.shape, jnp.float32))
    loss_pair[c] = core_total
    to_pair_loss = pltpu.make_async_remote_copy(
        src_ref=loss_pair.at[c], dst_ref=loss_pair.at[c], send_sem=sems.at[7], recv_sem=sems.at[8],
        device_id=partner, device_id_type=MESH,
    )
    to_pair_loss.start()
    to_pair_loss.wait()
    loss_ref[...] = loss_pair[0] + loss_pair[1]


def combine(x, pos, d):
    g, rows, width = x.shape[1:]
    return pl.pallas_call(
        functools.partial(combine_kernel, d),
        out_shape=(
            jax.ShapeDtypeStruct((rows, width), jnp.float32),
            jax.ShapeDtypeStruct((8, 128), jnp.float32),
        ),
        in_specs=[pl.BlockSpec(memory_space=pl.ANY), pl.BlockSpec(memory_space=pltpu.VMEM)],
        out_specs=(pl.BlockSpec(memory_space=pltpu.VMEM), pl.BlockSpec(memory_space=pltpu.VMEM)),
        scratch_shapes=[
            pltpu.VMEM((g, rows, width), jnp.float32),
            pltpu.VMEM((g, rows, width), jnp.float32),
            pltpu.VMEM((g, rows, width), jnp.float32),
            pltpu.VMEM((g, rows, width), jnp.float32),
            pltpu.VMEM((g, 8, 128), jnp.float32),
            pltpu.VMEM((2, 8, 128), jnp.float32),
            pltpu.SemaphoreType.DMA((9,)),
        ],
        compiler_params=pltpu.CompilerParams(collective_id=0, has_side_effects=True),
    )(x, pos)


def shards(queue_keys, fresh_keys, slots, queries, positives):
    dp_size = lax.axis_size("dp")
    queue_size = lax.axis_size("queue")
    n = dp_size * queue_size
    d = queries.shape[1]
    gathered = lax.all_gather(queries, "dp", axis=0, tiled=True)
    total_rows = gathered.shape[0]
    own_rows = total_rows // n
    all_queries = gathered.reshape(dp_size // 2, 2, total_rows // dp_size, d)
    all_queries = all_queries.transpose(1, 0, 2, 3).reshape(total_rows, d)
    digits = jnp.stack([slots // 16384, (slots // 128) % 128, slots % 128], axis=1)
    code = jnp.zeros((slots.shape[0], STAT), jnp.bfloat16).at[:, :3].set(digits.astype(jnp.bfloat16))
    fresh_ext = lax.all_gather(
        jnp.concatenate([fresh_keys, code], axis=1), ("dp", "queue"), axis=0, tiled=True
    )
    fresh_all = fresh_ext[:, :d]
    got = fresh_ext[:, d:d + 3].astype(jnp.int32)
    slots_all = got[:, 0] * 16384 + got[:, 1] * 128 + got[:, 2]
    queue_scores = score_rows(all_queries, queue_keys)
    fresh_scores = score_rows(all_queries, fresh_keys)
    local_top = jnp.maximum(jnp.max(queue_scores, axis=1), jnp.max(fresh_scores, axis=1))
    queue_exp = jnp.exp(queue_scores - local_top[:, None])
    fresh_exp = jnp.exp(fresh_scores - local_top[:, None])
    local_sum = jnp.sum(queue_exp, axis=1) + jnp.sum(fresh_exp, axis=1)
    local_pulled = jnp.dot(
        queue_exp.astype(jnp.bfloat16), queue_keys, preferred_element_type=jnp.float32
    ) + jnp.dot(fresh_exp.astype(jnp.bfloat16), fresh_keys, preferred_element_type=jnp.float32)
    stats = jnp.zeros((total_rows, STAT), jnp.float32)
    stats = stats.at[:, 0].set(local_top).at[:, 1].set(local_sum)
    packed = jnp.concatenate([local_pulled, stats], axis=1).reshape(2, n // 2, own_rows, d + STAT)

    queue_index = lax.axis_index("queue")
    device_index = _device_index()
    local_start = queue_index * own_rows
    positive_rows = lax.dynamic_slice_in_dim(positives, local_start, own_rows, 0)
    query_rows = lax.dynamic_slice_in_dim(queries, local_start, own_rows, 0)
    positive_keys = jnp.take(fresh_all, positive_rows, axis=0).astype(jnp.float32)
    positive_scores = jnp.sum(query_rows.astype(jnp.float32) * positive_keys, axis=1)
    pos_tile = jnp.zeros((own_rows, 128), jnp.float32).at[:, 0].set(positive_scores)
    combined, loss_tile = combine(packed, pos_tile, d)
    sum_rows = combined[:, d + 1]
    pulled = combined[:, :d]
    query_grad = pulled / sum_rows[:, None] - positive_keys
    mean_loss = loss_tile[0, 0] / total_rows
    held_rows = queue_keys.shape[0]
    local_slot = slots_all - device_index * held_rows
    inside = (local_slot >= 0) & (local_slot < held_rows)
    target = jnp.where(inside, local_slot, held_rows)
    new_queue = queue_keys.at[target].set(fresh_all, mode="drop")
    return (query_grad, mean_loss, new_queue)


def solution(mesh):
    placed = (
        P(("dp", "queue"), None),
        P(("dp", "queue"), None),
        P(("dp", "queue")),
        P("dp", None),
        P("dp"),
    )
    return jax.shard_map(
        shards,
        mesh=mesh,
        in_specs=placed,
        out_specs=(P(("dp", "queue"), None), P(), P(("dp", "queue"), None)),
        check_vma=False,
    )
```

```python
import functools

import jax
import jax.numpy as jnp
from jax import lax
from jax.experimental import pallas as pl
from jax.experimental.pallas import tpu as pltpu
from jax.sharding import PartitionSpec as P

MESH = pl.DeviceIdType.MESH
STAT = 128


def score_rows(query_rows, key_rows):
    return lax.dot_general(
        query_rows, key_rows, (((1,), (1,)), ((), ())), preferred_element_type=jnp.float32
    )


def _device_index():
    return lax.axis_index("dp") * lax.axis_size("queue") + lax.axis_index("queue")


def _wait_bytes(src, dst, send_sem, recv_sem, device_id):
    total = pltpu.make_async_remote_copy(
        src_ref=src, dst_ref=dst, send_sem=send_sem, recv_sem=recv_sem,
        device_id=device_id, device_id_type=MESH,
    )
    total.wait_send()
    total.wait_recv()


def combine_kernel(d, p_ref, s_ref, pos_ref, qk_ref, o_ref, loss_ref, nq_ref, own_p, own_s,
                   pair_p, pair_s, merged, gathered, loss_in, loss_pair, sems):
    q = lax.axis_size("queue")
    g = p_ref.shape[1]
    dp = lax.axis_index("dp")
    y, c = dp // 2, lax.rem(dp, 2)
    qi = lax.axis_index("queue")
    me = y * q + qi
    partner = (dp + 1 - 2 * c, qi)

    def peer(k):
        return ((k // q) * 2 + c, lax.rem(k, q))

    queue_copy = pltpu.make_async_copy(qk_ref, nq_ref, sems.at[9])
    queue_copy.start()

    barrier = pltpu.get_barrier_semaphore()
    pl.semaphore_signal(barrier, inc=1, device_id=partner, device_id_type=MESH)

    def greet(k, carry):
        pl.semaphore_signal(barrier, inc=1, device_id=peer(lax.rem(me + k, g)), device_id_type=MESH)
        return carry

    lax.fori_loop(1, g, greet, 0)
    pl.semaphore_wait(barrier, g)

    pair_copies = [
        pltpu.make_async_remote_copy(
            src_ref=src.at[1 - c], dst_ref=dst, send_sem=sems.at[2 * i], recv_sem=sems.at[2 * i + 1],
            device_id=partner, device_id_type=MESH,
        )
        for i, (src, dst) in enumerate(((p_ref, pair_p), (s_ref, pair_s)))
    ]
    for copy in pair_copies:
        copy.start()
    mine = [pltpu.make_async_copy(src.at[c], dst, sems.at[10 + i])
            for i, (src, dst) in enumerate(((p_ref, own_p), (s_ref, own_s)))]
    for copy in mine:
        copy.start()
    for copy in mine + pair_copies:
        copy.wait()

    def merge_pair(k, carry):
        a, b = own_s[k], pair_s[k]
        top = jnp.maximum(a[:, 0:1], b[:, 0:1])
        wa, wb = jnp.exp(a[:, 0:1] - top), jnp.exp(b[:, 0:1] - top)
        merged[k, :, :d] = own_p[k] * wa + pair_p[k] * wb
        col = lax.broadcasted_iota(jnp.int32, a.shape, 1)
        merged[k, :, d:] = jnp.where(col == 0, top, a * wa + b * wb)
        return carry

    lax.fori_loop(0, g, merge_pair, 0)

    def send(k, carry):
        dst = lax.rem(me + k, g)
        pltpu.make_async_remote_copy(
            src_ref=merged.at[dst], dst_ref=gathered.at[me], send_sem=sems.at[4],
            recv_sem=sems.at[5], device_id=peer(dst), device_id_type=MESH,
        ).start()
        return carry

    lax.fori_loop(1, g, send, 0)
    gathered[me] = merged[me]
    _wait_bytes(merged.at[pl.ds(0, g - 1)], gathered.at[pl.ds(0, g - 1)], sems.at[4], sems.at[5],
                peer(lax.rem(me + 1, g)))

    def top_of(k, m):
        return jnp.maximum(m, gathered[k][:, d:d + 1])

    top = lax.fori_loop(0, g, top_of, jnp.full((o_ref.shape[0], 1), -jnp.inf, jnp.float32))

    def add_block(k, acc):
        b = gathered[k]
        return acc + b * jnp.exp(b[:, d:d + 1] - top)

    acc = lax.fori_loop(0, g, add_block, jnp.zeros(o_ref.shape, jnp.float32))
    col = lax.broadcasted_iota(jnp.int32, acc.shape, 1)
    o_ref[...] = jnp.where(col == d, top, acc)

    sums = acc[:, d + 1:d + 2]
    part = jnp.sum(top + jnp.log(sums)) - pos_ref[0:1, 0:1]
    loss_in[me] = jnp.broadcast_to(part, loss_ref.shape)

    def send_loss(k, carry):
        dst = lax.rem(me + k, g)
        pltpu.make_async_remote_copy(
            src_ref=loss_in.at[me], dst_ref=loss_in.at[me], send_sem=sems.at[6],
            recv_sem=sems.at[7], device_id=peer(dst), device_id_type=MESH,
        ).start()
        return carry

    lax.fori_loop(1, g, send_loss, 0)
    _wait_bytes(loss_in.at[pl.ds(0, g - 1)], loss_in.at[pl.ds(0, g - 1)], sems.at[6], sems.at[7],
                peer(lax.rem(me + 1, g)))

    def add(k, total):
        return total + loss_in[k]

    core_total = lax.fori_loop(0, g, add, jnp.zeros(loss_ref.shape, jnp.float32))
    loss_pair[c] = core_total
    to_pair_loss = pltpu.make_async_remote_copy(
        src_ref=loss_pair.at[c], dst_ref=loss_pair.at[c], send_sem=sems.at[8], recv_sem=sems.at[12],
        device_id=partner, device_id_type=MESH,
    )
    to_pair_loss.start()
    to_pair_loss.wait()
    loss_ref[...] = loss_pair[0] + loss_pair[1]
    queue_copy.wait()


def combine(pulled, stats, pos, queue_keys, d):
    g, rows = pulled.shape[1:3]
    width = d + stats.shape[3]
    return pl.pallas_call(
        functools.partial(combine_kernel, d),
        out_shape=(
            jax.ShapeDtypeStruct((rows, width), jnp.float32),
            jax.ShapeDtypeStruct((8, 128), jnp.float32),
            jax.ShapeDtypeStruct(queue_keys.shape, queue_keys.dtype),
        ),
        in_specs=[
            pl.BlockSpec(memory_space=pl.ANY),
            pl.BlockSpec(memory_space=pl.ANY),
            pl.BlockSpec(memory_space=pltpu.VMEM),
            pl.BlockSpec(memory_space=pl.ANY),
        ],
        out_specs=(
            pl.BlockSpec(memory_space=pltpu.VMEM),
            pl.BlockSpec(memory_space=pltpu.VMEM),
            pl.BlockSpec(memory_space=pl.ANY),
        ),
        scratch_shapes=[
            pltpu.VMEM((g, rows, d), jnp.float32),
            pltpu.VMEM((g, rows, width - d), jnp.float32),
            pltpu.VMEM((g, rows, d), jnp.float32),
            pltpu.VMEM((g, rows, width - d), jnp.float32),
            pltpu.VMEM((g, rows, width), jnp.float32),
            pltpu.VMEM((g, rows, width), jnp.float32),
            pltpu.VMEM((g, 8, 128), jnp.float32),
            pltpu.VMEM((2, 8, 128), jnp.float32),
            pltpu.SemaphoreType.DMA((13,)),
        ],
        compiler_params=pltpu.CompilerParams(collective_id=0, has_side_effects=True),
    )(pulled, stats, pos, queue_keys)


def shards(queue_keys, fresh_keys, slots, queries, positives):
    dp_size = lax.axis_size("dp")
    queue_size = lax.axis_size("queue")
    n = dp_size * queue_size
    d = queries.shape[1]
    pos_code = jnp.zeros((queries.shape[0], STAT), jnp.bfloat16)
    pos_code = pos_code.at[:, 0].set((positives // 32).astype(jnp.bfloat16))
    pos_code = pos_code.at[:, 1].set((positives % 32).astype(jnp.bfloat16))
    gathered = lax.all_gather(
        jnp.concatenate([queries, pos_code], axis=1), "dp", axis=0, tiled=True
    )
    total_rows = gathered.shape[0]
    own_rows = total_rows // n
    gathered = gathered.reshape(dp_size // 2, 2, total_rows // dp_size, d + STAT)
    gathered = gathered.transpose(1, 0, 2, 3).reshape(total_rows, d + STAT)
    all_queries = gathered[:, :d]
    pos_digits = gathered[:, d:d + 2].astype(jnp.int32)
    all_positives = pos_digits[:, 0] * 32 + pos_digits[:, 1]
    digits = jnp.stack([slots // 16384, (slots // 128) % 128, slots % 128], axis=1)
    code = jnp.zeros((slots.shape[0], STAT), jnp.bfloat16).at[:, :3].set(digits.astype(jnp.bfloat16))
    fresh_ext = lax.all_gather(
        jnp.concatenate([fresh_keys, code], axis=1), ("dp", "queue"), axis=0, tiled=True
    )
    fresh_all = fresh_ext[:, :d]
    got = fresh_ext[:, d:d + 3].astype(jnp.int32)
    slots_all = got[:, 0] * 16384 + got[:, 1] * 128 + got[:, 2]

    device_index = _device_index()
    queue_scores = score_rows(all_queries, queue_keys)
    fresh_scores = score_rows(all_queries, fresh_keys)
    local_top = jnp.maximum(jnp.max(queue_scores, axis=1), jnp.max(fresh_scores, axis=1))
    queue_exp = jnp.exp(queue_scores - local_top[:, None])
    fresh_exp = jnp.exp(fresh_scores - local_top[:, None])
    local_sum = jnp.sum(queue_exp, axis=1) + jnp.sum(fresh_exp, axis=1)
    local_pulled = jnp.dot(
        queue_exp.astype(jnp.bfloat16), queue_keys, preferred_element_type=jnp.float32
    ) + jnp.dot(fresh_exp.astype(jnp.bfloat16), fresh_keys, preferred_element_type=jnp.float32)
    fresh_ids = device_index * fresh_keys.shape[0] + jnp.arange(fresh_keys.shape[0], dtype=jnp.int32)
    is_positive = all_positives[:, None] == fresh_ids[None, :]
    positive_total = jnp.sum(jnp.where(is_positive, fresh_scores, 0.0))
    stats = jnp.zeros((total_rows, STAT), jnp.float32)
    stats = stats.at[:, 0].set(local_top).at[:, 1].set(local_sum)
    halves = (2, n // 2, own_rows)
    combined, loss_tile, queue_copy = combine(
        local_pulled.reshape(halves + (d,)),
        stats.reshape(halves + (STAT,)),
        jnp.full((8, 128), positive_total, jnp.float32),
        queue_keys,
        d,
    )
    sum_rows = combined[:, d + 1]
    pulled = combined[:, :d]
    queue_index = lax.axis_index("queue")
    local_start = queue_index * own_rows
    positive_rows = lax.dynamic_slice_in_dim(positives, local_start, own_rows, 0)
    positive_keys = jnp.take(fresh_all, positive_rows, axis=0).astype(jnp.float32)
    query_grad = pulled / sum_rows[:, None] - positive_keys
    mean_loss = loss_tile[0, 0] / total_rows
    held_rows = queue_keys.shape[0]
    local_slot = slots_all - device_index * held_rows
    inside = (local_slot >= 0) & (local_slot < held_rows)
    target = jnp.where(inside, local_slot, held_rows)
    new_queue = queue_copy.at[target].set(fresh_all, mode="drop")
    return (query_grad, mean_loss, new_queue)


def solution(mesh):
    placed = (
        P(("dp", "queue"), None),
        P(("dp", "queue"), None),
        P(("dp", "queue")),
        P("dp", None),
        P("dp"),
    )
    return jax.shard_map(
        shards,
        mesh=mesh,
        in_specs=placed,
        out_specs=(P(("dp", "queue"), None), P(), P(("dp", "queue"), None)),
        check_vma=False,
    )
```

```python
import functools

import jax
import jax.numpy as jnp
from jax import lax
from jax.experimental import pallas as pl
from jax.experimental.pallas import tpu as pltpu
from jax.sharding import PartitionSpec as P

MESH = pl.DeviceIdType.MESH
STAT = 128


def score_rows(query_rows, key_rows):
    return lax.dot_general(
        query_rows, key_rows, (((1,), (1,)), ((), ())), preferred_element_type=jnp.float32
    )


def _device_index():
    return lax.axis_index("dp") * lax.axis_size("queue") + lax.axis_index("queue")


def _wait_bytes(src, dst, send_sem, recv_sem, device_id):
    total = pltpu.make_async_remote_copy(
        src_ref=src, dst_ref=dst, send_sem=send_sem, recv_sem=recv_sem,
        device_id=device_id, device_id_type=MESH,
    )
    total.wait_send()
    total.wait_recv()


def combine_kernel(d, p_ref, s_ref, pos_ref, o_ref, loss_ref, own_p, own_s,
                   pair_p, pair_s, merged, gathered, loss_in, loss_pair, sems):
    q = lax.axis_size("queue")
    g = p_ref.shape[1]
    dp = lax.axis_index("dp")
    y, c = dp // 2, lax.rem(dp, 2)
    qi = lax.axis_index("queue")
    me = y * q + qi
    partner = (dp + 1 - 2 * c, qi)

    def peer(k):
        return ((k // q) * 2 + c, lax.rem(k, q))

    barrier = pltpu.get_barrier_semaphore()
    pl.semaphore_signal(barrier, inc=1, device_id=partner, device_id_type=MESH)

    def greet(k, carry):
        pl.semaphore_signal(barrier, inc=1, device_id=peer(lax.rem(me + k, g)), device_id_type=MESH)
        return carry

    lax.fori_loop(1, g, greet, 0)
    pl.semaphore_wait(barrier, g)

    pair_copies = [
        pltpu.make_async_remote_copy(
            src_ref=src.at[1 - c], dst_ref=dst, send_sem=sems.at[2 * i], recv_sem=sems.at[2 * i + 1],
            device_id=partner, device_id_type=MESH,
        )
        for i, (src, dst) in enumerate(((p_ref, pair_p), (s_ref, pair_s)))
    ]
    for copy in pair_copies:
        copy.start()
    mine = [pltpu.make_async_copy(src.at[c], dst, sems.at[10 + i])
            for i, (src, dst) in enumerate(((p_ref, own_p), (s_ref, own_s)))]
    for copy in mine:
        copy.start()
    for copy in mine + pair_copies:
        copy.wait()

    def merge_pair(k, carry):
        a, b = own_s[k], pair_s[k]
        top = jnp.maximum(a[:, 0:1], b[:, 0:1])
        wa, wb = jnp.exp(a[:, 0:1] - top), jnp.exp(b[:, 0:1] - top)
        merged[k, :, :d] = own_p[k] * wa + pair_p[k] * wb
        col = lax.broadcasted_iota(jnp.int32, a.shape, 1)
        merged[k, :, d:] = jnp.where(col == 0, top, a * wa + b * wb)
        return carry

    lax.fori_loop(0, g, merge_pair, 0)

    def send(k, carry):
        dst = lax.rem(me + k, g)
        pltpu.make_async_remote_copy(
            src_ref=merged.at[dst], dst_ref=gathered.at[me], send_sem=sems.at[4],
            recv_sem=sems.at[5], device_id=peer(dst), device_id_type=MESH,
        ).start()
        return carry

    lax.fori_loop(1, g, send, 0)
    gathered[me] = merged[me]
    _wait_bytes(merged.at[pl.ds(0, g - 1)], gathered.at[pl.ds(0, g - 1)], sems.at[4], sems.at[5],
                peer(lax.rem(me + 1, g)))

    def top_of(k, m):
        return jnp.maximum(m, gathered[k][:, d:d + 1])

    top = lax.fori_loop(0, g, top_of, jnp.full((o_ref.shape[0], 1), -jnp.inf, jnp.float32))

    def add_block(k, acc):
        b = gathered[k]
        return acc + b * jnp.exp(b[:, d:d + 1] - top)

    acc = lax.fori_loop(0, g, add_block, jnp.zeros(o_ref.shape, jnp.float32))
    col = lax.broadcasted_iota(jnp.int32, acc.shape, 1)
    o_ref[...] = jnp.where(col == d, top, acc)

    sums = acc[:, d + 1:d + 2]
    part = jnp.sum(top + jnp.log(sums)) - pos_ref[0:1, 0:1]
    loss_in[me] = jnp.broadcast_to(part, loss_ref.shape)

    def send_loss(k, carry):
        dst = lax.rem(me + k, g)
        pltpu.make_async_remote_copy(
            src_ref=loss_in.at[me], dst_ref=loss_in.at[me], send_sem=sems.at[6],
            recv_sem=sems.at[7], device_id=peer(dst), device_id_type=MESH,
        ).start()
        return carry

    lax.fori_loop(1, g, send_loss, 0)
    _wait_bytes(loss_in.at[pl.ds(0, g - 1)], loss_in.at[pl.ds(0, g - 1)], sems.at[6], sems.at[7],
                peer(lax.rem(me + 1, g)))

    def add(k, total):
        return total + loss_in[k]

    core_total = lax.fori_loop(0, g, add, jnp.zeros(loss_ref.shape, jnp.float32))
    loss_pair[c] = core_total
    to_pair_loss = pltpu.make_async_remote_copy(
        src_ref=loss_pair.at[c], dst_ref=loss_pair.at[c], send_sem=sems.at[8], recv_sem=sems.at[12],
        device_id=partner, device_id_type=MESH,
    )
    to_pair_loss.start()
    to_pair_loss.wait()
    loss_ref[...] = loss_pair[0] + loss_pair[1]


def combine(pulled, stats, pos, d):
    g, rows = pulled.shape[1:3]
    width = d + stats.shape[3]
    return pl.pallas_call(
        functools.partial(combine_kernel, d),
        out_shape=(
            jax.ShapeDtypeStruct((rows, width), jnp.float32),
            jax.ShapeDtypeStruct((8, 128), jnp.float32),
        ),
        in_specs=[
            pl.BlockSpec(memory_space=pl.ANY),
            pl.BlockSpec(memory_space=pl.ANY),
            pl.BlockSpec(memory_space=pltpu.VMEM),
        ],
        out_specs=(
            pl.BlockSpec(memory_space=pltpu.VMEM),
            pl.BlockSpec(memory_space=pltpu.VMEM),
        ),
        scratch_shapes=[
            pltpu.VMEM((g, rows, d), jnp.float32),
            pltpu.VMEM((g, rows, width - d), jnp.float32),
            pltpu.VMEM((g, rows, d), jnp.float32),
            pltpu.VMEM((g, rows, width - d), jnp.float32),
            pltpu.VMEM((g, rows, width), jnp.float32),
            pltpu.VMEM((g, rows, width), jnp.float32),
            pltpu.VMEM((g, 8, 128), jnp.float32),
            pltpu.VMEM((2, 8, 128), jnp.float32),
            pltpu.SemaphoreType.DMA((13,)),
        ],
        compiler_params=pltpu.CompilerParams(collective_id=0, has_side_effects=True),
    )(pulled, stats, pos)


def shards(queue_keys, fresh_keys, slots, queries, positives):
    dp_size = lax.axis_size("dp")
    queue_size = lax.axis_size("queue")
    n = dp_size * queue_size
    d = queries.shape[1]
    pos_code = jnp.zeros((queries.shape[0], STAT), jnp.bfloat16)
    pos_code = pos_code.at[:, 0].set((positives // 32).astype(jnp.bfloat16))
    pos_code = pos_code.at[:, 1].set((positives % 32).astype(jnp.bfloat16))
    gathered = lax.all_gather(
        jnp.concatenate([queries, pos_code], axis=1), "dp", axis=0, tiled=True
    )
    total_rows = gathered.shape[0]
    own_rows = total_rows // n
    gathered = gathered.reshape(dp_size // 2, 2, total_rows // dp_size, d + STAT)
    gathered = gathered.transpose(1, 0, 2, 3).reshape(total_rows, d + STAT)
    all_queries = gathered[:, :d]
    pos_digits = gathered[:, d:d + 2].astype(jnp.int32)
    all_positives = pos_digits[:, 0] * 32 + pos_digits[:, 1]
    digits = jnp.stack([slots // 16384, (slots // 128) % 128, slots % 128], axis=1)
    code = jnp.zeros((slots.shape[0], STAT), jnp.bfloat16).at[:, :3].set(digits.astype(jnp.bfloat16))
    fresh_ext = lax.all_gather(
        jnp.concatenate([fresh_keys, code], axis=1), ("dp", "queue"), axis=0, tiled=True
    )
    fresh_all = fresh_ext[:, :d]
    got = fresh_ext[:, d:d + 3].astype(jnp.int32)
    slots_all = got[:, 0] * 16384 + got[:, 1] * 128 + got[:, 2]

    device_index = _device_index()
    queue_scores = score_rows(all_queries, queue_keys)
    fresh_scores = score_rows(all_queries, fresh_keys)
    local_top = jnp.maximum(jnp.max(queue_scores, axis=1), jnp.max(fresh_scores, axis=1))
    queue_exp = jnp.exp(queue_scores - local_top[:, None])
    fresh_exp = jnp.exp(fresh_scores - local_top[:, None])
    local_sum = jnp.sum(queue_exp, axis=1) + jnp.sum(fresh_exp, axis=1)
    local_pulled = jnp.dot(
        queue_exp.astype(jnp.bfloat16), queue_keys, preferred_element_type=jnp.float32
    ) + jnp.dot(fresh_exp.astype(jnp.bfloat16), fresh_keys, preferred_element_type=jnp.float32)
    fresh_ids = device_index * fresh_keys.shape[0] + jnp.arange(fresh_keys.shape[0], dtype=jnp.int32)
    is_positive = all_positives[:, None] == fresh_ids[None, :]
    positive_total = jnp.sum(jnp.where(is_positive, fresh_scores, 0.0))
    stats = jnp.zeros((total_rows, STAT), jnp.float32)
    stats = stats.at[:, 0].set(local_top).at[:, 1].set(local_sum)
    halves = (2, n // 2, own_rows)
    combined, loss_tile = combine(
        local_pulled.reshape(halves + (d,)),
        stats.reshape(halves + (STAT,)),
        jnp.full((8, 128), positive_total, jnp.float32),
        d,
    )
    sum_rows = combined[:, d + 1]
    pulled = combined[:, :d]
    queue_index = lax.axis_index("queue")
    local_start = queue_index * own_rows
    positive_rows = lax.dynamic_slice_in_dim(positives, local_start, own_rows, 0)
    positive_keys = jnp.take(fresh_all, positive_rows, axis=0).astype(jnp.float32)
    query_grad = pulled / sum_rows[:, None] - positive_keys
    mean_loss = loss_tile[0, 0] / total_rows
    held_rows = queue_keys.shape[0]
    local_slot = slots_all - device_index * held_rows
    inside = (local_slot >= 0) & (local_slot < held_rows)
    target = jnp.where(inside, local_slot, held_rows)
    new_queue = queue_keys.at[target].set(fresh_all, mode="drop")
    return (query_grad, mean_loss, new_queue)


def solution(mesh):
    placed = (
        P(("dp", "queue"), None),
        P(("dp", "queue"), None),
        P(("dp", "queue")),
        P("dp", None),
        P("dp"),
    )
    return jax.shard_map(
        shards,
        mesh=mesh,
        in_specs=placed,
        out_specs=(P(("dp", "queue"), None), P(), P(("dp", "queue"), None)),
        check_vma=False,
    )
```

```python
import functools

import jax
import jax.numpy as jnp
from jax import lax
from jax.experimental import pallas as pl
from jax.experimental.pallas import tpu as pltpu
from jax.sharding import PartitionSpec as P

MESH = pl.DeviceIdType.MESH
STAT = 128


def score_rows(query_rows, key_rows):
    return lax.dot_general(
        query_rows, key_rows, (((1,), (1,)), ((), ())), preferred_element_type=jnp.float32
    )


def _device_index():
    return lax.axis_index("dp") * lax.axis_size("queue") + lax.axis_index("queue")


def _wait_bytes(src, dst, send_sem, recv_sem, device_id):
    total = pltpu.make_async_remote_copy(
        src_ref=src, dst_ref=dst, send_sem=send_sem, recv_sem=recv_sem,
        device_id=device_id, device_id_type=MESH,
    )
    total.wait_send()
    total.wait_recv()


def combine_kernel(d, p_ref, s_ref, pos_ref, o_ref, loss_ref, own_p, own_s,
                   pair_p, pair_s, merged, gathered, loss_in, loss_pair, sems):
    q = lax.axis_size("queue")
    g = p_ref.shape[1]
    dp = lax.axis_index("dp")
    y, c = dp // 2, lax.rem(dp, 2)
    qi = lax.axis_index("queue")
    me = y * q + qi
    partner = (dp + 1 - 2 * c, qi)

    def peer(k):
        return ((k // q) * 2 + c, lax.rem(k, q))

    barrier = pltpu.get_barrier_semaphore()
    pl.semaphore_signal(barrier, inc=1, device_id=partner, device_id_type=MESH)

    def greet(k, carry):
        pl.semaphore_signal(barrier, inc=1, device_id=peer(lax.rem(me + k, g)), device_id_type=MESH)
        return carry

    lax.fori_loop(1, g, greet, 0)
    pl.semaphore_wait(barrier, g)

    pair_copies = [
        pltpu.make_async_remote_copy(
            src_ref=src.at[1 - c], dst_ref=dst, send_sem=sems.at[2 * i], recv_sem=sems.at[2 * i + 1],
            device_id=partner, device_id_type=MESH,
        )
        for i, (src, dst) in enumerate(((p_ref, pair_p), (s_ref, pair_s)))
    ]
    for copy in pair_copies:
        copy.start()
    mine = [pltpu.make_async_copy(src.at[c], dst, sems.at[10 + i])
            for i, (src, dst) in enumerate(((p_ref, own_p), (s_ref, own_s)))]
    for copy in mine:
        copy.start()
    for copy in mine + pair_copies:
        copy.wait()

    def merge_pair(k, carry):
        a, b = own_s[k], pair_s[k]
        top = jnp.maximum(a[:, 0:1], b[:, 0:1])
        wa, wb = jnp.exp(a[:, 0:1] - top), jnp.exp(b[:, 0:1] - top)
        merged[k, :, :d] = own_p[k] * wa + pair_p[k] * wb
        col = lax.broadcasted_iota(jnp.int32, a.shape, 1)
        merged[k, :, d:] = jnp.where(col == 0, top, a * wa + b * wb)
        return carry

    lax.fori_loop(0, g, merge_pair, 0)

    def send(k, carry):
        dst = lax.rem(me + k, g)
        pltpu.make_async_remote_copy(
            src_ref=merged.at[dst], dst_ref=gathered.at[me], send_sem=sems.at[4],
            recv_sem=sems.at[5], device_id=peer(dst), device_id_type=MESH,
        ).start()
        return carry

    lax.fori_loop(1, g, send, 0)
    gathered[me] = merged[me]
    _wait_bytes(merged.at[pl.ds(0, g - 1)], gathered.at[pl.ds(0, g - 1)], sems.at[4], sems.at[5],
                peer(lax.rem(me + 1, g)))

    def top_of(k, m):
        return jnp.maximum(m, gathered[k][:, d:d + 1])

    top = lax.fori_loop(0, g, top_of, jnp.full((o_ref.shape[0], 1), -jnp.inf, jnp.float32))

    def add_block(k, acc):
        b = gathered[k]
        return acc + b * jnp.exp(b[:, d:d + 1] - top)

    acc = lax.fori_loop(0, g, add_block, jnp.zeros(o_ref.shape, jnp.float32))
    col = lax.broadcasted_iota(jnp.int32, acc.shape, 1)
    o_ref[...] = jnp.where(col == d, top, acc)

    sums = acc[:, d + 1:d + 2]
    part = jnp.sum(top + jnp.log(sums)) - pos_ref[0:1, 0:1]
    loss_in[me] = jnp.broadcast_to(part, loss_ref.shape)

    def send_loss(k, carry):
        dst = lax.rem(me + k, g)
        pltpu.make_async_remote_copy(
            src_ref=loss_in.at[me], dst_ref=loss_in.at[me], send_sem=sems.at[6],
            recv_sem=sems.at[7], device_id=peer(dst), device_id_type=MESH,
        ).start()
        return carry

    lax.fori_loop(1, g, send_loss, 0)
    _wait_bytes(loss_in.at[pl.ds(0, g - 1)], loss_in.at[pl.ds(0, g - 1)], sems.at[6], sems.at[7],
                peer(lax.rem(me + 1, g)))

    def add(k, total):
        return total + loss_in[k]

    core_total = lax.fori_loop(0, g, add, jnp.zeros(loss_ref.shape, jnp.float32))
    loss_pair[c] = core_total
    to_pair_loss = pltpu.make_async_remote_copy(
        src_ref=loss_pair.at[c], dst_ref=loss_pair.at[c], send_sem=sems.at[8], recv_sem=sems.at[12],
        device_id=partner, device_id_type=MESH,
    )
    to_pair_loss.start()
    to_pair_loss.wait()
    loss_ref[...] = loss_pair[0] + loss_pair[1]


def combine(pulled, stats, pos, d):
    g, rows = pulled.shape[1:3]
    width = d + stats.shape[3]
    return pl.pallas_call(
        functools.partial(combine_kernel, d),
        out_shape=(
            jax.ShapeDtypeStruct((rows, width), jnp.float32),
            jax.ShapeDtypeStruct((8, 128), jnp.float32),
        ),
        in_specs=[
            pl.BlockSpec(memory_space=pl.ANY),
            pl.BlockSpec(memory_space=pl.ANY),
            pl.BlockSpec(memory_space=pltpu.VMEM),
        ],
        out_specs=(
            pl.BlockSpec(memory_space=pltpu.VMEM),
            pl.BlockSpec(memory_space=pltpu.VMEM),
        ),
        scratch_shapes=[
            pltpu.VMEM((g, rows, d), jnp.float32),
            pltpu.VMEM((g, rows, width - d), jnp.float32),
            pltpu.VMEM((g, rows, d), jnp.float32),
            pltpu.VMEM((g, rows, width - d), jnp.float32),
            pltpu.VMEM((g, rows, width), jnp.float32),
            pltpu.VMEM((g, rows, width), jnp.float32),
            pltpu.VMEM((g, 8, 128), jnp.float32),
            pltpu.VMEM((2, 8, 128), jnp.float32),
            pltpu.SemaphoreType.DMA((13,)),
        ],
        compiler_params=pltpu.CompilerParams(collective_id=0, has_side_effects=True),
    )(pulled, stats, pos)


def shards(queue_keys, fresh_keys, slots, queries, positives):
    dp_size = lax.axis_size("dp")
    queue_size = lax.axis_size("queue")
    n = dp_size * queue_size
    d = queries.shape[1]
    pos_code = jnp.zeros((queries.shape[0], STAT), jnp.bfloat16)
    pos_code = pos_code.at[:, 0].set((positives // 32).astype(jnp.bfloat16))
    pos_code = pos_code.at[:, 1].set((positives % 32).astype(jnp.bfloat16))
    gathered = lax.all_gather(
        jnp.concatenate([queries, pos_code], axis=1), "dp", axis=0, tiled=True
    )
    total_rows = gathered.shape[0]
    own_rows = total_rows // n
    gathered = gathered.reshape(dp_size // 2, 2, total_rows // dp_size, d + STAT)
    gathered = gathered.transpose(1, 0, 2, 3).reshape(total_rows, d + STAT)
    all_queries = gathered[:, :d]
    pos_digits = gathered[:, d:d + 2].astype(jnp.int32)
    all_positives = pos_digits[:, 0] * 32 + pos_digits[:, 1]
    digits = jnp.stack([slots // 16384, (slots // 128) % 128, slots % 128], axis=1)
    code = jnp.zeros((slots.shape[0], STAT), jnp.bfloat16).at[:, :3].set(digits.astype(jnp.bfloat16))
    fresh_ext = lax.all_gather(
        jnp.concatenate([fresh_keys, code], axis=1), ("dp", "queue"), axis=0, tiled=True
    )
    fresh_all = fresh_ext[:, :d]
    got = fresh_ext[:, d:d + 3].astype(jnp.int32)
    slots_all = got[:, 0] * 16384 + got[:, 1] * 128 + got[:, 2]

    device_index = _device_index()
    queue_scores = score_rows(all_queries, queue_keys)
    fresh_scores = score_rows(all_queries, fresh_keys)
    local_top = jnp.maximum(jnp.max(queue_scores, axis=1), jnp.max(fresh_scores, axis=1))
    queue_exp = jnp.exp(queue_scores - local_top[:, None])
    fresh_exp = jnp.exp(fresh_scores - local_top[:, None])
    local_sum = jnp.sum(queue_exp, axis=1) + jnp.sum(fresh_exp, axis=1)
    local_pulled = jnp.dot(
        queue_exp.astype(jnp.bfloat16), queue_keys, preferred_element_type=jnp.float32
    ) + jnp.dot(fresh_exp.astype(jnp.bfloat16), fresh_keys, preferred_element_type=jnp.float32)
    fresh_ids = device_index * fresh_keys.shape[0] + jnp.arange(fresh_keys.shape[0], dtype=jnp.int32)
    is_positive = all_positives[:, None] == fresh_ids[None, :]
    positive_total = jnp.sum(jnp.where(is_positive, fresh_scores, 0.0))
    stats = jnp.zeros((total_rows, STAT), jnp.float32)
    stats = stats.at[:, 0].set(local_top).at[:, 1].set(local_sum)
    halves = (2, n // 2, own_rows)
    combined, loss_tile = combine(
        local_pulled.reshape(halves + (d,)),
        stats.reshape(halves + (STAT,)),
        jnp.full((8, 128), positive_total, jnp.float32),
        d,
    )
    sum_rows = combined[:, d + 1]
    pulled = combined[:, :d]
    queue_index = lax.axis_index("queue")
    local_start = queue_index * own_rows
    positive_rows = lax.dynamic_slice_in_dim(positives, local_start, own_rows, 0)
    positive_keys = jnp.take(fresh_all, positive_rows, axis=0).astype(jnp.float32)
    query_grad = pulled / sum_rows[:, None] - positive_keys
    mean_loss = loss_tile[0, 0] / total_rows
    held_rows = queue_keys.shape[0]
    local_slot = slots_all - device_index * held_rows
    picks = jnp.arange(held_rows, dtype=jnp.int32)[:, None] == local_slot[None, :]
    inserted = jnp.dot(picks.astype(jnp.bfloat16), fresh_all, preferred_element_type=jnp.float32)
    replaced = jnp.any(picks, axis=1)
    new_queue = jnp.where(replaced[:, None], inserted.astype(jnp.bfloat16), queue_keys)
    return (query_grad, mean_loss, new_queue)


def solution(mesh):
    placed = (
        P(("dp", "queue"), None),
        P(("dp", "queue"), None),
        P(("dp", "queue")),
        P("dp", None),
        P("dp"),
    )
    return jax.shard_map(
        shards,
        mesh=mesh,
        in_specs=placed,
        out_specs=(P(("dp", "queue"), None), P(), P(("dp", "queue"), None)),
        check_vma=False,
    )
```

```python
import functools

import jax
import jax.numpy as jnp
from jax import lax
from jax.experimental import pallas as pl
from jax.experimental.pallas import tpu as pltpu
from jax.sharding import PartitionSpec as P

MESH = pl.DeviceIdType.MESH
STAT = 128


def score_rows(query_rows, key_rows):
    return lax.dot_general(
        query_rows, key_rows, (((1,), (1,)), ((), ())), preferred_element_type=jnp.float32
    )


def _device_index():
    return lax.axis_index("dp") * lax.axis_size("queue") + lax.axis_index("queue")


def _wait_bytes(src, dst, send_sem, recv_sem, device_id):
    total = pltpu.make_async_remote_copy(
        src_ref=src, dst_ref=dst, send_sem=send_sem, recv_sem=recv_sem,
        device_id=device_id, device_id_type=MESH,
    )
    total.wait_send()
    total.wait_recv()


def gather_kernel(x_ref, o_ref, buf, sems):
    dp = lax.axis_index("dp")
    y, c = dp // 2, lax.rem(dp, 2)
    ys = lax.axis_size("dp") // 2
    qi = lax.axis_index("queue")
    partner = (dp + 1 - 2 * c, qi)

    def along(k):
        return (lax.rem(y + k, ys) * 2 + c, qi)

    barrier = pltpu.get_barrier_semaphore()
    pl.semaphore_signal(barrier, inc=1, device_id=partner, device_id_type=MESH)
    for k in range(1, ys):
        pl.semaphore_signal(barrier, inc=1, device_id=along(k), device_id_type=MESH)
    pl.semaphore_wait(barrier, ys)

    mine = pltpu.make_async_copy(x_ref, buf.at[c, y], sems.at[4])
    mine.start()
    first = [
        pltpu.make_async_remote_copy(
            src_ref=x_ref, dst_ref=buf.at[c, y], send_sem=sems.at[0], recv_sem=sems.at[1],
            device_id=dst, device_id_type=MESH,
        )
        for dst in [partner] + [along(k) for k in range(1, ys)]
    ]
    for copy in first:
        copy.start()
    _wait_bytes(buf.at[0], buf.at[0], sems.at[0], sems.at[1], partner)
    mine.wait()
    second = [
        pltpu.make_async_remote_copy(
            src_ref=buf.at[c, lax.rem(y + k, ys)], dst_ref=buf.at[c, lax.rem(y + k, ys)],
            send_sem=sems.at[2], recv_sem=sems.at[3], device_id=partner, device_id_type=MESH,
        )
        for k in range(1, ys)
    ]
    for copy in second:
        copy.start()
    _wait_bytes(buf.at[0, pl.ds(0, ys - 1)], buf.at[0, pl.ds(0, ys - 1)], sems.at[2], sems.at[3], partner)
    o_ref[...] = buf[...]


def gather_dp(x, ys):
    return pl.pallas_call(
        gather_kernel,
        out_shape=jax.ShapeDtypeStruct((2, ys) + x.shape, x.dtype),
        in_specs=[pl.BlockSpec(memory_space=pltpu.VMEM)],
        out_specs=pl.BlockSpec(memory_space=pltpu.VMEM),
        scratch_shapes=[
            pltpu.VMEM((2, ys) + x.shape, x.dtype),
            pltpu.SemaphoreType.DMA((5,)),
        ],
        compiler_params=pltpu.CompilerParams(collective_id=1, has_side_effects=True),
    )(x)


def combine_kernel(d, p_ref, s_ref, pos_ref, o_ref, loss_ref, own_p, own_s,
                   pair_p, pair_s, merged, gathered, loss_in, loss_pair, sems):
    q = lax.axis_size("queue")
    g = p_ref.shape[1]
    dp = lax.axis_index("dp")
    y, c = dp // 2, lax.rem(dp, 2)
    qi = lax.axis_index("queue")
    me = y * q + qi
    partner = (dp + 1 - 2 * c, qi)

    def peer(k):
        return ((k // q) * 2 + c, lax.rem(k, q))

    barrier = pltpu.get_barrier_semaphore()
    pl.semaphore_signal(barrier, inc=1, device_id=partner, device_id_type=MESH)

    def greet(k, carry):
        pl.semaphore_signal(barrier, inc=1, device_id=peer(lax.rem(me + k, g)), device_id_type=MESH)
        return carry

    lax.fori_loop(1, g, greet, 0)
    pl.semaphore_wait(barrier, g)

    pair_copies = [
        pltpu.make_async_remote_copy(
            src_ref=src.at[1 - c], dst_ref=dst, send_sem=sems.at[2 * i], recv_sem=sems.at[2 * i + 1],
            device_id=partner, device_id_type=MESH,
        )
        for i, (src, dst) in enumerate(((p_ref, pair_p), (s_ref, pair_s)))
    ]
    for copy in pair_copies:
        copy.start()
    mine = [pltpu.make_async_copy(src.at[c], dst, sems.at[10 + i])
            for i, (src, dst) in enumerate(((p_ref, own_p), (s_ref, own_s)))]
    for copy in mine:
        copy.start()
    for copy in mine + pair_copies:
        copy.wait()

    def merge_pair(k, carry):
        a, b = own_s[k], pair_s[k]
        top = jnp.maximum(a[:, 0:1], b[:, 0:1])
        wa, wb = jnp.exp(a[:, 0:1] - top), jnp.exp(b[:, 0:1] - top)
        merged[k, :, :d] = own_p[k] * wa + pair_p[k] * wb
        col = lax.broadcasted_iota(jnp.int32, a.shape, 1)
        merged[k, :, d:] = jnp.where(col == 0, top, a * wa + b * wb)
        return carry

    lax.fori_loop(0, g, merge_pair, 0)

    def send(k, carry):
        dst = lax.rem(me + k, g)
        pltpu.make_async_remote_copy(
            src_ref=merged.at[dst], dst_ref=gathered.at[me], send_sem=sems.at[4],
            recv_sem=sems.at[5], device_id=peer(dst), device_id_type=MESH,
        ).start()
        return carry

    lax.fori_loop(1, g, send, 0)
    gathered[me] = merged[me]
    _wait_bytes(merged.at[pl.ds(0, g - 1)], gathered.at[pl.ds(0, g - 1)], sems.at[4], sems.at[5],
                peer(lax.rem(me + 1, g)))

    def top_of(k, m):
        return jnp.maximum(m, gathered[k][:, d:d + 1])

    top = lax.fori_loop(0, g, top_of, jnp.full((o_ref.shape[0], 1), -jnp.inf, jnp.float32))

    def add_block(k, acc):
        b = gathered[k]
        return acc + b * jnp.exp(b[:, d:d + 1] - top)

    acc = lax.fori_loop(0, g, add_block, jnp.zeros(o_ref.shape, jnp.float32))
    col = lax.broadcasted_iota(jnp.int32, acc.shape, 1)
    o_ref[...] = jnp.where(col == d, top, acc)

    sums = acc[:, d + 1:d + 2]
    part = jnp.sum(top + jnp.log(sums)) - pos_ref[0:1, 0:1]
    loss_in[me] = jnp.broadcast_to(part, loss_ref.shape)

    def send_loss(k, carry):
        dst = lax.rem(me + k, g)
        pltpu.make_async_remote_copy(
            src_ref=loss_in.at[me], dst_ref=loss_in.at[me], send_sem=sems.at[6],
            recv_sem=sems.at[7], device_id=peer(dst), device_id_type=MESH,
        ).start()
        return carry

    lax.fori_loop(1, g, send_loss, 0)
    _wait_bytes(loss_in.at[pl.ds(0, g - 1)], loss_in.at[pl.ds(0, g - 1)], sems.at[6], sems.at[7],
                peer(lax.rem(me + 1, g)))

    def add(k, total):
        return total + loss_in[k]

    core_total = lax.fori_loop(0, g, add, jnp.zeros(loss_ref.shape, jnp.float32))
    loss_pair[c] = core_total
    to_pair_loss = pltpu.make_async_remote_copy(
        src_ref=loss_pair.at[c], dst_ref=loss_pair.at[c], send_sem=sems.at[8], recv_sem=sems.at[12],
        device_id=partner, device_id_type=MESH,
    )
    to_pair_loss.start()
    to_pair_loss.wait()
    loss_ref[...] = loss_pair[0] + loss_pair[1]


def combine(pulled, stats, pos, d):
    g, rows = pulled.shape[1:3]
    width = d + stats.shape[3]
    return pl.pallas_call(
        functools.partial(combine_kernel, d),
        out_shape=(
            jax.ShapeDtypeStruct((rows, width), jnp.float32),
            jax.ShapeDtypeStruct((8, 128), jnp.float32),
        ),
        in_specs=[
            pl.BlockSpec(memory_space=pl.ANY),
            pl.BlockSpec(memory_space=pl.ANY),
            pl.BlockSpec(memory_space=pltpu.VMEM),
        ],
        out_specs=(
            pl.BlockSpec(memory_space=pltpu.VMEM),
            pl.BlockSpec(memory_space=pltpu.VMEM),
        ),
        scratch_shapes=[
            pltpu.VMEM((g, rows, d), jnp.float32),
            pltpu.VMEM((g, rows, width - d), jnp.float32),
            pltpu.VMEM((g, rows, d), jnp.float32),
            pltpu.VMEM((g, rows, width - d), jnp.float32),
            pltpu.VMEM((g, rows, width), jnp.float32),
            pltpu.VMEM((g, rows, width), jnp.float32),
            pltpu.VMEM((g, 8, 128), jnp.float32),
            pltpu.VMEM((2, 8, 128), jnp.float32),
            pltpu.SemaphoreType.DMA((13,)),
        ],
        compiler_params=pltpu.CompilerParams(collective_id=0, has_side_effects=True),
    )(pulled, stats, pos)


def shards(queue_keys, fresh_keys, slots, queries, positives):
    dp_size = lax.axis_size("dp")
    queue_size = lax.axis_size("queue")
    n = dp_size * queue_size
    d = queries.shape[1]
    pos_code = jnp.zeros((queries.shape[0], STAT), jnp.bfloat16)
    pos_code = pos_code.at[:, 0].set((positives // 32).astype(jnp.bfloat16))
    pos_code = pos_code.at[:, 1].set((positives % 32).astype(jnp.bfloat16))
    gathered = gather_dp(jnp.concatenate([queries, pos_code], axis=1), dp_size // 2)
    total_rows = dp_size * queries.shape[0]
    own_rows = total_rows // n
    gathered = gathered.reshape(total_rows, d + STAT)
    all_queries = gathered[:, :d]
    pos_digits = gathered[:, d:d + 2].astype(jnp.int32)
    all_positives = pos_digits[:, 0] * 32 + pos_digits[:, 1]
    digits = jnp.stack([slots // 16384, (slots // 128) % 128, slots % 128], axis=1)
    code = jnp.zeros((slots.shape[0], STAT), jnp.bfloat16).at[:, :3].set(digits.astype(jnp.bfloat16))
    fresh_ext = lax.all_gather(
        jnp.concatenate([fresh_keys, code], axis=1), ("dp", "queue"), axis=0, tiled=True
    )
    fresh_all = fresh_ext[:, :d]
    got = fresh_ext[:, d:d + 3].astype(jnp.int32)
    slots_all = got[:, 0] * 16384 + got[:, 1] * 128 + got[:, 2]

    device_index = _device_index()
    queue_scores = score_rows(all_queries, queue_keys)
    fresh_scores = score_rows(all_queries, fresh_keys)
    local_top = jnp.maximum(jnp.max(queue_scores, axis=1), jnp.max(fresh_scores, axis=1))
    queue_exp = jnp.exp(queue_scores - local_top[:, None])
    fresh_exp = jnp.exp(fresh_scores - local_top[:, None])
    local_sum = jnp.sum(queue_exp, axis=1) + jnp.sum(fresh_exp, axis=1)
    local_pulled = jnp.dot(
        queue_exp.astype(jnp.bfloat16), queue_keys, preferred_element_type=jnp.float32
    ) + jnp.dot(fresh_exp.astype(jnp.bfloat16), fresh_keys, preferred_element_type=jnp.float32)
    fresh_ids = device_index * fresh_keys.shape[0] + jnp.arange(fresh_keys.shape[0], dtype=jnp.int32)
    is_positive = all_positives[:, None] == fresh_ids[None, :]
    positive_total = jnp.sum(jnp.where(is_positive, fresh_scores, 0.0))
    stats = jnp.zeros((total_rows, STAT), jnp.float32)
    stats = stats.at[:, 0].set(local_top).at[:, 1].set(local_sum)
    halves = (2, n // 2, own_rows)
    combined, loss_tile = combine(
        local_pulled.reshape(halves + (d,)),
        stats.reshape(halves + (STAT,)),
        jnp.full((8, 128), positive_total, jnp.float32),
        d,
    )
    sum_rows = combined[:, d + 1]
    pulled = combined[:, :d]
    queue_index = lax.axis_index("queue")
    local_start = queue_index * own_rows
    positive_rows = lax.dynamic_slice_in_dim(positives, local_start, own_rows, 0)
    positive_keys = jnp.take(fresh_all, positive_rows, axis=0).astype(jnp.float32)
    query_grad = pulled / sum_rows[:, None] - positive_keys
    mean_loss = loss_tile[0, 0] / total_rows
    held_rows = queue_keys.shape[0]
    local_slot = slots_all - device_index * held_rows
    picks = jnp.arange(held_rows, dtype=jnp.int32)[:, None] == local_slot[None, :]
    inserted = jnp.dot(picks.astype(jnp.bfloat16), fresh_all, preferred_element_type=jnp.float32)
    replaced = jnp.any(picks, axis=1)
    new_queue = jnp.where(replaced[:, None], inserted.astype(jnp.bfloat16), queue_keys)
    return (query_grad, mean_loss, new_queue)


def solution(mesh):
    placed = (
        P(("dp", "queue"), None),
        P(("dp", "queue"), None),
        P(("dp", "queue")),
        P("dp", None),
        P("dp"),
    )
    return jax.shard_map(
        shards,
        mesh=mesh,
        in_specs=placed,
        out_specs=(P(("dp", "queue"), None), P(), P(("dp", "queue"), None)),
        check_vma=False,
    )
```

```python
import functools

import jax
import jax.numpy as jnp
from jax import lax
from jax.experimental import pallas as pl
from jax.experimental.pallas import tpu as pltpu
from jax.sharding import PartitionSpec as P

MESH = pl.DeviceIdType.MESH
STAT = 128


def score_rows(query_rows, key_rows):
    return lax.dot_general(
        query_rows, key_rows, (((1,), (1,)), ((), ())), preferred_element_type=jnp.float32
    )


def _device_index():
    return lax.axis_index("dp") * lax.axis_size("queue") + lax.axis_index("queue")


def _wait_bytes(src, dst, send_sem, recv_sem, device_id):
    total = pltpu.make_async_remote_copy(
        src_ref=src, dst_ref=dst, send_sem=send_sem, recv_sem=recv_sem,
        device_id=device_id, device_id_type=MESH,
    )
    total.wait_send()
    total.wait_recv()


def gather_kernel(x_ref, o_ref, buf, sems):
    dp = lax.axis_index("dp")
    y, c = dp // 2, lax.rem(dp, 2)
    ys = lax.axis_size("dp") // 2
    qi = lax.axis_index("queue")
    partner = (dp + 1 - 2 * c, qi)

    def along(k):
        return (lax.rem(y + k, ys) * 2 + c, qi)

    barrier = pltpu.get_barrier_semaphore()
    pl.semaphore_signal(barrier, inc=1, device_id=partner, device_id_type=MESH)
    for k in range(1, ys):
        pl.semaphore_signal(barrier, inc=1, device_id=along(k), device_id_type=MESH)
    pl.semaphore_wait(barrier, ys)

    mine = pltpu.make_async_copy(x_ref, buf.at[c, y], sems.at[4])
    mine.start()
    first = [
        pltpu.make_async_remote_copy(
            src_ref=x_ref, dst_ref=buf.at[c, y], send_sem=sems.at[0], recv_sem=sems.at[1],
            device_id=dst, device_id_type=MESH,
        )
        for dst in [partner] + [along(k) for k in range(1, ys)]
    ]
    for copy in first:
        copy.start()
    _wait_bytes(buf.at[0], buf.at[0], sems.at[0], sems.at[1], partner)
    mine.wait()
    second = [
        pltpu.make_async_remote_copy(
            src_ref=buf.at[c, lax.rem(y + k, ys)], dst_ref=buf.at[c, lax.rem(y + k, ys)],
            send_sem=sems.at[2], recv_sem=sems.at[3], device_id=partner, device_id_type=MESH,
        )
        for k in range(1, ys)
    ]
    for copy in second:
        copy.start()
    _wait_bytes(buf.at[0, pl.ds(0, ys - 1)], buf.at[0, pl.ds(0, ys - 1)], sems.at[2], sems.at[3], partner)
    o_ref[...] = buf[...]


def gather_dp(x, ys):
    return pl.pallas_call(
        gather_kernel,
        out_shape=jax.ShapeDtypeStruct((2, ys) + x.shape, x.dtype),
        in_specs=[pl.BlockSpec(memory_space=pltpu.VMEM)],
        out_specs=pl.BlockSpec(memory_space=pltpu.VMEM),
        scratch_shapes=[
            pltpu.VMEM((2, ys) + x.shape, x.dtype),
            pltpu.SemaphoreType.DMA((5,)),
        ],
        compiler_params=pltpu.CompilerParams(collective_id=1, has_side_effects=True),
    )(x)


def _merge(blocks, at):
    top = blocks[0][:, at:at + 1]
    for b in blocks[1:]:
        top = jnp.maximum(top, b[:, at:at + 1])
    acc = blocks[0] * jnp.exp(blocks[0][:, at:at + 1] - top)
    for b in blocks[1:]:
        acc = acc + b * jnp.exp(b[:, at:at + 1] - top)
    col = lax.broadcasted_iota(jnp.int32, acc.shape, 1)
    return jnp.where(col == at, top, acc)


TREES = (("x", "z", "y"), ("z", "y", "x"), ("y", "x", "z"))


def combine_kernel(d, side, p_ref, s_ref, pos_ref, o_ref, loss_ref, own_p, own_s, pair_p, pair_s,
                   send1, recv1, send2, recv2, send3, recv3, loss_buf, loss_pair, sems):
    r = side
    part = d // len(TREES)
    g = p_ref.shape[1]
    dp = lax.axis_index("dp")
    y, c = dp // 2, lax.rem(dp, 2)
    qi = lax.axis_index("queue")
    mine_at = {"y": y, "z": qi // r, "x": lax.rem(qi, r)}
    partner = (dp + 1 - 2 * c, qi)

    def device(at):
        return (at["y"] * 2 + c, at["z"] * r + at["x"])

    def along(axis, j):
        at = dict(mine_at)
        at[axis] = j
        return device(at)

    barrier = pltpu.get_barrier_semaphore()
    pl.semaphore_signal(barrier, inc=1, device_id=partner, device_id_type=MESH)
    for axis in ("x", "z", "y"):
        for k in range(1, r):
            pl.semaphore_signal(barrier, inc=1, device_id=along(axis, lax.rem(mine_at[axis] + k, r)),
                                device_id_type=MESH)
    pl.semaphore_wait(barrier, 1 + 3 * (r - 1))

    pair_copies = [
        pltpu.make_async_remote_copy(
            src_ref=src.at[1 - c], dst_ref=dst, send_sem=sems.at[2 * i], recv_sem=sems.at[2 * i + 1],
            device_id=partner, device_id_type=MESH,
        )
        for i, (src, dst) in enumerate(((p_ref, pair_p), (s_ref, pair_s)))
    ]
    for copy in pair_copies:
        copy.start()
    mine = [pltpu.make_async_copy(src.at[c], dst, sems.at[4 + i])
            for i, (src, dst) in enumerate(((p_ref, own_p), (s_ref, own_s)))]
    for copy in mine:
        copy.start()
    for copy in mine + pair_copies:
        copy.wait()

    def merge_pair(k, carry):
        a, b = own_s[k], pair_s[k]
        top = jnp.maximum(a[:, 0:1], b[:, 0:1])
        wa, wb = jnp.exp(a[:, 0:1] - top), jnp.exp(b[:, 0:1] - top)
        pulled = own_p[k] * wa + pair_p[k] * wb
        col = lax.broadcasted_iota(jnp.int32, a.shape, 1)
        stats = jnp.where(col == 0, top, a * wa + b * wb)
        at = {"y": k // (r * r), "z": lax.rem(k // r, r), "x": lax.rem(k, r)}
        for t, (a1, a2, a3) in enumerate(TREES):
            slot = at[a2] * r + at[a3]
            send1[t, at[a1], slot, :, :part] = pulled[:, t * part:(t + 1) * part]
            send1[t, at[a1], slot, :, part:] = stats
        return carry

    lax.fori_loop(0, g, merge_pair, 0)

    def level(lvl, send, recv, blocks):
        sent = []
        for t, axes in enumerate(TREES):
            axis = axes[lvl]
            me_a = mine_at[axis]
            for k in range(1, r):
                dst = lax.rem(me_a + k, r)
                copy = pltpu.make_async_remote_copy(
                    src_ref=send.at[t, pl.ds(dst * blocks, blocks)], dst_ref=recv.at[t, me_a],
                    send_sem=sems.at[6 + 2 * (3 * lvl + t)], recv_sem=sems.at[7 + 2 * (3 * lvl + t)],
                    device_id=along(axis, dst), device_id_type=MESH,
                )
                copy.start()
            recv[t, me_a] = send[t, pl.ds(me_a * blocks, blocks)]
            sent.append(axis)
        for t, axis in enumerate(sent):
            _wait_bytes(recv.at[t, pl.ds(0, r - 1)], recv.at[t, pl.ds(0, r - 1)],
                        sems.at[6 + 2 * (3 * lvl + t)], sems.at[7 + 2 * (3 * lvl + t)],
                        along(axis, lax.rem(mine_at[axis] + 1, r)))

    def run_level1():
        sent_axes = []
        for t, axes in enumerate(TREES):
            axis = axes[0]
            me_a = mine_at[axis]
            for k in range(1, r):
                dst = lax.rem(me_a + k, r)
                pltpu.make_async_remote_copy(
                    src_ref=send1.at[t, dst], dst_ref=recv1.at[t, me_a],
                    send_sem=sems.at[6 + 2 * t], recv_sem=sems.at[7 + 2 * t],
                    device_id=along(axis, dst), device_id_type=MESH,
                ).start()
            recv1[t, me_a] = send1[t, me_a]
            sent_axes.append(axis)
        for t, axis in enumerate(sent_axes):
            _wait_bytes(send1.at[t, pl.ds(0, r - 1)], recv1.at[t, pl.ds(0, r - 1)],
                        sems.at[6 + 2 * t], sems.at[7 + 2 * t],
                        along(axis, lax.rem(mine_at[axis] + 1, r)))

    run_level1()

    def merge1(b, carry):
        for t in range(len(TREES)):
            send2[t, b] = _merge([recv1[t, i, b] for i in range(r)], part)
        return carry

    lax.fori_loop(0, r * r, merge1, 0)
    level(1, send2, recv2, r)

    for t in range(len(TREES)):
        for a3 in range(r):
            send3[t, a3] = _merge([recv2[t, i, a3] for i in range(r)], part)
    level(2, send3, recv3, 1)

    finals = [_merge([recv3[t, i, 0] for i in range(r)], part) for t in range(len(TREES))]
    stats = finals[0][:, part:]
    for t in range(len(TREES)):
        o_ref[:, t * part:(t + 1) * part] = finals[t][:, :part]
    o_ref[:, d:] = stats
    top = stats[:, 0:1]
    sums = stats[:, 1:2]

    total = jnp.broadcast_to(jnp.sum(top + jnp.log(sums)) - pos_ref[0:1, 0:1], loss_ref.shape)
    for n_axis, axis in enumerate(("x", "z", "y")):
        me_a = mine_at[axis]
        loss_buf[n_axis, me_a] = total
        for k in range(1, r):
            dst = lax.rem(me_a + k, r)
            pltpu.make_async_remote_copy(
                src_ref=loss_buf.at[n_axis, me_a], dst_ref=loss_buf.at[n_axis, me_a],
                send_sem=sems.at[24 + 2 * n_axis], recv_sem=sems.at[25 + 2 * n_axis],
                device_id=along(axis, dst), device_id_type=MESH,
            ).start()
        _wait_bytes(loss_buf.at[n_axis, pl.ds(0, r - 1)], loss_buf.at[n_axis, pl.ds(0, r - 1)],
                    sems.at[24 + 2 * n_axis], sems.at[25 + 2 * n_axis],
                    along(axis, lax.rem(me_a + 1, r)))
        total = loss_buf[n_axis, 0]
        for i in range(1, r):
            total = total + loss_buf[n_axis, i]
    loss_pair[c] = total
    to_pair_loss = pltpu.make_async_remote_copy(
        src_ref=loss_pair.at[c], dst_ref=loss_pair.at[c], send_sem=sems.at[30], recv_sem=sems.at[31],
        device_id=partner, device_id_type=MESH,
    )
    to_pair_loss.start()
    to_pair_loss.wait()
    loss_ref[...] = loss_pair[0] + loss_pair[1]


def combine(pulled, stats, pos, d, side):
    g, rows = pulled.shape[1:3]
    width = d + stats.shape[3]
    trees = len(TREES)
    block = (rows, d // trees + STAT)
    return pl.pallas_call(
        functools.partial(combine_kernel, d, side),
        out_shape=(
            jax.ShapeDtypeStruct((rows, width), jnp.float32),
            jax.ShapeDtypeStruct((8, 128), jnp.float32),
        ),
        in_specs=[
            pl.BlockSpec(memory_space=pl.ANY),
            pl.BlockSpec(memory_space=pl.ANY),
            pl.BlockSpec(memory_space=pltpu.VMEM),
        ],
        out_specs=(
            pl.BlockSpec(memory_space=pltpu.VMEM),
            pl.BlockSpec(memory_space=pltpu.VMEM),
        ),
        scratch_shapes=[
            pltpu.VMEM((g, rows, d), jnp.float32),
            pltpu.VMEM((g, rows, width - d), jnp.float32),
            pltpu.VMEM((g, rows, d), jnp.float32),
            pltpu.VMEM((g, rows, width - d), jnp.float32),
            pltpu.VMEM((trees, side, side * side) + block, jnp.float32),
            pltpu.VMEM((trees, side, side * side) + block, jnp.float32),
            pltpu.VMEM((trees, side * side) + block, jnp.float32),
            pltpu.VMEM((trees, side, side) + block, jnp.float32),
            pltpu.VMEM((trees, side) + block, jnp.float32),
            pltpu.VMEM((trees, side, 1) + block, jnp.float32),
            pltpu.VMEM((3, side, 8, 128), jnp.float32),
            pltpu.VMEM((2, 8, 128), jnp.float32),
            pltpu.SemaphoreType.DMA((32,)),
        ],
        compiler_params=pltpu.CompilerParams(collective_id=0, has_side_effects=True),
    )(pulled, stats, pos)


def shards(queue_keys, fresh_keys, slots, queries, positives):
    dp_size = lax.axis_size("dp")
    queue_size = lax.axis_size("queue")
    n = dp_size * queue_size
    assert queue_size == (dp_size // 2) ** 2
    d = queries.shape[1]
    pos_code = jnp.zeros((queries.shape[0], STAT), jnp.bfloat16)
    pos_code = pos_code.at[:, 0].set((positives // 32).astype(jnp.bfloat16))
    pos_code = pos_code.at[:, 1].set((positives % 32).astype(jnp.bfloat16))
    gathered = gather_dp(jnp.concatenate([queries, pos_code], axis=1), dp_size // 2)
    total_rows = dp_size * queries.shape[0]
    own_rows = total_rows // n
    gathered = gathered.reshape(total_rows, d + STAT)
    all_queries = gathered[:, :d]
    pos_digits = gathered[:, d:d + 2].astype(jnp.int32)
    all_positives = pos_digits[:, 0] * 32 + pos_digits[:, 1]
    digits = jnp.stack([slots // 16384, (slots // 128) % 128, slots % 128], axis=1)
    code = jnp.zeros((slots.shape[0], STAT), jnp.bfloat16).at[:, :3].set(digits.astype(jnp.bfloat16))
    fresh_ext = lax.all_gather(
        jnp.concatenate([fresh_keys, code], axis=1), ("dp", "queue"), axis=0, tiled=True
    )
    fresh_all = fresh_ext[:, :d]
    got = fresh_ext[:, d:d + 3].astype(jnp.int32)
    slots_all = got[:, 0] * 16384 + got[:, 1] * 128 + got[:, 2]

    device_index = _device_index()
    queue_scores = score_rows(all_queries, queue_keys)
    fresh_scores = score_rows(all_queries, fresh_keys)
    local_top = jnp.maximum(jnp.max(queue_scores, axis=1), jnp.max(fresh_scores, axis=1))
    queue_exp = jnp.exp(queue_scores - local_top[:, None])
    fresh_exp = jnp.exp(fresh_scores - local_top[:, None])
    local_sum = jnp.sum(queue_exp, axis=1) + jnp.sum(fresh_exp, axis=1)
    local_pulled = jnp.dot(
        queue_exp.astype(jnp.bfloat16), queue_keys, preferred_element_type=jnp.float32
    ) + jnp.dot(fresh_exp.astype(jnp.bfloat16), fresh_keys, preferred_element_type=jnp.float32)
    fresh_ids = device_index * fresh_keys.shape[0] + jnp.arange(fresh_keys.shape[0], dtype=jnp.int32)
    is_positive = all_positives[:, None] == fresh_ids[None, :]
    positive_total = jnp.sum(jnp.where(is_positive, fresh_scores, 0.0))
    stats = jnp.zeros((total_rows, STAT), jnp.float32)
    stats = stats.at[:, 0].set(local_top).at[:, 1].set(local_sum)
    halves = (2, n // 2, own_rows)
    combined, loss_tile = combine(
        local_pulled.reshape(halves + (d,)),
        stats.reshape(halves + (STAT,)),
        jnp.full((8, 128), positive_total, jnp.float32),
        d,
        dp_size // 2,
    )
    sum_rows = combined[:, d + 1]
    pulled = combined[:, :d]
    queue_index = lax.axis_index("queue")
    local_start = queue_index * own_rows
    positive_rows = lax.dynamic_slice_in_dim(positives, local_start, own_rows, 0)
    positive_keys = jnp.take(fresh_all, positive_rows, axis=0).astype(jnp.float32)
    query_grad = pulled / sum_rows[:, None] - positive_keys
    mean_loss = loss_tile[0, 0] / total_rows
    held_rows = queue_keys.shape[0]
    local_slot = slots_all - device_index * held_rows
    picks = jnp.arange(held_rows, dtype=jnp.int32)[:, None] == local_slot[None, :]
    inserted = jnp.dot(picks.astype(jnp.bfloat16), fresh_all, preferred_element_type=jnp.float32)
    replaced = jnp.any(picks, axis=1)
    new_queue = jnp.where(replaced[:, None], inserted.astype(jnp.bfloat16), queue_keys)
    return (query_grad, mean_loss, new_queue)


def solution(mesh):
    placed = (
        P(("dp", "queue"), None),
        P(("dp", "queue"), None),
        P(("dp", "queue")),
        P("dp", None),
        P("dp"),
    )
    return jax.shard_map(
        shards,
        mesh=mesh,
        in_specs=placed,
        out_specs=(P(("dp", "queue"), None), P(), P(("dp", "queue"), None)),
        check_vma=False,
    )
```

```python
import functools

import jax
import jax.numpy as jnp
from jax import lax
from jax.experimental import pallas as pl
from jax.experimental.pallas import tpu as pltpu
from jax.sharding import PartitionSpec as P

MESH = pl.DeviceIdType.MESH
STAT = 128
FRESH_HELD = 8


def score_rows(query_rows, key_rows):
    return lax.dot_general(
        query_rows, key_rows, (((1,), (1,)), ((), ())), preferred_element_type=jnp.float32
    )


def _device_index():
    return lax.axis_index("dp") * lax.axis_size("queue") + lax.axis_index("queue")


def _wait_bytes(src, dst, send_sem, recv_sem, device_id):
    total = pltpu.make_async_remote_copy(
        src_ref=src, dst_ref=dst, send_sem=send_sem, recv_sem=recv_sem,
        device_id=device_id, device_id_type=MESH,
    )
    total.wait_send()
    total.wait_recv()


def partial_kernel(q_ref, k_ref, f_ref, p_ref, s_ref):
    q = q_ref[...]
    dims = (((1,), (1,)), ((), ()))
    scores = lax.dot_general(q, k_ref[...], dims, preferred_element_type=jnp.float32)
    fresh = lax.dot_general(q, f_ref[...], dims, preferred_element_type=jnp.float32)
    held = lax.broadcasted_iota(jnp.int32, fresh.shape, 1) < FRESH_HELD
    fresh = jnp.where(held, fresh, -jnp.inf)
    top = jnp.maximum(jnp.max(scores, axis=1, keepdims=True), jnp.max(fresh, axis=1, keepdims=True))
    weights = jnp.exp(scores - top)
    fresh_weights = jnp.exp(fresh - top)
    total = jnp.sum(weights, axis=1, keepdims=True) + jnp.sum(fresh_weights, axis=1, keepdims=True)
    p_ref[...] = jnp.dot(
        weights.astype(jnp.bfloat16), k_ref[...], preferred_element_type=jnp.float32
    ) + jnp.dot(fresh_weights.astype(jnp.bfloat16), f_ref[...], preferred_element_type=jnp.float32)
    col = lax.broadcasted_iota(jnp.int32, s_ref.shape, 1)
    s_ref[...] = jnp.where(col == 0, top, jnp.where(col == 1, total, 0.0))


def local_partials(queries, keys, fresh_padded, block):
    rows, d = queries.shape
    return pl.pallas_call(
        partial_kernel,
        grid=(rows // block,),
        out_shape=(
            jax.ShapeDtypeStruct((rows, d), jnp.float32),
            jax.ShapeDtypeStruct((rows, STAT), jnp.float32),
        ),
        in_specs=[
            pl.BlockSpec((block, d), lambda i: (i, 0)),
            pl.BlockSpec(keys.shape, lambda i: (0, 0)),
            pl.BlockSpec(fresh_padded.shape, lambda i: (0, 0)),
        ],
        out_specs=(
            pl.BlockSpec((block, d), lambda i: (i, 0)),
            pl.BlockSpec((block, STAT), lambda i: (i, 0)),
        ),
        compiler_params=pltpu.CompilerParams(vmem_limit_bytes=60 * 1024 * 1024),
    )(queries, keys, fresh_padded)


def gather_kernel(x_ref, o_ref, buf, sems):
    dp = lax.axis_index("dp")
    y, c = dp // 2, lax.rem(dp, 2)
    ys = lax.axis_size("dp") // 2
    qi = lax.axis_index("queue")
    partner = (dp + 1 - 2 * c, qi)

    def along(k):
        return (lax.rem(y + k, ys) * 2 + c, qi)

    barrier = pltpu.get_barrier_semaphore()
    pl.semaphore_signal(barrier, inc=1, device_id=partner, device_id_type=MESH)
    for k in range(1, ys):
        pl.semaphore_signal(barrier, inc=1, device_id=along(k), device_id_type=MESH)
    pl.semaphore_wait(barrier, ys)

    mine = pltpu.make_async_copy(x_ref, buf.at[c, y], sems.at[4])
    mine.start()
    first = [
        pltpu.make_async_remote_copy(
            src_ref=x_ref, dst_ref=buf.at[c, y], send_sem=sems.at[0], recv_sem=sems.at[1],
            device_id=dst, device_id_type=MESH,
        )
        for dst in [partner] + [along(k) for k in range(1, ys)]
    ]
    for copy in first:
        copy.start()
    _wait_bytes(buf.at[0], buf.at[0], sems.at[0], sems.at[1], partner)
    mine.wait()
    second = [
        pltpu.make_async_remote_copy(
            src_ref=buf.at[c, lax.rem(y + k, ys)], dst_ref=buf.at[c, lax.rem(y + k, ys)],
            send_sem=sems.at[2], recv_sem=sems.at[3], device_id=partner, device_id_type=MESH,
        )
        for k in range(1, ys)
    ]
    for copy in second:
        copy.start()
    _wait_bytes(buf.at[0, pl.ds(0, ys - 1)], buf.at[0, pl.ds(0, ys - 1)], sems.at[2], sems.at[3], partner)
    o_ref[...] = buf[...]


def gather_dp(x, ys):
    return pl.pallas_call(
        gather_kernel,
        out_shape=jax.ShapeDtypeStruct((2, ys) + x.shape, x.dtype),
        in_specs=[pl.BlockSpec(memory_space=pltpu.VMEM)],
        out_specs=pl.BlockSpec(memory_space=pltpu.VMEM),
        scratch_shapes=[
            pltpu.VMEM((2, ys) + x.shape, x.dtype),
            pltpu.SemaphoreType.DMA((5,)),
        ],
        compiler_params=pltpu.CompilerParams(collective_id=1, has_side_effects=True),
    )(x)


def _merge(blocks, at):
    top = blocks[0][:, at:at + 1]
    for b in blocks[1:]:
        top = jnp.maximum(top, b[:, at:at + 1])
    acc = blocks[0] * jnp.exp(blocks[0][:, at:at + 1] - top)
    for b in blocks[1:]:
        acc = acc + b * jnp.exp(b[:, at:at + 1] - top)
    col = lax.broadcasted_iota(jnp.int32, acc.shape, 1)
    return jnp.where(col == at, top, acc)


TREES = (("x", "z", "y"), ("z", "y", "x"), ("y", "x", "z"))


def combine_kernel(d, side, p_ref, s_ref, pos_ref, o_ref, loss_ref, own_p, own_s, pair_p, pair_s,
                   send1, recv1, send2, recv2, send3, recv3, loss_buf, loss_pair, sems):
    r = side
    part = d // len(TREES)
    g = p_ref.shape[1]
    dp = lax.axis_index("dp")
    y, c = dp // 2, lax.rem(dp, 2)
    qi = lax.axis_index("queue")
    mine_at = {"y": y, "z": qi // r, "x": lax.rem(qi, r)}
    partner = (dp + 1 - 2 * c, qi)

    def device(at):
        return (at["y"] * 2 + c, at["z"] * r + at["x"])

    def along(axis, j):
        at = dict(mine_at)
        at[axis] = j
        return device(at)

    barrier = pltpu.get_barrier_semaphore()
    pl.semaphore_signal(barrier, inc=1, device_id=partner, device_id_type=MESH)
    for axis in ("x", "z", "y"):
        for k in range(1, r):
            pl.semaphore_signal(barrier, inc=1, device_id=along(axis, lax.rem(mine_at[axis] + k, r)),
                                device_id_type=MESH)
    pl.semaphore_wait(barrier, 1 + 3 * (r - 1))

    pair_copies = [
        pltpu.make_async_remote_copy(
            src_ref=src.at[1 - c], dst_ref=dst, send_sem=sems.at[2 * i], recv_sem=sems.at[2 * i + 1],
            device_id=partner, device_id_type=MESH,
        )
        for i, (src, dst) in enumerate(((p_ref, pair_p), (s_ref, pair_s)))
    ]
    for copy in pair_copies:
        copy.start()
    mine = [pltpu.make_async_copy(src.at[c], dst, sems.at[4 + i])
            for i, (src, dst) in enumerate(((p_ref, own_p), (s_ref, own_s)))]
    for copy in mine:
        copy.start()
    for copy in mine + pair_copies:
        copy.wait()

    def merge_pair(k, carry):
        a, b = own_s[k], pair_s[k]
        top = jnp.maximum(a[:, 0:1], b[:, 0:1])
        wa, wb = jnp.exp(a[:, 0:1] - top), jnp.exp(b[:, 0:1] - top)
        pulled = own_p[k] * wa + pair_p[k] * wb
        col = lax.broadcasted_iota(jnp.int32, a.shape, 1)
        stats = jnp.where(col == 0, top, a * wa + b * wb)
        at = {"y": k // (r * r), "z": lax.rem(k // r, r), "x": lax.rem(k, r)}
        for t, (a1, a2, a3) in enumerate(TREES):
            slot = at[a2] * r + at[a3]
            send1[t, at[a1], slot, :, :part] = pulled[:, t * part:(t + 1) * part]
            send1[t, at[a1], slot, :, part:] = stats
        return carry

    lax.fori_loop(0, g, merge_pair, 0)

    def level(lvl, send, recv, blocks):
        sent = []
        for t, axes in enumerate(TREES):
            axis = axes[lvl]
            me_a = mine_at[axis]
            for k in range(1, r):
                dst = lax.rem(me_a + k, r)
                copy = pltpu.make_async_remote_copy(
                    src_ref=send.at[t, pl.ds(dst * blocks, blocks)], dst_ref=recv.at[t, me_a],
                    send_sem=sems.at[6 + 2 * (3 * lvl + t)], recv_sem=sems.at[7 + 2 * (3 * lvl + t)],
                    device_id=along(axis, dst), device_id_type=MESH,
                )
                copy.start()
            recv[t, me_a] = send[t, pl.ds(me_a * blocks, blocks)]
            sent.append(axis)
        for t, axis in enumerate(sent):
            _wait_bytes(recv.at[t, pl.ds(0, r - 1)], recv.at[t, pl.ds(0, r - 1)],
                        sems.at[6 + 2 * (3 * lvl + t)], sems.at[7 + 2 * (3 * lvl + t)],
                        along(axis, lax.rem(mine_at[axis] + 1, r)))

    def run_level1():
        sent_axes = []
        for t, axes in enumerate(TREES):
            axis = axes[0]
            me_a = mine_at[axis]
            for k in range(1, r):
                dst = lax.rem(me_a + k, r)
                pltpu.make_async_remote_copy(
                    src_ref=send1.at[t, dst], dst_ref=recv1.at[t, me_a],
                    send_sem=sems.at[6 + 2 * t], recv_sem=sems.at[7 + 2 * t],
                    device_id=along(axis, dst), device_id_type=MESH,
                ).start()
            recv1[t, me_a] = send1[t, me_a]
            sent_axes.append(axis)
        for t, axis in enumerate(sent_axes):
            _wait_bytes(send1.at[t, pl.ds(0, r - 1)], recv1.at[t, pl.ds(0, r - 1)],
                        sems.at[6 + 2 * t], sems.at[7 + 2 * t],
                        along(axis, lax.rem(mine_at[axis] + 1, r)))

    run_level1()

    def merge1(b, carry):
        for t in range(len(TREES)):
            send2[t, b] = _merge([recv1[t, i, b] for i in range(r)], part)
        return carry

    lax.fori_loop(0, r * r, merge1, 0)
    level(1, send2, recv2, r)

    for t in range(len(TREES)):
        for a3 in range(r):
            send3[t, a3] = _merge([recv2[t, i, a3] for i in range(r)], part)
    level(2, send3, recv3, 1)

    finals = [_merge([recv3[t, i, 0] for i in range(r)], part) for t in range(len(TREES))]
    stats = finals[0][:, part:]
    for t in range(len(TREES)):
        o_ref[:, t * part:(t + 1) * part] = finals[t][:, :part]
    o_ref[:, d:] = stats
    top = stats[:, 0:1]
    sums = stats[:, 1:2]

    total = jnp.broadcast_to(jnp.sum(top + jnp.log(sums)) - pos_ref[0:1, 0:1], loss_ref.shape)
    for n_axis, axis in enumerate(("x", "z", "y")):
        me_a = mine_at[axis]
        loss_buf[n_axis, me_a] = total
        for k in range(1, r):
            dst = lax.rem(me_a + k, r)
            pltpu.make_async_remote_copy(
                src_ref=loss_buf.at[n_axis, me_a], dst_ref=loss_buf.at[n_axis, me_a],
                send_sem=sems.at[24 + 2 * n_axis], recv_sem=sems.at[25 + 2 * n_axis],
                device_id=along(axis, dst), device_id_type=MESH,
            ).start()
        _wait_bytes(loss_buf.at[n_axis, pl.ds(0, r - 1)], loss_buf.at[n_axis, pl.ds(0, r - 1)],
                    sems.at[24 + 2 * n_axis], sems.at[25 + 2 * n_axis],
                    along(axis, lax.rem(me_a + 1, r)))
        total = loss_buf[n_axis, 0]
        for i in range(1, r):
            total = total + loss_buf[n_axis, i]
    loss_pair[c] = total
    to_pair_loss = pltpu.make_async_remote_copy(
        src_ref=loss_pair.at[c], dst_ref=loss_pair.at[c], send_sem=sems.at[30], recv_sem=sems.at[31],
        device_id=partner, device_id_type=MESH,
    )
    to_pair_loss.start()
    to_pair_loss.wait()
    loss_ref[...] = loss_pair[0] + loss_pair[1]


def combine(pulled, stats, pos, d, side):
    g, rows = pulled.shape[1:3]
    width = d + stats.shape[3]
    trees = len(TREES)
    block = (rows, d // trees + STAT)
    return pl.pallas_call(
        functools.partial(combine_kernel, d, side),
        out_shape=(
            jax.ShapeDtypeStruct((rows, width), jnp.float32),
            jax.ShapeDtypeStruct((8, 128), jnp.float32),
        ),
        in_specs=[
            pl.BlockSpec(memory_space=pl.ANY),
            pl.BlockSpec(memory_space=pl.ANY),
            pl.BlockSpec(memory_space=pltpu.VMEM),
        ],
        out_specs=(
            pl.BlockSpec(memory_space=pltpu.VMEM),
            pl.BlockSpec(memory_space=pltpu.VMEM),
        ),
        scratch_shapes=[
            pltpu.VMEM((g, rows, d), jnp.float32),
            pltpu.VMEM((g, rows, width - d), jnp.float32),
            pltpu.VMEM((g, rows, d), jnp.float32),
            pltpu.VMEM((g, rows, width - d), jnp.float32),
            pltpu.VMEM((trees, side, side * side) + block, jnp.float32),
            pltpu.VMEM((trees, side, side * side) + block, jnp.float32),
            pltpu.VMEM((trees, side * side) + block, jnp.float32),
            pltpu.VMEM((trees, side, side) + block, jnp.float32),
            pltpu.VMEM((trees, side) + block, jnp.float32),
            pltpu.VMEM((trees, side, 1) + block, jnp.float32),
            pltpu.VMEM((3, side, 8, 128), jnp.float32),
            pltpu.VMEM((2, 8, 128), jnp.float32),
            pltpu.SemaphoreType.DMA((32,)),
        ],
        compiler_params=pltpu.CompilerParams(collective_id=0, has_side_effects=True),
    )(pulled, stats, pos)


def shards(queue_keys, fresh_keys, slots, queries, positives):
    dp_size = lax.axis_size("dp")
    queue_size = lax.axis_size("queue")
    n = dp_size * queue_size
    assert fresh_keys.shape[0] == FRESH_HELD
    assert queue_size == (dp_size // 2) ** 2
    d = queries.shape[1]
    pos_code = jnp.zeros((queries.shape[0], STAT), jnp.bfloat16)
    pos_code = pos_code.at[:, 0].set((positives // 32).astype(jnp.bfloat16))
    pos_code = pos_code.at[:, 1].set((positives % 32).astype(jnp.bfloat16))
    gathered = gather_dp(jnp.concatenate([queries, pos_code], axis=1), dp_size // 2)
    total_rows = dp_size * queries.shape[0]
    own_rows = total_rows // n
    gathered = gathered.reshape(total_rows, d + STAT)
    all_queries = gathered[:, :d]
    pos_digits = gathered[:, d:d + 2].astype(jnp.int32)
    all_positives = pos_digits[:, 0] * 32 + pos_digits[:, 1]
    digits = jnp.stack([slots // 16384, (slots // 128) % 128, slots % 128], axis=1)
    code = jnp.zeros((slots.shape[0], STAT), jnp.bfloat16).at[:, :3].set(digits.astype(jnp.bfloat16))
    fresh_ext = lax.all_gather(
        jnp.concatenate([fresh_keys, code], axis=1), ("dp", "queue"), axis=0, tiled=True
    )
    fresh_all = fresh_ext[:, :d]
    got = fresh_ext[:, d:d + 3].astype(jnp.int32)
    slots_all = got[:, 0] * 16384 + got[:, 1] * 128 + got[:, 2]

    device_index = _device_index()
    fresh_padded = jnp.zeros((STAT, d), fresh_keys.dtype).at[:fresh_keys.shape[0]].set(fresh_keys)
    local_pulled, stats = local_partials(all_queries, queue_keys, fresh_padded, min(256, total_rows))
    fresh_scores = score_rows(all_queries, fresh_keys)
    fresh_ids = device_index * fresh_keys.shape[0] + jnp.arange(fresh_keys.shape[0], dtype=jnp.int32)
    is_positive = all_positives[:, None] == fresh_ids[None, :]
    positive_total = jnp.sum(jnp.where(is_positive, fresh_scores, 0.0))
    halves = (2, n // 2, own_rows)
    combined, loss_tile = combine(
        local_pulled.reshape(halves + (d,)),
        stats.reshape(halves + (STAT,)),
        jnp.full((8, 128), positive_total, jnp.float32),
        d,
        dp_size // 2,
    )
    sum_rows = combined[:, d + 1]
    pulled = combined[:, :d]
    queue_index = lax.axis_index("queue")
    local_start = queue_index * own_rows
    positive_rows = lax.dynamic_slice_in_dim(positives, local_start, own_rows, 0)
    positive_keys = jnp.take(fresh_all, positive_rows, axis=0).astype(jnp.float32)
    query_grad = pulled / sum_rows[:, None] - positive_keys
    mean_loss = loss_tile[0, 0] / total_rows
    held_rows = queue_keys.shape[0]
    local_slot = slots_all - device_index * held_rows
    picks = jnp.arange(held_rows, dtype=jnp.int32)[:, None] == local_slot[None, :]
    inserted = jnp.dot(picks.astype(jnp.bfloat16), fresh_all, preferred_element_type=jnp.float32)
    replaced = jnp.any(picks, axis=1)
    new_queue = jnp.where(replaced[:, None], inserted.astype(jnp.bfloat16), queue_keys)
    return (query_grad, mean_loss, new_queue)


def solution(mesh):
    placed = (
        P(("dp", "queue"), None),
        P(("dp", "queue"), None),
        P(("dp", "queue")),
        P("dp", None),
        P("dp"),
    )
    return jax.shard_map(
        shards,
        mesh=mesh,
        in_specs=placed,
        out_specs=(P(("dp", "queue"), None), P(), P(("dp", "queue"), None)),
        check_vma=False,
    )
```

```python
import functools

import jax
import jax.numpy as jnp
from jax import lax
from jax.experimental import pallas as pl
from jax.experimental.pallas import tpu as pltpu
from jax.sharding import PartitionSpec as P

MESH = pl.DeviceIdType.MESH
STAT = 128
FRESH_HELD = 8


def score_rows(query_rows, key_rows):
    return lax.dot_general(
        query_rows, key_rows, (((1,), (1,)), ((), ())), preferred_element_type=jnp.float32
    )


def _device_index():
    return lax.axis_index("dp") * lax.axis_size("queue") + lax.axis_index("queue")


def _wait_bytes(src, dst, send_sem, recv_sem, device_id):
    total = pltpu.make_async_remote_copy(
        src_ref=src, dst_ref=dst, send_sem=send_sem, recv_sem=recv_sem,
        device_id=device_id, device_id_type=MESH,
    )
    total.wait_send()
    total.wait_recv()


def partial_kernel(q_ref, k_ref, f_ref, p_ref, s_ref):
    q = q_ref[:, :k_ref.shape[1]]
    dims = (((1,), (1,)), ((), ()))
    scores = lax.dot_general(q, k_ref[...], dims, preferred_element_type=jnp.float32)
    fresh = lax.dot_general(q, f_ref[...], dims, preferred_element_type=jnp.float32)
    held = lax.broadcasted_iota(jnp.int32, fresh.shape, 1) < FRESH_HELD
    fresh = jnp.where(held, fresh, -jnp.inf)
    top = jnp.maximum(jnp.max(scores, axis=1, keepdims=True), jnp.max(fresh, axis=1, keepdims=True))
    weights = jnp.exp(scores - top)
    fresh_weights = jnp.exp(fresh - top)
    total = jnp.sum(weights, axis=1, keepdims=True) + jnp.sum(fresh_weights, axis=1, keepdims=True)
    p_ref[...] = jnp.dot(
        weights.astype(jnp.bfloat16), k_ref[...], preferred_element_type=jnp.float32
    ) + jnp.dot(fresh_weights.astype(jnp.bfloat16), f_ref[...], preferred_element_type=jnp.float32)
    col = lax.broadcasted_iota(jnp.int32, s_ref.shape, 1)
    s_ref[...] = jnp.where(col == 0, top, jnp.where(col == 1, total, 0.0))


def local_partials(queries, keys, fresh_padded, block):
    rows, width = queries.shape
    d = keys.shape[1]
    return pl.pallas_call(
        partial_kernel,
        grid=(rows // block,),
        out_shape=(
            jax.ShapeDtypeStruct((rows, d), jnp.float32),
            jax.ShapeDtypeStruct((rows, STAT), jnp.float32),
        ),
        in_specs=[
            pl.BlockSpec((block, width), lambda i: (i, 0)),
            pl.BlockSpec(keys.shape, lambda i: (0, 0)),
            pl.BlockSpec(fresh_padded.shape, lambda i: (0, 0)),
        ],
        out_specs=(
            pl.BlockSpec((block, d), lambda i: (i, 0)),
            pl.BlockSpec((block, STAT), lambda i: (i, 0)),
        ),
        compiler_params=pltpu.CompilerParams(vmem_limit_bytes=60 * 1024 * 1024),
    )(queries, keys, fresh_padded)


def gather_kernel(x_ref, o_ref, buf, sems):
    dp = lax.axis_index("dp")
    y, c = dp // 2, lax.rem(dp, 2)
    ys = lax.axis_size("dp") // 2
    qi = lax.axis_index("queue")
    partner = (dp + 1 - 2 * c, qi)

    def along(k):
        return (lax.rem(y + k, ys) * 2 + c, qi)

    barrier = pltpu.get_barrier_semaphore()
    pl.semaphore_signal(barrier, inc=1, device_id=partner, device_id_type=MESH)
    for k in range(1, ys):
        pl.semaphore_signal(barrier, inc=1, device_id=along(k), device_id_type=MESH)
    pl.semaphore_wait(barrier, ys)

    mine = pltpu.make_async_copy(x_ref, buf.at[c, y], sems.at[4])
    mine.start()
    first = [
        pltpu.make_async_remote_copy(
            src_ref=x_ref, dst_ref=buf.at[c, y], send_sem=sems.at[0], recv_sem=sems.at[1],
            device_id=dst, device_id_type=MESH,
        )
        for dst in [partner] + [along(k) for k in range(1, ys)]
    ]
    for copy in first:
        copy.start()
    _wait_bytes(buf.at[0], buf.at[0], sems.at[0], sems.at[1], partner)
    mine.wait()
    second = [
        pltpu.make_async_remote_copy(
            src_ref=buf.at[c, lax.rem(y + k, ys)], dst_ref=buf.at[c, lax.rem(y + k, ys)],
            send_sem=sems.at[2], recv_sem=sems.at[3], device_id=partner, device_id_type=MESH,
        )
        for k in range(1, ys)
    ]
    for copy in second:
        copy.start()
    _wait_bytes(buf.at[0, pl.ds(0, ys - 1)], buf.at[0, pl.ds(0, ys - 1)], sems.at[2], sems.at[3], partner)
    o_ref[...] = buf[...]


def gather_dp(x, ys):
    return pl.pallas_call(
        gather_kernel,
        out_shape=jax.ShapeDtypeStruct((2, ys) + x.shape, x.dtype),
        in_specs=[pl.BlockSpec(memory_space=pltpu.VMEM)],
        out_specs=pl.BlockSpec(memory_space=pltpu.VMEM),
        scratch_shapes=[
            pltpu.VMEM((2, ys) + x.shape, x.dtype),
            pltpu.SemaphoreType.DMA((5,)),
        ],
        compiler_params=pltpu.CompilerParams(collective_id=1, has_side_effects=True),
    )(x)


def _merge(blocks, at):
    top = blocks[0][:, at:at + 1]
    for b in blocks[1:]:
        top = jnp.maximum(top, b[:, at:at + 1])
    acc = blocks[0] * jnp.exp(blocks[0][:, at:at + 1] - top)
    for b in blocks[1:]:
        acc = acc + b * jnp.exp(b[:, at:at + 1] - top)
    col = lax.broadcasted_iota(jnp.int32, acc.shape, 1)
    return jnp.where(col == at, top, acc)


TREES = (("x", "z", "y"), ("z", "y", "x"), ("y", "x", "z"))


def combine_kernel(d, side, p_ref, s_ref, pos_ref, o_ref, loss_ref, own_p, own_s, pair_p, pair_s,
                   send1, recv1, send2, recv2, send3, recv3, loss_buf, loss_pair, sems):
    r = side
    part = d // len(TREES)
    g = p_ref.shape[1]
    dp = lax.axis_index("dp")
    y, c = dp // 2, lax.rem(dp, 2)
    qi = lax.axis_index("queue")
    mine_at = {"y": y, "z": qi // r, "x": lax.rem(qi, r)}
    partner = (dp + 1 - 2 * c, qi)

    def device(at):
        return (at["y"] * 2 + c, at["z"] * r + at["x"])

    def along(axis, j):
        at = dict(mine_at)
        at[axis] = j
        return device(at)

    barrier = pltpu.get_barrier_semaphore()
    pl.semaphore_signal(barrier, inc=1, device_id=partner, device_id_type=MESH)
    for axis in ("x", "z", "y"):
        for k in range(1, r):
            pl.semaphore_signal(barrier, inc=1, device_id=along(axis, lax.rem(mine_at[axis] + k, r)),
                                device_id_type=MESH)
    pl.semaphore_wait(barrier, 1 + 3 * (r - 1))

    pair_copies = [
        pltpu.make_async_remote_copy(
            src_ref=src.at[1 - c], dst_ref=dst, send_sem=sems.at[2 * i], recv_sem=sems.at[2 * i + 1],
            device_id=partner, device_id_type=MESH,
        )
        for i, (src, dst) in enumerate(((p_ref, pair_p), (s_ref, pair_s)))
    ]
    for copy in pair_copies:
        copy.start()
    mine = [pltpu.make_async_copy(src.at[c], dst, sems.at[4 + i])
            for i, (src, dst) in enumerate(((p_ref, own_p), (s_ref, own_s)))]
    for copy in mine:
        copy.start()
    for copy in mine + pair_copies:
        copy.wait()

    def merge_pair(k, carry):
        a, b = own_s[k], pair_s[k]
        top = jnp.maximum(a[:, 0:1], b[:, 0:1])
        wa, wb = jnp.exp(a[:, 0:1] - top), jnp.exp(b[:, 0:1] - top)
        pulled = own_p[k] * wa + pair_p[k] * wb
        col = lax.broadcasted_iota(jnp.int32, a.shape, 1)
        stats = jnp.where(col == 0, top, a * wa + b * wb)
        at = {"y": k // (r * r), "z": lax.rem(k // r, r), "x": lax.rem(k, r)}
        for t, (a1, a2, a3) in enumerate(TREES):
            slot = at[a2] * r + at[a3]
            send1[t, at[a1], slot, :, :part] = pulled[:, t * part:(t + 1) * part]
            send1[t, at[a1], slot, :, part:] = stats
        return carry

    lax.fori_loop(0, g, merge_pair, 0)

    def level(lvl, send, recv, blocks):
        sent = []
        for t, axes in enumerate(TREES):
            axis = axes[lvl]
            me_a = mine_at[axis]
            for k in range(1, r):
                dst = lax.rem(me_a + k, r)
                copy = pltpu.make_async_remote_copy(
                    src_ref=send.at[t, pl.ds(dst * blocks, blocks)], dst_ref=recv.at[t, me_a],
                    send_sem=sems.at[6 + 2 * (3 * lvl + t)], recv_sem=sems.at[7 + 2 * (3 * lvl + t)],
                    device_id=along(axis, dst), device_id_type=MESH,
                )
                copy.start()
            recv[t, me_a] = send[t, pl.ds(me_a * blocks, blocks)]
            sent.append(axis)
        for t, axis in enumerate(sent):
            _wait_bytes(recv.at[t, pl.ds(0, r - 1)], recv.at[t, pl.ds(0, r - 1)],
                        sems.at[6 + 2 * (3 * lvl + t)], sems.at[7 + 2 * (3 * lvl + t)],
                        along(axis, lax.rem(mine_at[axis] + 1, r)))

    def run_level1():
        sent_axes = []
        for t, axes in enumerate(TREES):
            axis = axes[0]
            me_a = mine_at[axis]
            for k in range(1, r):
                dst = lax.rem(me_a + k, r)
                pltpu.make_async_remote_copy(
                    src_ref=send1.at[t, dst], dst_ref=recv1.at[t, me_a],
                    send_sem=sems.at[6 + 2 * t], recv_sem=sems.at[7 + 2 * t],
                    device_id=along(axis, dst), device_id_type=MESH,
                ).start()
            recv1[t, me_a] = send1[t, me_a]
            sent_axes.append(axis)
        for t, axis in enumerate(sent_axes):
            _wait_bytes(send1.at[t, pl.ds(0, r - 1)], recv1.at[t, pl.ds(0, r - 1)],
                        sems.at[6 + 2 * t], sems.at[7 + 2 * t],
                        along(axis, lax.rem(mine_at[axis] + 1, r)))

    run_level1()

    def merge1(b, carry):
        for t in range(len(TREES)):
            send2[t, b] = _merge([recv1[t, i, b] for i in range(r)], part)
        return carry

    lax.fori_loop(0, r * r, merge1, 0)
    level(1, send2, recv2, r)

    for t in range(len(TREES)):
        for a3 in range(r):
            send3[t, a3] = _merge([recv2[t, i, a3] for i in range(r)], part)
    level(2, send3, recv3, 1)

    finals = [_merge([recv3[t, i, 0] for i in range(r)], part) for t in range(len(TREES))]
    stats = finals[0][:, part:]
    for t in range(len(TREES)):
        o_ref[:, t * part:(t + 1) * part] = finals[t][:, :part]
    o_ref[:, d:] = stats
    top = stats[:, 0:1]
    sums = stats[:, 1:2]

    total = jnp.broadcast_to(jnp.sum(top + jnp.log(sums)) - pos_ref[0:1, 0:1], loss_ref.shape)
    for n_axis, axis in enumerate(("x", "z", "y")):
        me_a = mine_at[axis]
        loss_buf[n_axis, me_a] = total
        for k in range(1, r):
            dst = lax.rem(me_a + k, r)
            pltpu.make_async_remote_copy(
                src_ref=loss_buf.at[n_axis, me_a], dst_ref=loss_buf.at[n_axis, me_a],
                send_sem=sems.at[24 + 2 * n_axis], recv_sem=sems.at[25 + 2 * n_axis],
                device_id=along(axis, dst), device_id_type=MESH,
            ).start()
        _wait_bytes(loss_buf.at[n_axis, pl.ds(0, r - 1)], loss_buf.at[n_axis, pl.ds(0, r - 1)],
                    sems.at[24 + 2 * n_axis], sems.at[25 + 2 * n_axis],
                    along(axis, lax.rem(me_a + 1, r)))
        total = loss_buf[n_axis, 0]
        for i in range(1, r):
            total = total + loss_buf[n_axis, i]
    loss_pair[c] = total
    to_pair_loss = pltpu.make_async_remote_copy(
        src_ref=loss_pair.at[c], dst_ref=loss_pair.at[c], send_sem=sems.at[30], recv_sem=sems.at[31],
        device_id=partner, device_id_type=MESH,
    )
    to_pair_loss.start()
    to_pair_loss.wait()
    loss_ref[...] = loss_pair[0] + loss_pair[1]


def combine(pulled, stats, pos, d, side):
    g, rows = pulled.shape[1:3]
    width = d + stats.shape[3]
    trees = len(TREES)
    block = (rows, d // trees + STAT)
    return pl.pallas_call(
        functools.partial(combine_kernel, d, side),
        out_shape=(
            jax.ShapeDtypeStruct((rows, width), jnp.float32),
            jax.ShapeDtypeStruct((8, 128), jnp.float32),
        ),
        in_specs=[
            pl.BlockSpec(memory_space=pl.ANY),
            pl.BlockSpec(memory_space=pl.ANY),
            pl.BlockSpec(memory_space=pltpu.VMEM),
        ],
        out_specs=(
            pl.BlockSpec(memory_space=pltpu.VMEM),
            pl.BlockSpec(memory_space=pltpu.VMEM),
        ),
        scratch_shapes=[
            pltpu.VMEM((g, rows, d), jnp.float32),
            pltpu.VMEM((g, rows, width - d), jnp.float32),
            pltpu.VMEM((g, rows, d), jnp.float32),
            pltpu.VMEM((g, rows, width - d), jnp.float32),
            pltpu.VMEM((trees, side, side * side) + block, jnp.float32),
            pltpu.VMEM((trees, side, side * side) + block, jnp.float32),
            pltpu.VMEM((trees, side * side) + block, jnp.float32),
            pltpu.VMEM((trees, side, side) + block, jnp.float32),
            pltpu.VMEM((trees, side) + block, jnp.float32),
            pltpu.VMEM((trees, side, 1) + block, jnp.float32),
            pltpu.VMEM((3, side, 8, 128), jnp.float32),
            pltpu.VMEM((2, 8, 128), jnp.float32),
            pltpu.SemaphoreType.DMA((32,)),
        ],
        compiler_params=pltpu.CompilerParams(collective_id=0, has_side_effects=True),
    )(pulled, stats, pos)


def shards(queue_keys, fresh_keys, slots, queries, positives):
    dp_size = lax.axis_size("dp")
    queue_size = lax.axis_size("queue")
    n = dp_size * queue_size
    assert fresh_keys.shape[0] == FRESH_HELD
    assert queue_size == (dp_size // 2) ** 2
    d = queries.shape[1]
    pos_code = jnp.zeros((queries.shape[0], STAT), jnp.bfloat16)
    pos_code = pos_code.at[:, 0].set((positives // 32).astype(jnp.bfloat16))
    pos_code = pos_code.at[:, 1].set((positives % 32).astype(jnp.bfloat16))
    gathered = gather_dp(jnp.concatenate([queries, pos_code], axis=1), dp_size // 2)
    total_rows = dp_size * queries.shape[0]
    own_rows = total_rows // n
    gathered = gathered.reshape(total_rows, d + STAT)
    all_queries = gathered[:, :d]
    pos_digits = gathered[:, d:d + 2].astype(jnp.int32)
    all_positives = pos_digits[:, 0] * 32 + pos_digits[:, 1]
    digits = jnp.stack([slots // 16384, (slots // 128) % 128, slots % 128], axis=1)
    code = jnp.zeros((slots.shape[0], STAT), jnp.bfloat16).at[:, :3].set(digits.astype(jnp.bfloat16))
    fresh_ext = lax.all_gather(
        jnp.concatenate([fresh_keys, code], axis=1), ("dp", "queue"), axis=0, tiled=True
    )
    fresh_all = fresh_ext[:, :d]
    got = fresh_ext[:, d:d + 3].astype(jnp.int32)
    slots_all = got[:, 0] * 16384 + got[:, 1] * 128 + got[:, 2]

    device_index = _device_index()
    fresh_padded = jnp.zeros((STAT, d), fresh_keys.dtype).at[:fresh_keys.shape[0]].set(fresh_keys)
    local_pulled, stats = local_partials(gathered, queue_keys, fresh_padded, min(256, total_rows))
    fresh_scores = score_rows(all_queries, fresh_keys)
    fresh_ids = device_index * fresh_keys.shape[0] + jnp.arange(fresh_keys.shape[0], dtype=jnp.int32)
    is_positive = all_positives[:, None] == fresh_ids[None, :]
    positive_total = jnp.sum(jnp.where(is_positive, fresh_scores, 0.0))
    halves = (2, n // 2, own_rows)
    combined, loss_tile = combine(
        local_pulled.reshape(halves + (d,)),
        stats.reshape(halves + (STAT,)),
        jnp.full((8, 128), positive_total, jnp.float32),
        d,
        dp_size // 2,
    )
    sum_rows = combined[:, d + 1]
    pulled = combined[:, :d]
    queue_index = lax.axis_index("queue")
    local_start = queue_index * own_rows
    positive_rows = lax.dynamic_slice_in_dim(positives, local_start, own_rows, 0)
    positive_keys = jnp.take(fresh_all, positive_rows, axis=0).astype(jnp.float32)
    query_grad = pulled / sum_rows[:, None] - positive_keys
    mean_loss = loss_tile[0, 0] / total_rows
    held_rows = queue_keys.shape[0]
    local_slot = slots_all - device_index * held_rows
    picks = jnp.arange(held_rows, dtype=jnp.int32)[:, None] == local_slot[None, :]
    inserted = jnp.dot(picks.astype(jnp.bfloat16), fresh_all, preferred_element_type=jnp.float32)
    replaced = jnp.any(picks, axis=1)
    new_queue = jnp.where(replaced[:, None], inserted.astype(jnp.bfloat16), queue_keys)
    return (query_grad, mean_loss, new_queue)


def solution(mesh):
    placed = (
        P(("dp", "queue"), None),
        P(("dp", "queue"), None),
        P(("dp", "queue")),
        P("dp", None),
        P("dp"),
    )
    return jax.shard_map(
        shards,
        mesh=mesh,
        in_specs=placed,
        out_specs=(P(("dp", "queue"), None), P(), P(("dp", "queue"), None)),
        check_vma=False,
    )
```

```python
import functools

import jax
import jax.numpy as jnp
from jax import lax
from jax.experimental import pallas as pl
from jax.experimental.pallas import tpu as pltpu
from jax.sharding import PartitionSpec as P

MESH = pl.DeviceIdType.MESH
STAT = 128
FRESH_HELD = 8


def score_rows(query_rows, key_rows):
    return lax.dot_general(
        query_rows, key_rows, (((1,), (1,)), ((), ())), preferred_element_type=jnp.float32
    )


def _device_index():
    return lax.axis_index("dp") * lax.axis_size("queue") + lax.axis_index("queue")


def _wait_bytes(src, dst, send_sem, recv_sem, device_id):
    total = pltpu.make_async_remote_copy(
        src_ref=src, dst_ref=dst, send_sem=send_sem, recv_sem=recv_sem,
        device_id=device_id, device_id_type=MESH,
    )
    total.wait_send()
    total.wait_recv()


def partial_kernel(q_ref, k_ref, f_ref, p_ref, s_ref):
    q = q_ref[:, :k_ref.shape[1]]
    dims = (((1,), (1,)), ((), ()))
    scores = lax.dot_general(q, k_ref[...], dims, preferred_element_type=jnp.float32)
    fresh = lax.dot_general(q, f_ref[...], dims, preferred_element_type=jnp.float32)
    held = lax.broadcasted_iota(jnp.int32, fresh.shape, 1) < FRESH_HELD
    fresh = jnp.where(held, fresh, -jnp.inf)
    top = jnp.maximum(jnp.max(scores, axis=1, keepdims=True), jnp.max(fresh, axis=1, keepdims=True))
    weights = jnp.exp(scores - top)
    fresh_weights = jnp.exp(fresh - top)
    total = jnp.sum(weights, axis=1, keepdims=True) + jnp.sum(fresh_weights, axis=1, keepdims=True)
    p_ref[...] = jnp.dot(
        weights.astype(jnp.bfloat16), k_ref[...], preferred_element_type=jnp.float32
    ) + jnp.dot(fresh_weights.astype(jnp.bfloat16), f_ref[...], preferred_element_type=jnp.float32)
    col = lax.broadcasted_iota(jnp.int32, s_ref.shape, 1)
    s_ref[...] = jnp.where(col == 0, top, jnp.where(col == 1, total, 0.0))


def local_partials(queries, keys, fresh_padded, block):
    rows, width = queries.shape
    d = keys.shape[1]
    return pl.pallas_call(
        partial_kernel,
        grid=(rows // block,),
        out_shape=(
            jax.ShapeDtypeStruct((rows, d), jnp.float32),
            jax.ShapeDtypeStruct((rows, STAT), jnp.float32),
        ),
        in_specs=[
            pl.BlockSpec((block, width), lambda i: (i, 0)),
            pl.BlockSpec(keys.shape, lambda i: (0, 0)),
            pl.BlockSpec(fresh_padded.shape, lambda i: (0, 0)),
        ],
        out_specs=(
            pl.BlockSpec((block, d), lambda i: (i, 0)),
            pl.BlockSpec((block, STAT), lambda i: (i, 0)),
        ),
        compiler_params=pltpu.CompilerParams(vmem_limit_bytes=60 * 1024 * 1024),
    )(queries, keys, fresh_padded)


def gather_kernel(x_ref, o_ref, buf, sems):
    dp = lax.axis_index("dp")
    y, c = dp // 2, lax.rem(dp, 2)
    ys = lax.axis_size("dp") // 2
    qi = lax.axis_index("queue")
    partner = (dp + 1 - 2 * c, qi)

    def along(k):
        return (lax.rem(y + k, ys) * 2 + c, qi)

    barrier = pltpu.get_barrier_semaphore()
    pl.semaphore_signal(barrier, inc=1, device_id=partner, device_id_type=MESH)
    for k in range(1, ys):
        pl.semaphore_signal(barrier, inc=1, device_id=along(k), device_id_type=MESH)
    pl.semaphore_wait(barrier, ys)

    mine = pltpu.make_async_copy(x_ref, buf.at[c, y], sems.at[4])
    mine.start()
    first = [
        pltpu.make_async_remote_copy(
            src_ref=x_ref, dst_ref=buf.at[c, y], send_sem=sems.at[0], recv_sem=sems.at[1],
            device_id=dst, device_id_type=MESH,
        )
        for dst in [partner] + [along(k) for k in range(1, ys)]
    ]
    for copy in first:
        copy.start()
    _wait_bytes(buf.at[0], buf.at[0], sems.at[0], sems.at[1], partner)
    mine.wait()
    second = [
        pltpu.make_async_remote_copy(
            src_ref=buf.at[c, lax.rem(y + k, ys)], dst_ref=buf.at[c, lax.rem(y + k, ys)],
            send_sem=sems.at[2], recv_sem=sems.at[3], device_id=partner, device_id_type=MESH,
        )
        for k in range(1, ys)
    ]
    for copy in second:
        copy.start()
    _wait_bytes(buf.at[0, pl.ds(0, ys - 1)], buf.at[0, pl.ds(0, ys - 1)], sems.at[2], sems.at[3], partner)
    o_ref[...] = buf[...]


def gather_dp(x, ys):
    return pl.pallas_call(
        gather_kernel,
        out_shape=jax.ShapeDtypeStruct((2, ys) + x.shape, x.dtype),
        in_specs=[pl.BlockSpec(memory_space=pltpu.VMEM)],
        out_specs=pl.BlockSpec(memory_space=pltpu.VMEM),
        scratch_shapes=[
            pltpu.VMEM((2, ys) + x.shape, x.dtype),
            pltpu.SemaphoreType.DMA((5,)),
        ],
        compiler_params=pltpu.CompilerParams(collective_id=1, has_side_effects=True),
    )(x)


def _merge(blocks, at):
    top = blocks[0][:, at:at + 1]
    for b in blocks[1:]:
        top = jnp.maximum(top, b[:, at:at + 1])
    acc = blocks[0] * jnp.exp(blocks[0][:, at:at + 1] - top)
    for b in blocks[1:]:
        acc = acc + b * jnp.exp(b[:, at:at + 1] - top)
    col = lax.broadcasted_iota(jnp.int32, acc.shape, 1)
    return jnp.where(col == at, top, acc)


TREES = (("x", "z", "y"), ("z", "y", "x"), ("y", "x", "z"))


def combine_kernel(d, side, p_ref, s_ref, pos_ref, f_ref, o_ref, loss_ref, fresh_out, own_p, own_s,
                   pair_p, pair_s, send1, recv1, send2, recv2, send3, recv3, loss_buf, loss_pair,
                   fbuf, sems):
    r = side
    part = d // len(TREES)
    g = p_ref.shape[1]
    dp = lax.axis_index("dp")
    y, c = dp // 2, lax.rem(dp, 2)
    qi = lax.axis_index("queue")
    mine_at = {"y": y, "z": qi // r, "x": lax.rem(qi, r)}
    partner = (dp + 1 - 2 * c, qi)

    def device(at):
        return (at["y"] * 2 + c, at["z"] * r + at["x"])

    def along(axis, j):
        at = dict(mine_at)
        at[axis] = j
        return device(at)

    barrier = pltpu.get_barrier_semaphore()
    pl.semaphore_signal(barrier, inc=1, device_id=partner, device_id_type=MESH)
    for axis in ("x", "z", "y"):
        for k in range(1, r):
            pl.semaphore_signal(barrier, inc=1, device_id=along(axis, lax.rem(mine_at[axis] + k, r)),
                                device_id_type=MESH)
    pl.semaphore_wait(barrier, 1 + 3 * (r - 1))

    yi, zi, xi = mine_at["y"], mine_at["z"], mine_at["x"]
    own_fresh = pltpu.make_async_copy(f_ref, fbuf.at[yi, c, zi, xi], sems.at[40])
    own_fresh.start()

    def fresh_round(i, axis, src, dst_of):
        for k in range(1, r):
            dst = lax.rem(mine_at[axis] + k, r)
            pltpu.make_async_remote_copy(
                src_ref=src, dst_ref=dst_of(), send_sem=sems.at[32 + 2 * i], recv_sem=sems.at[33 + 2 * i],
                device_id=along(axis, dst), device_id_type=MESH,
            ).start()

    fresh_round(0, "x", f_ref, lambda: fbuf.at[yi, c, zi, xi])

    pair_copies = [
        pltpu.make_async_remote_copy(
            src_ref=src.at[1 - c], dst_ref=dst, send_sem=sems.at[2 * i], recv_sem=sems.at[2 * i + 1],
            device_id=partner, device_id_type=MESH,
        )
        for i, (src, dst) in enumerate(((p_ref, pair_p), (s_ref, pair_s)))
    ]
    for copy in pair_copies:
        copy.start()
    mine = [pltpu.make_async_copy(src.at[c], dst, sems.at[4 + i])
            for i, (src, dst) in enumerate(((p_ref, own_p), (s_ref, own_s)))]
    for copy in mine:
        copy.start()
    for copy in mine + pair_copies:
        copy.wait()
    own_fresh.wait()
    _wait_bytes(fbuf.at[0, 0, 0, pl.ds(0, r - 1)], fbuf.at[0, 0, 0, pl.ds(0, r - 1)],
                sems.at[32], sems.at[33], along("x", lax.rem(xi + 1, r)))
    fresh_round(1, "z", fbuf.at[yi, c, zi], lambda: fbuf.at[yi, c, zi])

    def merge_pair(k, carry):
        a, b = own_s[k], pair_s[k]
        top = jnp.maximum(a[:, 0:1], b[:, 0:1])
        wa, wb = jnp.exp(a[:, 0:1] - top), jnp.exp(b[:, 0:1] - top)
        pulled = own_p[k] * wa + pair_p[k] * wb
        col = lax.broadcasted_iota(jnp.int32, a.shape, 1)
        stats = jnp.where(col == 0, top, a * wa + b * wb)
        at = {"y": k // (r * r), "z": lax.rem(k // r, r), "x": lax.rem(k, r)}
        for t, (a1, a2, a3) in enumerate(TREES):
            slot = at[a2] * r + at[a3]
            send1[t, at[a1], slot, :, :part] = pulled[:, t * part:(t + 1) * part]
            send1[t, at[a1], slot, :, part:] = stats
        return carry

    lax.fori_loop(0, g, merge_pair, 0)
    _wait_bytes(fbuf.at[0, 0, pl.ds(0, r - 1)], fbuf.at[0, 0, pl.ds(0, r - 1)],
                sems.at[34], sems.at[35], along("z", lax.rem(zi + 1, r)))
    fresh_round(2, "y", fbuf.at[yi, c], lambda: fbuf.at[yi, c])

    def level(lvl, send, recv, blocks):
        sent = []
        for t, axes in enumerate(TREES):
            axis = axes[lvl]
            me_a = mine_at[axis]
            for k in range(1, r):
                dst = lax.rem(me_a + k, r)
                copy = pltpu.make_async_remote_copy(
                    src_ref=send.at[t, pl.ds(dst * blocks, blocks)], dst_ref=recv.at[t, me_a],
                    send_sem=sems.at[6 + 2 * (3 * lvl + t)], recv_sem=sems.at[7 + 2 * (3 * lvl + t)],
                    device_id=along(axis, dst), device_id_type=MESH,
                )
                copy.start()
            recv[t, me_a] = send[t, pl.ds(me_a * blocks, blocks)]
            sent.append(axis)
        for t, axis in enumerate(sent):
            _wait_bytes(recv.at[t, pl.ds(0, r - 1)], recv.at[t, pl.ds(0, r - 1)],
                        sems.at[6 + 2 * (3 * lvl + t)], sems.at[7 + 2 * (3 * lvl + t)],
                        along(axis, lax.rem(mine_at[axis] + 1, r)))

    def run_level1():
        sent_axes = []
        for t, axes in enumerate(TREES):
            axis = axes[0]
            me_a = mine_at[axis]
            for k in range(1, r):
                dst = lax.rem(me_a + k, r)
                pltpu.make_async_remote_copy(
                    src_ref=send1.at[t, dst], dst_ref=recv1.at[t, me_a],
                    send_sem=sems.at[6 + 2 * t], recv_sem=sems.at[7 + 2 * t],
                    device_id=along(axis, dst), device_id_type=MESH,
                ).start()
            recv1[t, me_a] = send1[t, me_a]
            sent_axes.append(axis)
        for t, axis in enumerate(sent_axes):
            _wait_bytes(send1.at[t, pl.ds(0, r - 1)], recv1.at[t, pl.ds(0, r - 1)],
                        sems.at[6 + 2 * t], sems.at[7 + 2 * t],
                        along(axis, lax.rem(mine_at[axis] + 1, r)))

    run_level1()

    def merge1(b, carry):
        for t in range(len(TREES)):
            send2[t, b] = _merge([recv1[t, i, b] for i in range(r)], part)
        return carry

    lax.fori_loop(0, r * r, merge1, 0)
    _wait_bytes(fbuf.at[pl.ds(0, r - 1), 0], fbuf.at[pl.ds(0, r - 1), 0],
                sems.at[36], sems.at[37], along("y", lax.rem(yi + 1, r)))
    for j in range(r):
        pltpu.make_async_remote_copy(
            src_ref=fbuf.at[j, c], dst_ref=fbuf.at[j, c], send_sem=sems.at[38], recv_sem=sems.at[39],
            device_id=partner, device_id_type=MESH,
        ).start()
    level(1, send2, recv2, r)

    for t in range(len(TREES)):
        for a3 in range(r):
            send3[t, a3] = _merge([recv2[t, i, a3] for i in range(r)], part)
    level(2, send3, recv3, 1)

    finals = [_merge([recv3[t, i, 0] for i in range(r)], part) for t in range(len(TREES))]
    stats = finals[0][:, part:]
    for t in range(len(TREES)):
        o_ref[:, t * part:(t + 1) * part] = finals[t][:, :part]
    o_ref[:, d:] = stats
    top = stats[:, 0:1]
    sums = stats[:, 1:2]

    total = jnp.broadcast_to(jnp.sum(top + jnp.log(sums)) - pos_ref[0:1, 0:1], loss_ref.shape)
    for n_axis, axis in enumerate(("x", "z", "y")):
        me_a = mine_at[axis]
        loss_buf[n_axis, me_a] = total
        for k in range(1, r):
            dst = lax.rem(me_a + k, r)
            pltpu.make_async_remote_copy(
                src_ref=loss_buf.at[n_axis, me_a], dst_ref=loss_buf.at[n_axis, me_a],
                send_sem=sems.at[24 + 2 * n_axis], recv_sem=sems.at[25 + 2 * n_axis],
                device_id=along(axis, dst), device_id_type=MESH,
            ).start()
        _wait_bytes(loss_buf.at[n_axis, pl.ds(0, r - 1)], loss_buf.at[n_axis, pl.ds(0, r - 1)],
                    sems.at[24 + 2 * n_axis], sems.at[25 + 2 * n_axis],
                    along(axis, lax.rem(me_a + 1, r)))
        total = loss_buf[n_axis, 0]
        for i in range(1, r):
            total = total + loss_buf[n_axis, i]
    loss_pair[c] = total
    to_pair_loss = pltpu.make_async_remote_copy(
        src_ref=loss_pair.at[c], dst_ref=loss_pair.at[c], send_sem=sems.at[30], recv_sem=sems.at[31],
        device_id=partner, device_id_type=MESH,
    )
    to_pair_loss.start()
    to_pair_loss.wait()
    loss_ref[...] = loss_pair[0] + loss_pair[1]
    _wait_bytes(fbuf.at[:, 0], fbuf.at[:, 0], sems.at[38], sems.at[39], partner)
    fresh_out[...] = fbuf[...]


def combine(pulled, stats, pos, fresh, d, side):
    g, rows = pulled.shape[1:3]
    width = d + stats.shape[3]
    trees = len(TREES)
    block = (rows, d // trees + STAT)
    return pl.pallas_call(
        functools.partial(combine_kernel, d, side),
        out_shape=(
            jax.ShapeDtypeStruct((rows, width), jnp.float32),
            jax.ShapeDtypeStruct((8, 128), jnp.float32),
            jax.ShapeDtypeStruct((side, 2, side, side) + fresh.shape, fresh.dtype),
        ),
        in_specs=[
            pl.BlockSpec(memory_space=pl.ANY),
            pl.BlockSpec(memory_space=pl.ANY),
            pl.BlockSpec(memory_space=pltpu.VMEM),
            pl.BlockSpec(memory_space=pltpu.VMEM),
        ],
        out_specs=(
            pl.BlockSpec(memory_space=pltpu.VMEM),
            pl.BlockSpec(memory_space=pltpu.VMEM),
            pl.BlockSpec(memory_space=pltpu.VMEM),
        ),
        scratch_shapes=[
            pltpu.VMEM((g, rows, d), jnp.float32),
            pltpu.VMEM((g, rows, width - d), jnp.float32),
            pltpu.VMEM((g, rows, d), jnp.float32),
            pltpu.VMEM((g, rows, width - d), jnp.float32),
            pltpu.VMEM((trees, side, side * side) + block, jnp.float32),
            pltpu.VMEM((trees, side, side * side) + block, jnp.float32),
            pltpu.VMEM((trees, side * side) + block, jnp.float32),
            pltpu.VMEM((trees, side, side) + block, jnp.float32),
            pltpu.VMEM((trees, side) + block, jnp.float32),
            pltpu.VMEM((trees, side, 1) + block, jnp.float32),
            pltpu.VMEM((3, side, 8, 128), jnp.float32),
            pltpu.VMEM((2, 8, 128), jnp.float32),
            pltpu.VMEM((side, 2, side, side) + fresh.shape, fresh.dtype),
            pltpu.SemaphoreType.DMA((41,)),
        ],
        compiler_params=pltpu.CompilerParams(collective_id=0, has_side_effects=True),
    )(pulled, stats, pos, fresh)


def shards(queue_keys, fresh_keys, slots, queries, positives):
    dp_size = lax.axis_size("dp")
    queue_size = lax.axis_size("queue")
    n = dp_size * queue_size
    assert fresh_keys.shape[0] == FRESH_HELD
    assert queue_size == (dp_size // 2) ** 2
    d = queries.shape[1]
    pos_code = jnp.zeros((queries.shape[0], STAT), jnp.bfloat16)
    pos_code = pos_code.at[:, 0].set((positives // 32).astype(jnp.bfloat16))
    pos_code = pos_code.at[:, 1].set((positives % 32).astype(jnp.bfloat16))
    gathered = gather_dp(jnp.concatenate([queries, pos_code], axis=1), dp_size // 2)
    total_rows = dp_size * queries.shape[0]
    own_rows = total_rows // n
    gathered = gathered.reshape(total_rows, d + STAT)
    all_queries = gathered[:, :d]
    pos_digits = gathered[:, d:d + 2].astype(jnp.int32)
    all_positives = pos_digits[:, 0] * 32 + pos_digits[:, 1]
    digits = jnp.stack([slots // 16384, (slots // 128) % 128, slots % 128], axis=1)
    code = jnp.zeros((slots.shape[0], STAT), jnp.bfloat16).at[:, :3].set(digits.astype(jnp.bfloat16))
    fresh_block = jnp.concatenate([fresh_keys, code], axis=1)

    device_index = _device_index()
    fresh_padded = jnp.zeros((STAT, d), fresh_keys.dtype).at[:fresh_keys.shape[0]].set(fresh_keys)
    local_pulled, stats = local_partials(gathered, queue_keys, fresh_padded, min(256, total_rows))
    fresh_scores = score_rows(all_queries, fresh_keys)
    fresh_ids = device_index * fresh_keys.shape[0] + jnp.arange(fresh_keys.shape[0], dtype=jnp.int32)
    is_positive = all_positives[:, None] == fresh_ids[None, :]
    positive_total = jnp.sum(jnp.where(is_positive, fresh_scores, 0.0))
    halves = (2, n // 2, own_rows)
    combined, loss_tile, fresh_ext = combine(
        local_pulled.reshape(halves + (d,)),
        stats.reshape(halves + (STAT,)),
        jnp.full((8, 128), positive_total, jnp.float32),
        fresh_block,
        d,
        dp_size // 2,
    )
    fresh_ext = fresh_ext.reshape(n * fresh_keys.shape[0], d + STAT)
    fresh_all = fresh_ext[:, :d]
    got = fresh_ext[:, d:d + 3].astype(jnp.int32)
    slots_all = got[:, 0] * 16384 + got[:, 1] * 128 + got[:, 2]
    sum_rows = combined[:, d + 1]
    pulled = combined[:, :d]
    queue_index = lax.axis_index("queue")
    local_start = queue_index * own_rows
    positive_rows = lax.dynamic_slice_in_dim(positives, local_start, own_rows, 0)
    positive_keys = jnp.take(fresh_all, positive_rows, axis=0).astype(jnp.float32)
    query_grad = pulled / sum_rows[:, None] - positive_keys
    mean_loss = loss_tile[0, 0] / total_rows
    held_rows = queue_keys.shape[0]
    local_slot = slots_all - device_index * held_rows
    picks = jnp.arange(held_rows, dtype=jnp.int32)[:, None] == local_slot[None, :]
    inserted = jnp.dot(picks.astype(jnp.bfloat16), fresh_all, preferred_element_type=jnp.float32)
    replaced = jnp.any(picks, axis=1)
    new_queue = jnp.where(replaced[:, None], inserted.astype(jnp.bfloat16), queue_keys)
    return (query_grad, mean_loss, new_queue)


def solution(mesh):
    placed = (
        P(("dp", "queue"), None),
        P(("dp", "queue"), None),
        P(("dp", "queue")),
        P("dp", None),
        P("dp"),
    )
    return jax.shard_map(
        shards,
        mesh=mesh,
        in_specs=placed,
        out_specs=(P(("dp", "queue"), None), P(), P(("dp", "queue"), None)),
        check_vma=False,
    )
```

```python
import functools

import jax
import jax.numpy as jnp
from jax import lax
from jax.experimental import pallas as pl
from jax.experimental.pallas import tpu as pltpu
from jax.sharding import PartitionSpec as P

MESH = pl.DeviceIdType.MESH
STAT = 128
FRESH_HELD = 8


def score_rows(query_rows, key_rows):
    return lax.dot_general(
        query_rows, key_rows, (((1,), (1,)), ((), ())), preferred_element_type=jnp.float32
    )


def _device_index():
    return lax.axis_index("dp") * lax.axis_size("queue") + lax.axis_index("queue")


def _wait_bytes(src, dst, send_sem, recv_sem, device_id):
    total = pltpu.make_async_remote_copy(
        src_ref=src, dst_ref=dst, send_sem=send_sem, recv_sem=recv_sem,
        device_id=device_id, device_id_type=MESH,
    )
    total.wait_send()
    total.wait_recv()


def partial_kernel(q_ref, k_ref, f_ref, p_ref, s_ref):
    q = q_ref[:, :k_ref.shape[1]]
    dims = (((1,), (1,)), ((), ()))
    scores = lax.dot_general(q, k_ref[...], dims, preferred_element_type=jnp.float32)
    fresh = lax.dot_general(q, f_ref[...], dims, preferred_element_type=jnp.float32)
    held = lax.broadcasted_iota(jnp.int32, fresh.shape, 1) < FRESH_HELD
    fresh = jnp.where(held, fresh, -jnp.inf)
    top = jnp.maximum(jnp.max(scores, axis=1, keepdims=True), jnp.max(fresh, axis=1, keepdims=True))
    weights = jnp.exp(scores - top)
    fresh_weights = jnp.exp(fresh - top)
    total = jnp.sum(weights, axis=1, keepdims=True) + jnp.sum(fresh_weights, axis=1, keepdims=True)
    p_ref[...] = jnp.dot(
        weights.astype(jnp.bfloat16), k_ref[...], preferred_element_type=jnp.float32
    ) + jnp.dot(fresh_weights.astype(jnp.bfloat16), f_ref[...], preferred_element_type=jnp.float32)
    col = lax.broadcasted_iota(jnp.int32, s_ref.shape, 1)
    s_ref[...] = jnp.where(col == 0, top, jnp.where(col == 1, total, 0.0))


def local_partials(queries, keys, fresh_padded, block):
    rows, width = queries.shape
    d = keys.shape[1]
    return pl.pallas_call(
        partial_kernel,
        grid=(rows // block,),
        out_shape=(
            jax.ShapeDtypeStruct((rows, d), jnp.float32),
            jax.ShapeDtypeStruct((rows, STAT), jnp.float32),
        ),
        in_specs=[
            pl.BlockSpec((block, width), lambda i: (i, 0)),
            pl.BlockSpec(keys.shape, lambda i: (0, 0)),
            pl.BlockSpec(fresh_padded.shape, lambda i: (0, 0)),
        ],
        out_specs=(
            pl.BlockSpec((block, d), lambda i: (i, 0)),
            pl.BlockSpec((block, STAT), lambda i: (i, 0)),
        ),
        compiler_params=pltpu.CompilerParams(vmem_limit_bytes=60 * 1024 * 1024),
    )(queries, keys, fresh_padded)


def gather_kernel(x_ref, o_ref, buf, sems):
    dp = lax.axis_index("dp")
    y, c = dp // 2, lax.rem(dp, 2)
    ys = lax.axis_size("dp") // 2
    qi = lax.axis_index("queue")
    partner = (dp + 1 - 2 * c, qi)

    def along(k):
        return (lax.rem(y + k, ys) * 2 + c, qi)

    barrier = pltpu.get_barrier_semaphore()
    pl.semaphore_signal(barrier, inc=1, device_id=partner, device_id_type=MESH)
    for k in range(1, ys):
        pl.semaphore_signal(barrier, inc=1, device_id=along(k), device_id_type=MESH)
    pl.semaphore_wait(barrier, ys)

    mine = pltpu.make_async_copy(x_ref, buf.at[c, y], sems.at[4])
    mine.start()
    first = [
        pltpu.make_async_remote_copy(
            src_ref=x_ref, dst_ref=buf.at[c, y], send_sem=sems.at[0], recv_sem=sems.at[1],
            device_id=dst, device_id_type=MESH,
        )
        for dst in [partner] + [along(k) for k in range(1, ys)]
    ]
    for copy in first:
        copy.start()
    _wait_bytes(buf.at[0], buf.at[0], sems.at[0], sems.at[1], partner)
    mine.wait()
    second = [
        pltpu.make_async_remote_copy(
            src_ref=buf.at[c, lax.rem(y + k, ys)], dst_ref=buf.at[c, lax.rem(y + k, ys)],
            send_sem=sems.at[2], recv_sem=sems.at[3], device_id=partner, device_id_type=MESH,
        )
        for k in range(1, ys)
    ]
    for copy in second:
        copy.start()
    _wait_bytes(buf.at[0, pl.ds(0, ys - 1)], buf.at[0, pl.ds(0, ys - 1)], sems.at[2], sems.at[3], partner)
    o_ref[...] = buf[...]


def gather_dp(x, ys):
    return pl.pallas_call(
        gather_kernel,
        out_shape=jax.ShapeDtypeStruct((2, ys) + x.shape, x.dtype),
        in_specs=[pl.BlockSpec(memory_space=pltpu.VMEM)],
        out_specs=pl.BlockSpec(memory_space=pltpu.VMEM),
        scratch_shapes=[
            pltpu.VMEM((2, ys) + x.shape, x.dtype),
            pltpu.SemaphoreType.DMA((5,)),
        ],
        compiler_params=pltpu.CompilerParams(collective_id=1, has_side_effects=True),
    )(x)


def _merge(blocks, at):
    top = blocks[0][:, at:at + 1]
    for b in blocks[1:]:
        top = jnp.maximum(top, b[:, at:at + 1])
    acc = blocks[0] * jnp.exp(blocks[0][:, at:at + 1] - top)
    for b in blocks[1:]:
        acc = acc + b * jnp.exp(b[:, at:at + 1] - top)
    col = lax.broadcasted_iota(jnp.int32, acc.shape, 1)
    return jnp.where(col == at, top, acc)


TREES = (("x", "z", "y"), ("z", "y", "x"), ("y", "x", "z"))


def combine_kernel(d, side, p_ref, s_ref, pos_ref, f_ref, o_ref, loss_ref, fresh_out, own_p, own_s,
                   pair_p, pair_s, send1, recv1, send2, recv2, send3, recv3, loss_buf, loss_pair,
                   fbuf, sems):
    r = side
    part = d // len(TREES)
    g = p_ref.shape[1]
    dp = lax.axis_index("dp")
    y, c = dp // 2, lax.rem(dp, 2)
    qi = lax.axis_index("queue")
    mine_at = {"y": y, "z": qi // r, "x": lax.rem(qi, r)}
    partner = (dp + 1 - 2 * c, qi)

    def device(at):
        return (at["y"] * 2 + c, at["z"] * r + at["x"])

    def along(axis, j):
        at = dict(mine_at)
        at[axis] = j
        return device(at)

    barrier = pltpu.get_barrier_semaphore()
    pl.semaphore_signal(barrier, inc=1, device_id=partner, device_id_type=MESH)
    for axis in ("x", "z", "y"):
        for k in range(1, r):
            pl.semaphore_signal(barrier, inc=1, device_id=along(axis, lax.rem(mine_at[axis] + k, r)),
                                device_id_type=MESH)
    pl.semaphore_wait(barrier, 1 + 3 * (r - 1))

    yi, zi, xi = mine_at["y"], mine_at["z"], mine_at["x"]
    own_fresh = pltpu.make_async_copy(f_ref, fbuf.at[yi, c, zi, xi], sems.at[40])
    own_fresh.start()

    def fresh_round(i, axis, src, dst_of):
        for k in range(1, r):
            dst = lax.rem(mine_at[axis] + k, r)
            pltpu.make_async_remote_copy(
                src_ref=src, dst_ref=dst_of(), send_sem=sems.at[32 + 2 * i], recv_sem=sems.at[33 + 2 * i],
                device_id=along(axis, dst), device_id_type=MESH,
            ).start()

    fresh_round(0, "x", f_ref, lambda: fbuf.at[yi, c, zi, xi])

    pair_copies = [
        pltpu.make_async_remote_copy(
            src_ref=src.at[1 - c], dst_ref=dst, send_sem=sems.at[2 * i], recv_sem=sems.at[2 * i + 1],
            device_id=partner, device_id_type=MESH,
        )
        for i, (src, dst) in enumerate(((p_ref, pair_p), (s_ref, pair_s)))
    ]
    for copy in pair_copies:
        copy.start()
    mine = [pltpu.make_async_copy(src.at[c], dst, sems.at[4 + i])
            for i, (src, dst) in enumerate(((p_ref, own_p), (s_ref, own_s)))]
    for copy in mine:
        copy.start()
    for copy in mine + pair_copies:
        copy.wait()
    own_fresh.wait()
    _wait_bytes(fbuf.at[0, 0, 0, pl.ds(0, r - 1)], fbuf.at[0, 0, 0, pl.ds(0, r - 1)],
                sems.at[32], sems.at[33], along("x", lax.rem(xi + 1, r)))
    fresh_round(1, "z", fbuf.at[yi, c, zi], lambda: fbuf.at[yi, c, zi])

    def merge_pair(k, carry):
        a, b = own_s[k], pair_s[k]
        top = jnp.maximum(a[:, 0:1], b[:, 0:1])
        wa, wb = jnp.exp(a[:, 0:1] - top), jnp.exp(b[:, 0:1] - top)
        pulled = own_p[k] * wa + pair_p[k] * wb
        col = lax.broadcasted_iota(jnp.int32, a.shape, 1)
        stats = jnp.where(col == 0, top, a * wa + b * wb)
        at = {"y": k // (r * r), "z": lax.rem(k // r, r), "x": lax.rem(k, r)}
        for t, (a1, a2, a3) in enumerate(TREES):
            slot = at[a2] * r + at[a3]
            send1[t, at[a1], slot, :, :part] = pulled[:, t * part:(t + 1) * part]
            send1[t, at[a1], slot, :, part:] = stats
        return carry

    lax.fori_loop(0, g, merge_pair, 0)

    def level(lvl, send, recv, blocks):
        sent = []
        for t, axes in enumerate(TREES):
            axis = axes[lvl]
            me_a = mine_at[axis]
            for k in range(1, r):
                dst = lax.rem(me_a + k, r)
                copy = pltpu.make_async_remote_copy(
                    src_ref=send.at[t, pl.ds(dst * blocks, blocks)], dst_ref=recv.at[t, me_a],
                    send_sem=sems.at[6 + 2 * (3 * lvl + t)], recv_sem=sems.at[7 + 2 * (3 * lvl + t)],
                    device_id=along(axis, dst), device_id_type=MESH,
                )
                copy.start()
            recv[t, me_a] = send[t, pl.ds(me_a * blocks, blocks)]
            sent.append(axis)
        for t, axis in enumerate(sent):
            _wait_bytes(recv.at[t, pl.ds(0, r - 1)], recv.at[t, pl.ds(0, r - 1)],
                        sems.at[6 + 2 * (3 * lvl + t)], sems.at[7 + 2 * (3 * lvl + t)],
                        along(axis, lax.rem(mine_at[axis] + 1, r)))

    def run_level1():
        sent_axes = []
        for t, axes in enumerate(TREES):
            axis = axes[0]
            me_a = mine_at[axis]
            for k in range(1, r):
                dst = lax.rem(me_a + k, r)
                pltpu.make_async_remote_copy(
                    src_ref=send1.at[t, dst], dst_ref=recv1.at[t, me_a],
                    send_sem=sems.at[6 + 2 * t], recv_sem=sems.at[7 + 2 * t],
                    device_id=along(axis, dst), device_id_type=MESH,
                ).start()
            recv1[t, me_a] = send1[t, me_a]
            sent_axes.append(axis)
        for t, axis in enumerate(sent_axes):
            _wait_bytes(send1.at[t, pl.ds(0, r - 1)], recv1.at[t, pl.ds(0, r - 1)],
                        sems.at[6 + 2 * t], sems.at[7 + 2 * t],
                        along(axis, lax.rem(mine_at[axis] + 1, r)))

    run_level1()

    def merge1(b, carry):
        for t in range(len(TREES)):
            send2[t, b] = _merge([recv1[t, i, b] for i in range(r)], part)
        return carry

    lax.fori_loop(0, r * r, merge1, 0)
    _wait_bytes(fbuf.at[0, 0, pl.ds(0, r - 1)], fbuf.at[0, 0, pl.ds(0, r - 1)],
                sems.at[34], sems.at[35], along("z", lax.rem(zi + 1, r)))
    level(1, send2, recv2, r)

    for t in range(len(TREES)):
        for a3 in range(r):
            send3[t, a3] = _merge([recv2[t, i, a3] for i in range(r)], part)
    fresh_round(2, "y", fbuf.at[yi, c], lambda: fbuf.at[yi, c])
    level(2, send3, recv3, 1)

    finals = [_merge([recv3[t, i, 0] for i in range(r)], part) for t in range(len(TREES))]
    stats = finals[0][:, part:]
    for t in range(len(TREES)):
        o_ref[:, t * part:(t + 1) * part] = finals[t][:, :part]
    o_ref[:, d:] = stats
    top = stats[:, 0:1]
    sums = stats[:, 1:2]

    total = jnp.broadcast_to(jnp.sum(top + jnp.log(sums)) - pos_ref[0:1, 0:1], loss_ref.shape)
    for n_axis, axis in enumerate(("x", "z", "y")):
        me_a = mine_at[axis]
        loss_buf[n_axis, me_a] = total
        for k in range(1, r):
            dst = lax.rem(me_a + k, r)
            pltpu.make_async_remote_copy(
                src_ref=loss_buf.at[n_axis, me_a], dst_ref=loss_buf.at[n_axis, me_a],
                send_sem=sems.at[24 + 2 * n_axis], recv_sem=sems.at[25 + 2 * n_axis],
                device_id=along(axis, dst), device_id_type=MESH,
            ).start()
        _wait_bytes(loss_buf.at[n_axis, pl.ds(0, r - 1)], loss_buf.at[n_axis, pl.ds(0, r - 1)],
                    sems.at[24 + 2 * n_axis], sems.at[25 + 2 * n_axis],
                    along(axis, lax.rem(me_a + 1, r)))
        total = loss_buf[n_axis, 0]
        for i in range(1, r):
            total = total + loss_buf[n_axis, i]
    _wait_bytes(fbuf.at[pl.ds(0, r - 1), 0], fbuf.at[pl.ds(0, r - 1), 0],
                sems.at[36], sems.at[37], along("y", lax.rem(yi + 1, r)))
    for j in range(r):
        pltpu.make_async_remote_copy(
            src_ref=fbuf.at[j, c], dst_ref=fbuf.at[j, c], send_sem=sems.at[38], recv_sem=sems.at[39],
            device_id=partner, device_id_type=MESH,
        ).start()
    loss_pair[c] = total
    to_pair_loss = pltpu.make_async_remote_copy(
        src_ref=loss_pair.at[c], dst_ref=loss_pair.at[c], send_sem=sems.at[30], recv_sem=sems.at[31],
        device_id=partner, device_id_type=MESH,
    )
    to_pair_loss.start()
    to_pair_loss.wait()
    loss_ref[...] = loss_pair[0] + loss_pair[1]
    _wait_bytes(fbuf.at[:, 0], fbuf.at[:, 0], sems.at[38], sems.at[39], partner)
    fresh_out[...] = fbuf[...]


def combine(pulled, stats, pos, fresh, d, side):
    g, rows = pulled.shape[1:3]
    width = d + stats.shape[3]
    trees = len(TREES)
    block = (rows, d // trees + STAT)
    return pl.pallas_call(
        functools.partial(combine_kernel, d, side),
        out_shape=(
            jax.ShapeDtypeStruct((rows, width), jnp.float32),
            jax.ShapeDtypeStruct((8, 128), jnp.float32),
            jax.ShapeDtypeStruct((side, 2, side, side) + fresh.shape, fresh.dtype),
        ),
        in_specs=[
            pl.BlockSpec(memory_space=pl.ANY),
            pl.BlockSpec(memory_space=pl.ANY),
            pl.BlockSpec(memory_space=pltpu.VMEM),
            pl.BlockSpec(memory_space=pltpu.VMEM),
        ],
        out_specs=(
            pl.BlockSpec(memory_space=pltpu.VMEM),
            pl.BlockSpec(memory_space=pltpu.VMEM),
            pl.BlockSpec(memory_space=pltpu.VMEM),
        ),
        scratch_shapes=[
            pltpu.VMEM((g, rows, d), jnp.float32),
            pltpu.VMEM((g, rows, width - d), jnp.float32),
            pltpu.VMEM((g, rows, d), jnp.float32),
            pltpu.VMEM((g, rows, width - d), jnp.float32),
            pltpu.VMEM((trees, side, side * side) + block, jnp.float32),
            pltpu.VMEM((trees, side, side * side) + block, jnp.float32),
            pltpu.VMEM((trees, side * side) + block, jnp.float32),
            pltpu.VMEM((trees, side, side) + block, jnp.float32),
            pltpu.VMEM((trees, side) + block, jnp.float32),
            pltpu.VMEM((trees, side, 1) + block, jnp.float32),
            pltpu.VMEM((3, side, 8, 128), jnp.float32),
            pltpu.VMEM((2, 8, 128), jnp.float32),
            pltpu.VMEM((side, 2, side, side) + fresh.shape, fresh.dtype),
            pltpu.SemaphoreType.DMA((41,)),
        ],
        compiler_params=pltpu.CompilerParams(collective_id=0, has_side_effects=True),
    )(pulled, stats, pos, fresh)


def shards(queue_keys, fresh_keys, slots, queries, positives):
    dp_size = lax.axis_size("dp")
    queue_size = lax.axis_size("queue")
    n = dp_size * queue_size
    assert fresh_keys.shape[0] == FRESH_HELD
    assert queue_size == (dp_size // 2) ** 2
    d = queries.shape[1]
    pos_code = jnp.zeros((queries.shape[0], STAT), jnp.bfloat16)
    pos_code = pos_code.at[:, 0].set((positives // 32).astype(jnp.bfloat16))
    pos_code = pos_code.at[:, 1].set((positives % 32).astype(jnp.bfloat16))
    gathered = gather_dp(jnp.concatenate([queries, pos_code], axis=1), dp_size // 2)
    total_rows = dp_size * queries.shape[0]
    own_rows = total_rows // n
    gathered = gathered.reshape(total_rows, d + STAT)
    all_queries = gathered[:, :d]
    pos_digits = gathered[:, d:d + 2].astype(jnp.int32)
    all_positives = pos_digits[:, 0] * 32 + pos_digits[:, 1]
    digits = jnp.stack([slots // 16384, (slots // 128) % 128, slots % 128], axis=1)
    code = jnp.zeros((slots.shape[0], STAT), jnp.bfloat16).at[:, :3].set(digits.astype(jnp.bfloat16))
    fresh_block = jnp.concatenate([fresh_keys, code], axis=1)

    device_index = _device_index()
    fresh_padded = jnp.zeros((STAT, d), fresh_keys.dtype).at[:fresh_keys.shape[0]].set(fresh_keys)
    local_pulled, stats = local_partials(gathered, queue_keys, fresh_padded, min(256, total_rows))
    fresh_scores = score_rows(all_queries, fresh_keys)
    fresh_ids = device_index * fresh_keys.shape[0] + jnp.arange(fresh_keys.shape[0], dtype=jnp.int32)
    is_positive = all_positives[:, None] == fresh_ids[None, :]
    positive_total = jnp.sum(jnp.where(is_positive, fresh_scores, 0.0))
    halves = (2, n // 2, own_rows)
    combined, loss_tile, fresh_ext = combine(
        local_pulled.reshape(halves + (d,)),
        stats.reshape(halves + (STAT,)),
        jnp.full((8, 128), positive_total, jnp.float32),
        fresh_block,
        d,
        dp_size // 2,
    )
    fresh_ext = fresh_ext.reshape(n * fresh_keys.shape[0], d + STAT)
    fresh_all = fresh_ext[:, :d]
    got = fresh_ext[:, d:d + 3].astype(jnp.int32)
    slots_all = got[:, 0] * 16384 + got[:, 1] * 128 + got[:, 2]
    sum_rows = combined[:, d + 1]
    pulled = combined[:, :d]
    queue_index = lax.axis_index("queue")
    local_start = queue_index * own_rows
    positive_rows = lax.dynamic_slice_in_dim(positives, local_start, own_rows, 0)
    positive_keys = jnp.take(fresh_all, positive_rows, axis=0).astype(jnp.float32)
    query_grad = pulled / sum_rows[:, None] - positive_keys
    mean_loss = loss_tile[0, 0] / total_rows
    held_rows = queue_keys.shape[0]
    local_slot = slots_all - device_index * held_rows
    picks = jnp.arange(held_rows, dtype=jnp.int32)[:, None] == local_slot[None, :]
    inserted = jnp.dot(picks.astype(jnp.bfloat16), fresh_all, preferred_element_type=jnp.float32)
    replaced = jnp.any(picks, axis=1)
    new_queue = jnp.where(replaced[:, None], inserted.astype(jnp.bfloat16), queue_keys)
    return (query_grad, mean_loss, new_queue)


def solution(mesh):
    placed = (
        P(("dp", "queue"), None),
        P(("dp", "queue"), None),
        P(("dp", "queue")),
        P("dp", None),
        P("dp"),
    )
    return jax.shard_map(
        shards,
        mesh=mesh,
        in_specs=placed,
        out_specs=(P(("dp", "queue"), None), P(), P(("dp", "queue"), None)),
        check_vma=False,
    )
```

```python
import functools

import jax
import jax.numpy as jnp
from jax import lax
from jax.experimental import pallas as pl
from jax.experimental.pallas import tpu as pltpu
from jax.sharding import PartitionSpec as P

MESH = pl.DeviceIdType.MESH
STAT = 128
FRESH_HELD = 8
KEY_CHUNK = 512


def score_rows(query_rows, key_rows):
    return lax.dot_general(
        query_rows, key_rows, (((1,), (1,)), ((), ())), preferred_element_type=jnp.float32
    )


def _device_index():
    return lax.axis_index("dp") * lax.axis_size("queue") + lax.axis_index("queue")


def _wait_bytes(src, dst, send_sem, recv_sem, device_id):
    total = pltpu.make_async_remote_copy(
        src_ref=src, dst_ref=dst, send_sem=send_sem, recv_sem=recv_sem,
        device_id=device_id, device_id_type=MESH,
    )
    total.wait_send()
    total.wait_recv()


def partial_kernel(q_ref, k_ref, f_ref, p_ref, s_ref):
    q = q_ref[:, :k_ref.shape[1]]
    dims = (((1,), (1,)), ((), ()))
    scores = lax.dot_general(q, k_ref[...], dims, preferred_element_type=jnp.float32)
    fresh = lax.dot_general(q, f_ref[...], dims, preferred_element_type=jnp.float32)
    held = lax.broadcasted_iota(jnp.int32, fresh.shape, 1) < FRESH_HELD
    fresh = jnp.where(held, fresh, -jnp.inf)
    top = jnp.maximum(jnp.max(scores, axis=1, keepdims=True), jnp.max(fresh, axis=1, keepdims=True))
    fresh_weights = jnp.exp(fresh - top)
    total = jnp.sum(fresh_weights, axis=1, keepdims=True)
    acc = jnp.dot(fresh_weights.astype(jnp.bfloat16), f_ref[...], preferred_element_type=jnp.float32)
    chunk = min(KEY_CHUNK, k_ref.shape[0])
    for j in range(k_ref.shape[0] // chunk):
        weights = jnp.exp(scores[:, j * chunk:(j + 1) * chunk] - top)
        total = total + jnp.sum(weights, axis=1, keepdims=True)
        acc = acc + jnp.dot(
            weights.astype(jnp.bfloat16), k_ref[j * chunk:(j + 1) * chunk, :],
            preferred_element_type=jnp.float32,
        )
    p_ref[...] = acc
    col = lax.broadcasted_iota(jnp.int32, s_ref.shape, 1)
    s_ref[...] = jnp.where(col == 0, top, jnp.where(col == 1, total, 0.0))


def local_partials(queries, keys, fresh_padded, block):
    rows, width = queries.shape
    d = keys.shape[1]
    return pl.pallas_call(
        partial_kernel,
        grid=(rows // block,),
        out_shape=(
            jax.ShapeDtypeStruct((rows, d), jnp.float32),
            jax.ShapeDtypeStruct((rows, STAT), jnp.float32),
        ),
        in_specs=[
            pl.BlockSpec((block, width), lambda i: (i, 0)),
            pl.BlockSpec(keys.shape, lambda i: (0, 0)),
            pl.BlockSpec(fresh_padded.shape, lambda i: (0, 0)),
        ],
        out_specs=(
            pl.BlockSpec((block, d), lambda i: (i, 0)),
            pl.BlockSpec((block, STAT), lambda i: (i, 0)),
        ),
        compiler_params=pltpu.CompilerParams(vmem_limit_bytes=60 * 1024 * 1024),
    )(queries, keys, fresh_padded)


def gather_kernel(x_ref, o_ref, buf, sems):
    dp = lax.axis_index("dp")
    y, c = dp // 2, lax.rem(dp, 2)
    ys = lax.axis_size("dp") // 2
    qi = lax.axis_index("queue")
    partner = (dp + 1 - 2 * c, qi)

    def along(k):
        return (lax.rem(y + k, ys) * 2 + c, qi)

    barrier = pltpu.get_barrier_semaphore()
    pl.semaphore_signal(barrier, inc=1, device_id=partner, device_id_type=MESH)
    for k in range(1, ys):
        pl.semaphore_signal(barrier, inc=1, device_id=along(k), device_id_type=MESH)
    pl.semaphore_wait(barrier, ys)

    mine = pltpu.make_async_copy(x_ref, buf.at[c, y], sems.at[4])
    mine.start()
    first = [
        pltpu.make_async_remote_copy(
            src_ref=x_ref, dst_ref=buf.at[c, y], send_sem=sems.at[0], recv_sem=sems.at[1],
            device_id=dst, device_id_type=MESH,
        )
        for dst in [partner] + [along(k) for k in range(1, ys)]
    ]
    for copy in first:
        copy.start()
    _wait_bytes(buf.at[0], buf.at[0], sems.at[0], sems.at[1], partner)
    mine.wait()
    second = [
        pltpu.make_async_remote_copy(
            src_ref=buf.at[c, lax.rem(y + k, ys)], dst_ref=buf.at[c, lax.rem(y + k, ys)],
            send_sem=sems.at[2], recv_sem=sems.at[3], device_id=partner, device_id_type=MESH,
        )
        for k in range(1, ys)
    ]
    for copy in second:
        copy.start()
    _wait_bytes(buf.at[0, pl.ds(0, ys - 1)], buf.at[0, pl.ds(0, ys - 1)], sems.at[2], sems.at[3], partner)
    o_ref[...] = buf[...]


def gather_dp(x, ys):
    return pl.pallas_call(
        gather_kernel,
        out_shape=jax.ShapeDtypeStruct((2, ys) + x.shape, x.dtype),
        in_specs=[pl.BlockSpec(memory_space=pltpu.VMEM)],
        out_specs=pl.BlockSpec(memory_space=pltpu.VMEM),
        scratch_shapes=[
            pltpu.VMEM((2, ys) + x.shape, x.dtype),
            pltpu.SemaphoreType.DMA((5,)),
        ],
        compiler_params=pltpu.CompilerParams(collective_id=1, has_side_effects=True),
    )(x)


def _merge(blocks, at):
    top = blocks[0][:, at:at + 1]
    for b in blocks[1:]:
        top = jnp.maximum(top, b[:, at:at + 1])
    acc = blocks[0] * jnp.exp(blocks[0][:, at:at + 1] - top)
    for b in blocks[1:]:
        acc = acc + b * jnp.exp(b[:, at:at + 1] - top)
    col = lax.broadcasted_iota(jnp.int32, acc.shape, 1)
    return jnp.where(col == at, top, acc)


TREES = (("x", "z", "y"), ("z", "y", "x"), ("y", "x", "z"))


def combine_kernel(d, side, p_ref, s_ref, pos_ref, o_ref, loss_ref, own_p, own_s, pair_p, pair_s,
                   send1, recv1, send2, recv2, send3, recv3, loss_buf, loss_pair, sems):
    r = side
    part = d // len(TREES)
    g = p_ref.shape[1]
    dp = lax.axis_index("dp")
    y, c = dp // 2, lax.rem(dp, 2)
    qi = lax.axis_index("queue")
    mine_at = {"y": y, "z": qi // r, "x": lax.rem(qi, r)}
    partner = (dp + 1 - 2 * c, qi)

    def device(at):
        return (at["y"] * 2 + c, at["z"] * r + at["x"])

    def along(axis, j):
        at = dict(mine_at)
        at[axis] = j
        return device(at)

    barrier = pltpu.get_barrier_semaphore()
    pl.semaphore_signal(barrier, inc=1, device_id=partner, device_id_type=MESH)
    for axis in ("x", "z", "y"):
        for k in range(1, r):
            pl.semaphore_signal(barrier, inc=1, device_id=along(axis, lax.rem(mine_at[axis] + k, r)),
                                device_id_type=MESH)
    pl.semaphore_wait(barrier, 1 + 3 * (r - 1))

    pair_copies = [
        pltpu.make_async_remote_copy(
            src_ref=src.at[1 - c], dst_ref=dst, send_sem=sems.at[2 * i], recv_sem=sems.at[2 * i + 1],
            device_id=partner, device_id_type=MESH,
        )
        for i, (src, dst) in enumerate(((p_ref, pair_p), (s_ref, pair_s)))
    ]
    for copy in pair_copies:
        copy.start()
    mine = [pltpu.make_async_copy(src.at[c], dst, sems.at[4 + i])
            for i, (src, dst) in enumerate(((p_ref, own_p), (s_ref, own_s)))]
    for copy in mine:
        copy.start()
    for copy in mine + pair_copies:
        copy.wait()

    def merge_pair(k, carry):
        a, b = own_s[k], pair_s[k]
        top = jnp.maximum(a[:, 0:1], b[:, 0:1])
        wa, wb = jnp.exp(a[:, 0:1] - top), jnp.exp(b[:, 0:1] - top)
        pulled = own_p[k] * wa + pair_p[k] * wb
        col = lax.broadcasted_iota(jnp.int32, a.shape, 1)
        stats = jnp.where(col == 0, top, a * wa + b * wb)
        at = {"y": k // (r * r), "z": lax.rem(k // r, r), "x": lax.rem(k, r)}
        for t, (a1, a2, a3) in enumerate(TREES):
            slot = at[a2] * r + at[a3]
            send1[t, at[a1], slot, :, :part] = pulled[:, t * part:(t + 1) * part]
            send1[t, at[a1], slot, :, part:] = stats
        return carry

    lax.fori_loop(0, g, merge_pair, 0)

    def level(lvl, send, recv, blocks):
        sent = []
        for t, axes in enumerate(TREES):
            axis = axes[lvl]
            me_a = mine_at[axis]
            for k in range(1, r):
                dst = lax.rem(me_a + k, r)
                copy = pltpu.make_async_remote_copy(
                    src_ref=send.at[t, pl.ds(dst * blocks, blocks)], dst_ref=recv.at[t, me_a],
                    send_sem=sems.at[6 + 2 * (3 * lvl + t)], recv_sem=sems.at[7 + 2 * (3 * lvl + t)],
                    device_id=along(axis, dst), device_id_type=MESH,
                )
                copy.start()
            recv[t, me_a] = send[t, pl.ds(me_a * blocks, blocks)]
            sent.append(axis)
        for t, axis in enumerate(sent):
            _wait_bytes(recv.at[t, pl.ds(0, r - 1)], recv.at[t, pl.ds(0, r - 1)],
                        sems.at[6 + 2 * (3 * lvl + t)], sems.at[7 + 2 * (3 * lvl + t)],
                        along(axis, lax.rem(mine_at[axis] + 1, r)))

    def run_level1():
        sent_axes = []
        for t, axes in enumerate(TREES):
            axis = axes[0]
            me_a = mine_at[axis]
            for k in range(1, r):
                dst = lax.rem(me_a + k, r)
                pltpu.make_async_remote_copy(
                    src_ref=send1.at[t, dst], dst_ref=recv1.at[t, me_a],
                    send_sem=sems.at[6 + 2 * t], recv_sem=sems.at[7 + 2 * t],
                    device_id=along(axis, dst), device_id_type=MESH,
                ).start()
            recv1[t, me_a] = send1[t, me_a]
            sent_axes.append(axis)
        for t, axis in enumerate(sent_axes):
            _wait_bytes(send1.at[t, pl.ds(0, r - 1)], recv1.at[t, pl.ds(0, r - 1)],
                        sems.at[6 + 2 * t], sems.at[7 + 2 * t],
                        along(axis, lax.rem(mine_at[axis] + 1, r)))

    run_level1()

    def merge1(b, carry):
        for t in range(len(TREES)):
            send2[t, b] = _merge([recv1[t, i, b] for i in range(r)], part)
        return carry

    lax.fori_loop(0, r * r, merge1, 0)
    level(1, send2, recv2, r)

    for t in range(len(TREES)):
        for a3 in range(r):
            send3[t, a3] = _merge([recv2[t, i, a3] for i in range(r)], part)
    level(2, send3, recv3, 1)

    finals = [_merge([recv3[t, i, 0] for i in range(r)], part) for t in range(len(TREES))]
    stats = finals[0][:, part:]
    for t in range(len(TREES)):
        o_ref[:, t * part:(t + 1) * part] = finals[t][:, :part]
    o_ref[:, d:] = stats
    top = stats[:, 0:1]
    sums = stats[:, 1:2]

    total = jnp.broadcast_to(jnp.sum(top + jnp.log(sums)) - pos_ref[0:1, 0:1], loss_ref.shape)
    for n_axis, axis in enumerate(("x", "z", "y")):
        me_a = mine_at[axis]
        loss_buf[n_axis, me_a] = total
        for k in range(1, r):
            dst = lax.rem(me_a + k, r)
            pltpu.make_async_remote_copy(
                src_ref=loss_buf.at[n_axis, me_a], dst_ref=loss_buf.at[n_axis, me_a],
                send_sem=sems.at[24 + 2 * n_axis], recv_sem=sems.at[25 + 2 * n_axis],
                device_id=along(axis, dst), device_id_type=MESH,
            ).start()
        _wait_bytes(loss_buf.at[n_axis, pl.ds(0, r - 1)], loss_buf.at[n_axis, pl.ds(0, r - 1)],
                    sems.at[24 + 2 * n_axis], sems.at[25 + 2 * n_axis],
                    along(axis, lax.rem(me_a + 1, r)))
        total = loss_buf[n_axis, 0]
        for i in range(1, r):
            total = total + loss_buf[n_axis, i]
    loss_pair[c] = total
    to_pair_loss = pltpu.make_async_remote_copy(
        src_ref=loss_pair.at[c], dst_ref=loss_pair.at[c], send_sem=sems.at[30], recv_sem=sems.at[31],
        device_id=partner, device_id_type=MESH,
    )
    to_pair_loss.start()
    to_pair_loss.wait()
    loss_ref[...] = loss_pair[0] + loss_pair[1]


def combine(pulled, stats, pos, d, side):
    g, rows = pulled.shape[1:3]
    width = d + stats.shape[3]
    trees = len(TREES)
    block = (rows, d // trees + STAT)
    return pl.pallas_call(
        functools.partial(combine_kernel, d, side),
        out_shape=(
            jax.ShapeDtypeStruct((rows, width), jnp.float32),
            jax.ShapeDtypeStruct((8, 128), jnp.float32),
        ),
        in_specs=[
            pl.BlockSpec(memory_space=pl.ANY),
            pl.BlockSpec(memory_space=pl.ANY),
            pl.BlockSpec(memory_space=pltpu.VMEM),
        ],
        out_specs=(
            pl.BlockSpec(memory_space=pltpu.VMEM),
            pl.BlockSpec(memory_space=pltpu.VMEM),
        ),
        scratch_shapes=[
            pltpu.VMEM((g, rows, d), jnp.float32),
            pltpu.VMEM((g, rows, width - d), jnp.float32),
            pltpu.VMEM((g, rows, d), jnp.float32),
            pltpu.VMEM((g, rows, width - d), jnp.float32),
            pltpu.VMEM((trees, side, side * side) + block, jnp.float32),
            pltpu.VMEM((trees, side, side * side) + block, jnp.float32),
            pltpu.VMEM((trees, side * side) + block, jnp.float32),
            pltpu.VMEM((trees, side, side) + block, jnp.float32),
            pltpu.VMEM((trees, side) + block, jnp.float32),
            pltpu.VMEM((trees, side, 1) + block, jnp.float32),
            pltpu.VMEM((3, side, 8, 128), jnp.float32),
            pltpu.VMEM((2, 8, 128), jnp.float32),
            pltpu.SemaphoreType.DMA((32,)),
        ],
        compiler_params=pltpu.CompilerParams(collective_id=0, has_side_effects=True),
    )(pulled, stats, pos)


def shards(queue_keys, fresh_keys, slots, queries, positives):
    dp_size = lax.axis_size("dp")
    queue_size = lax.axis_size("queue")
    n = dp_size * queue_size
    assert fresh_keys.shape[0] == FRESH_HELD
    assert queue_size == (dp_size // 2) ** 2
    d = queries.shape[1]
    pos_code = jnp.zeros((queries.shape[0], STAT), jnp.bfloat16)
    pos_code = pos_code.at[:, 0].set((positives // 32).astype(jnp.bfloat16))
    pos_code = pos_code.at[:, 1].set((positives % 32).astype(jnp.bfloat16))
    gathered = gather_dp(jnp.concatenate([queries, pos_code], axis=1), dp_size // 2)
    total_rows = dp_size * queries.shape[0]
    own_rows = total_rows // n
    gathered = gathered.reshape(total_rows, d + STAT)
    all_queries = gathered[:, :d]
    pos_digits = gathered[:, d:d + 2].astype(jnp.int32)
    all_positives = pos_digits[:, 0] * 32 + pos_digits[:, 1]
    digits = jnp.stack([slots // 16384, (slots // 128) % 128, slots % 128], axis=1)
    code = jnp.zeros((slots.shape[0], STAT), jnp.bfloat16).at[:, :3].set(digits.astype(jnp.bfloat16))
    fresh_ext = lax.all_gather(
        jnp.concatenate([fresh_keys, code], axis=1), ("dp", "queue"), axis=0, tiled=True
    )
    fresh_all = fresh_ext[:, :d]
    got = fresh_ext[:, d:d + 3].astype(jnp.int32)
    slots_all = got[:, 0] * 16384 + got[:, 1] * 128 + got[:, 2]

    device_index = _device_index()
    fresh_padded = jnp.zeros((STAT, d), fresh_keys.dtype).at[:fresh_keys.shape[0]].set(fresh_keys)
    local_pulled, stats = local_partials(gathered, queue_keys, fresh_padded, min(256, total_rows))
    fresh_scores = score_rows(all_queries, fresh_keys)
    fresh_ids = device_index * fresh_keys.shape[0] + jnp.arange(fresh_keys.shape[0], dtype=jnp.int32)
    is_positive = all_positives[:, None] == fresh_ids[None, :]
    positive_total = jnp.sum(jnp.where(is_positive, fresh_scores, 0.0))
    halves = (2, n // 2, own_rows)
    combined, loss_tile = combine(
        local_pulled.reshape(halves + (d,)),
        stats.reshape(halves + (STAT,)),
        jnp.full((8, 128), positive_total, jnp.float32),
        d,
        dp_size // 2,
    )
    sum_rows = combined[:, d + 1]
    pulled = combined[:, :d]
    queue_index = lax.axis_index("queue")
    local_start = queue_index * own_rows
    positive_rows = lax.dynamic_slice_in_dim(positives, local_start, own_rows, 0)
    positive_keys = jnp.take(fresh_all, positive_rows, axis=0).astype(jnp.float32)
    query_grad = pulled / sum_rows[:, None] - positive_keys
    mean_loss = loss_tile[0, 0] / total_rows
    held_rows = queue_keys.shape[0]
    local_slot = slots_all - device_index * held_rows
    picks = jnp.arange(held_rows, dtype=jnp.int32)[:, None] == local_slot[None, :]
    inserted = jnp.dot(picks.astype(jnp.bfloat16), fresh_all, preferred_element_type=jnp.float32)
    replaced = jnp.any(picks, axis=1)
    new_queue = jnp.where(replaced[:, None], inserted.astype(jnp.bfloat16), queue_keys)
    return (query_grad, mean_loss, new_queue)


def solution(mesh):
    placed = (
        P(("dp", "queue"), None),
        P(("dp", "queue"), None),
        P(("dp", "queue")),
        P("dp", None),
        P("dp"),
    )
    return jax.shard_map(
        shards,
        mesh=mesh,
        in_specs=placed,
        out_specs=(P(("dp", "queue"), None), P(), P(("dp", "queue"), None)),
        check_vma=False,
    )
```

```python
import functools

import jax
import jax.numpy as jnp
from jax import lax
from jax.experimental import pallas as pl
from jax.experimental.pallas import tpu as pltpu
from jax.sharding import PartitionSpec as P

MESH = pl.DeviceIdType.MESH
STAT = 128
FRESH_HELD = 8
KEY_CHUNK = 512


def score_rows(query_rows, key_rows):
    return lax.dot_general(
        query_rows, key_rows, (((1,), (1,)), ((), ())), preferred_element_type=jnp.float32
    )


def _device_index():
    return lax.axis_index("dp") * lax.axis_size("queue") + lax.axis_index("queue")


def _wait_bytes(src, dst, send_sem, recv_sem, device_id):
    total = pltpu.make_async_remote_copy(
        src_ref=src, dst_ref=dst, send_sem=send_sem, recv_sem=recv_sem,
        device_id=device_id, device_id_type=MESH,
    )
    total.wait_send()
    total.wait_recv()


def partial_kernel(q_ref, k_ref, f_ref, p_ref, s_ref):
    q = q_ref[:, :k_ref.shape[1]]
    dims = (((1,), (1,)), ((), ()))
    scores = lax.dot_general(q, k_ref[...], dims, preferred_element_type=jnp.float32)
    fresh = lax.dot_general(q, f_ref[...], dims, preferred_element_type=jnp.float32)
    held = lax.broadcasted_iota(jnp.int32, fresh.shape, 1) < FRESH_HELD
    fresh = jnp.where(held, fresh, -jnp.inf)
    top = jnp.maximum(jnp.max(scores, axis=1, keepdims=True), jnp.max(fresh, axis=1, keepdims=True))
    fresh_weights = jnp.exp(fresh - top)
    total = jnp.sum(fresh_weights, axis=1, keepdims=True)
    acc = jnp.dot(fresh_weights.astype(jnp.bfloat16), f_ref[...], preferred_element_type=jnp.float32)
    chunk = min(KEY_CHUNK, k_ref.shape[0])
    for j in range(k_ref.shape[0] // chunk):
        weights = jnp.exp(scores[:, j * chunk:(j + 1) * chunk] - top)
        total = total + jnp.sum(weights, axis=1, keepdims=True)
        acc = acc + jnp.dot(
            weights.astype(jnp.bfloat16), k_ref[j * chunk:(j + 1) * chunk, :],
            preferred_element_type=jnp.float32,
        )
    p_ref[...] = acc
    col = lax.broadcasted_iota(jnp.int32, s_ref.shape, 1)
    s_ref[...] = jnp.where(col == 0, top, jnp.where(col == 1, total, 0.0))


def local_partials(queries, keys, fresh_padded, block):
    rows, width = queries.shape
    d = keys.shape[1]
    return pl.pallas_call(
        partial_kernel,
        grid=(rows // block,),
        out_shape=(
            jax.ShapeDtypeStruct((rows, d), jnp.float32),
            jax.ShapeDtypeStruct((rows, STAT), jnp.float32),
        ),
        in_specs=[
            pl.BlockSpec((block, width), lambda i: (i, 0)),
            pl.BlockSpec(keys.shape, lambda i: (0, 0)),
            pl.BlockSpec(fresh_padded.shape, lambda i: (0, 0)),
        ],
        out_specs=(
            pl.BlockSpec((block, d), lambda i: (i, 0)),
            pl.BlockSpec((block, STAT), lambda i: (i, 0)),
        ),
        compiler_params=pltpu.CompilerParams(vmem_limit_bytes=60 * 1024 * 1024),
    )(queries, keys, fresh_padded)


def gather_kernel(x_ref, o_ref, buf, sems):
    dp = lax.axis_index("dp")
    y, c = dp // 2, lax.rem(dp, 2)
    ys = lax.axis_size("dp") // 2
    qi = lax.axis_index("queue")
    partner = (dp + 1 - 2 * c, qi)

    def along(k):
        return (lax.rem(y + k, ys) * 2 + c, qi)

    barrier = pltpu.get_barrier_semaphore()
    pl.semaphore_signal(barrier, inc=1, device_id=partner, device_id_type=MESH)
    for k in range(1, ys):
        pl.semaphore_signal(barrier, inc=1, device_id=along(k), device_id_type=MESH)
    pl.semaphore_wait(barrier, ys)

    mine = pltpu.make_async_copy(x_ref, buf.at[c, y], sems.at[4])
    mine.start()
    first = [
        pltpu.make_async_remote_copy(
            src_ref=x_ref, dst_ref=buf.at[c, y], send_sem=sems.at[0], recv_sem=sems.at[1],
            device_id=dst, device_id_type=MESH,
        )
        for dst in [partner] + [along(k) for k in range(1, ys)]
    ]
    for copy in first:
        copy.start()
    _wait_bytes(buf.at[0], buf.at[0], sems.at[0], sems.at[1], partner)
    mine.wait()
    second = [
        pltpu.make_async_remote_copy(
            src_ref=buf.at[c, lax.rem(y + k, ys)], dst_ref=buf.at[c, lax.rem(y + k, ys)],
            send_sem=sems.at[2], recv_sem=sems.at[3], device_id=partner, device_id_type=MESH,
        )
        for k in range(1, ys)
    ]
    for copy in second:
        copy.start()
    _wait_bytes(buf.at[0, pl.ds(0, ys - 1)], buf.at[0, pl.ds(0, ys - 1)], sems.at[2], sems.at[3], partner)
    o_ref[...] = buf[...]


def gather_dp(x, ys):
    return pl.pallas_call(
        gather_kernel,
        out_shape=jax.ShapeDtypeStruct((2, ys) + x.shape, x.dtype),
        in_specs=[pl.BlockSpec(memory_space=pltpu.VMEM)],
        out_specs=pl.BlockSpec(memory_space=pltpu.VMEM),
        scratch_shapes=[
            pltpu.VMEM((2, ys) + x.shape, x.dtype),
            pltpu.SemaphoreType.DMA((5,)),
        ],
        compiler_params=pltpu.CompilerParams(collective_id=1, has_side_effects=True),
    )(x)


def _merge(blocks, at):
    top = blocks[0][:, at:at + 1]
    for b in blocks[1:]:
        top = jnp.maximum(top, b[:, at:at + 1])
    acc = blocks[0] * jnp.exp(blocks[0][:, at:at + 1] - top)
    for b in blocks[1:]:
        acc = acc + b * jnp.exp(b[:, at:at + 1] - top)
    col = lax.broadcasted_iota(jnp.int32, acc.shape, 1)
    return jnp.where(col == at, top, acc)


TREES = (("x", "z", "y"), ("z", "y", "x"), ("y", "x", "z"))


def combine_kernel(d, side, p_ref, s_ref, pos_ref, o_ref, loss_ref, own_p, own_s, pair_p, pair_s,
                   send1, recv1, send2, recv2, send3, recv3, loss_buf, loss_pair, sems):
    r = side
    part = d // len(TREES)
    g = p_ref.shape[1]
    dp = lax.axis_index("dp")
    y, c = dp // 2, lax.rem(dp, 2)
    qi = lax.axis_index("queue")
    mine_at = {"y": y, "z": qi // r, "x": lax.rem(qi, r)}
    partner = (dp + 1 - 2 * c, qi)

    def device(at):
        return (at["y"] * 2 + c, at["z"] * r + at["x"])

    def along(axis, j):
        at = dict(mine_at)
        at[axis] = j
        return device(at)

    barrier = pltpu.get_barrier_semaphore()
    pl.semaphore_signal(barrier, inc=1, device_id=partner, device_id_type=MESH)
    for axis in ("x", "z", "y"):
        for k in range(1, r):
            pl.semaphore_signal(barrier, inc=1, device_id=along(axis, lax.rem(mine_at[axis] + k, r)),
                                device_id_type=MESH)
    pl.semaphore_wait(barrier, 1 + 3 * (r - 1))

    pair_copies = [
        pltpu.make_async_remote_copy(
            src_ref=src.at[1 - c], dst_ref=dst, send_sem=sems.at[2 * i], recv_sem=sems.at[2 * i + 1],
            device_id=partner, device_id_type=MESH,
        )
        for i, (src, dst) in enumerate(((p_ref, pair_p), (s_ref, pair_s)))
    ]
    for copy in pair_copies:
        copy.start()
    mine = [pltpu.make_async_copy(src.at[c], dst, sems.at[4 + i])
            for i, (src, dst) in enumerate(((p_ref, own_p), (s_ref, own_s)))]
    for copy in mine:
        copy.start()
    for copy in mine + pair_copies:
        copy.wait()

    def merge_pair(k, carry):
        a, b = own_s[k], pair_s[k]
        top = jnp.maximum(a[:, 0:1], b[:, 0:1])
        wa, wb = jnp.exp(a[:, 0:1] - top), jnp.exp(b[:, 0:1] - top)
        pulled = own_p[k] * wa + pair_p[k] * wb
        col = lax.broadcasted_iota(jnp.int32, a.shape, 1)
        stats = jnp.where(col == 0, top, a * wa + b * wb)
        at = {"y": k // (r * r), "z": lax.rem(k // r, r), "x": lax.rem(k, r)}
        for t, (a1, a2, a3) in enumerate(TREES):
            slot = at[a2] * r + at[a3]
            send1[t, at[a1], slot, :, :part] = pulled[:, t * part:(t + 1) * part]
            send1[t, at[a1], slot, :, part:] = stats
        return carry

    lax.fori_loop(0, g, merge_pair, 0)

    def level(lvl, send, recv, blocks):
        sent = []
        for t, axes in enumerate(TREES):
            axis = axes[lvl]
            me_a = mine_at[axis]
            for k in range(1, r):
                dst = lax.rem(me_a + k, r)
                copy = pltpu.make_async_remote_copy(
                    src_ref=send.at[t, pl.ds(dst * blocks, blocks)], dst_ref=recv.at[t, me_a],
                    send_sem=sems.at[6 + 2 * (3 * lvl + t)], recv_sem=sems.at[7 + 2 * (3 * lvl + t)],
                    device_id=along(axis, dst), device_id_type=MESH,
                )
                copy.start()
            recv[t, me_a] = send[t, pl.ds(me_a * blocks, blocks)]
            sent.append(axis)
        for t, axis in enumerate(sent):
            _wait_bytes(recv.at[t, pl.ds(0, r - 1)], recv.at[t, pl.ds(0, r - 1)],
                        sems.at[6 + 2 * (3 * lvl + t)], sems.at[7 + 2 * (3 * lvl + t)],
                        along(axis, lax.rem(mine_at[axis] + 1, r)))

    def run_level1():
        sent_axes = []
        for t, axes in enumerate(TREES):
            axis = axes[0]
            me_a = mine_at[axis]
            for k in range(1, r):
                dst = lax.rem(me_a + k, r)
                pltpu.make_async_remote_copy(
                    src_ref=send1.at[t, dst], dst_ref=recv1.at[t, me_a],
                    send_sem=sems.at[6 + 2 * t], recv_sem=sems.at[7 + 2 * t],
                    device_id=along(axis, dst), device_id_type=MESH,
                ).start()
            recv1[t, me_a] = send1[t, me_a]
            sent_axes.append(axis)
        for t, axis in enumerate(sent_axes):
            _wait_bytes(send1.at[t, pl.ds(0, r - 1)], recv1.at[t, pl.ds(0, r - 1)],
                        sems.at[6 + 2 * t], sems.at[7 + 2 * t],
                        along(axis, lax.rem(mine_at[axis] + 1, r)))

    run_level1()

    def merge1(b, carry):
        for t in range(len(TREES)):
            send2[t, b] = _merge([recv1[t, i, b] for i in range(r)], part)
        return carry

    lax.fori_loop(0, r * r, merge1, 0)
    level(1, send2, recv2, r)

    for t in range(len(TREES)):
        for a3 in range(r):
            send3[t, a3] = _merge([recv2[t, i, a3] for i in range(r)], part)
    level(2, send3, recv3, 1)

    finals = [_merge([recv3[t, i, 0] for i in range(r)], part) for t in range(len(TREES))]
    stats = finals[0][:, part:]
    for t in range(len(TREES)):
        o_ref[:, t * part:(t + 1) * part] = finals[t][:, :part]
    o_ref[:, d:] = stats
    top = stats[:, 0:1]
    sums = stats[:, 1:2]

    total = jnp.broadcast_to(jnp.sum(top + jnp.log(sums)) - pos_ref[0:1, 0:1], loss_ref.shape)
    for n_axis, axis in enumerate(("x", "z", "y")):
        me_a = mine_at[axis]
        loss_buf[n_axis, me_a] = total
        for k in range(1, r):
            dst = lax.rem(me_a + k, r)
            pltpu.make_async_remote_copy(
                src_ref=loss_buf.at[n_axis, me_a], dst_ref=loss_buf.at[n_axis, me_a],
                send_sem=sems.at[24 + 2 * n_axis], recv_sem=sems.at[25 + 2 * n_axis],
                device_id=along(axis, dst), device_id_type=MESH,
            ).start()
        _wait_bytes(loss_buf.at[n_axis, pl.ds(0, r - 1)], loss_buf.at[n_axis, pl.ds(0, r - 1)],
                    sems.at[24 + 2 * n_axis], sems.at[25 + 2 * n_axis],
                    along(axis, lax.rem(me_a + 1, r)))
        total = loss_buf[n_axis, 0]
        for i in range(1, r):
            total = total + loss_buf[n_axis, i]
    loss_pair[c] = total
    to_pair_loss = pltpu.make_async_remote_copy(
        src_ref=loss_pair.at[c], dst_ref=loss_pair.at[c], send_sem=sems.at[30], recv_sem=sems.at[31],
        device_id=partner, device_id_type=MESH,
    )
    to_pair_loss.start()
    to_pair_loss.wait()
    loss_ref[...] = loss_pair[0] + loss_pair[1]


def combine(pulled, stats, pos, d, side):
    g, rows = pulled.shape[1:3]
    width = d + stats.shape[3]
    trees = len(TREES)
    block = (rows, d // trees + STAT)
    return pl.pallas_call(
        functools.partial(combine_kernel, d, side),
        out_shape=(
            jax.ShapeDtypeStruct((rows, width), jnp.float32),
            jax.ShapeDtypeStruct((8, 128), jnp.float32),
        ),
        in_specs=[
            pl.BlockSpec(memory_space=pl.ANY),
            pl.BlockSpec(memory_space=pl.ANY),
            pl.BlockSpec(memory_space=pltpu.VMEM),
        ],
        out_specs=(
            pl.BlockSpec(memory_space=pltpu.VMEM),
            pl.BlockSpec(memory_space=pltpu.VMEM),
        ),
        scratch_shapes=[
            pltpu.VMEM((g, rows, d), jnp.float32),
            pltpu.VMEM((g, rows, width - d), jnp.float32),
            pltpu.VMEM((g, rows, d), jnp.float32),
            pltpu.VMEM((g, rows, width - d), jnp.float32),
            pltpu.VMEM((trees, side, side * side) + block, jnp.float32),
            pltpu.VMEM((trees, side, side * side) + block, jnp.float32),
            pltpu.VMEM((trees, side * side) + block, jnp.float32),
            pltpu.VMEM((trees, side, side) + block, jnp.float32),
            pltpu.VMEM((trees, side) + block, jnp.float32),
            pltpu.VMEM((trees, side, 1) + block, jnp.float32),
            pltpu.VMEM((3, side, 8, 128), jnp.float32),
            pltpu.VMEM((2, 8, 128), jnp.float32),
            pltpu.SemaphoreType.DMA((32,)),
        ],
        compiler_params=pltpu.CompilerParams(collective_id=0, has_side_effects=True),
    )(pulled, stats, pos)


def shards(queue_keys, fresh_keys, slots, queries, positives):
    dp_size = lax.axis_size("dp")
    queue_size = lax.axis_size("queue")
    n = dp_size * queue_size
    assert fresh_keys.shape[0] == FRESH_HELD
    assert queue_size == (dp_size // 2) ** 2
    d = queries.shape[1]
    pos_code = jnp.zeros((queries.shape[0], STAT), jnp.bfloat16)
    pos_code = pos_code.at[:, 0].set((positives // 32).astype(jnp.bfloat16))
    pos_code = pos_code.at[:, 1].set((positives % 32).astype(jnp.bfloat16))
    gathered = gather_dp(jnp.concatenate([queries, pos_code], axis=1), dp_size // 2)
    total_rows = dp_size * queries.shape[0]
    own_rows = total_rows // n
    gathered = gathered.reshape(total_rows, d + STAT)
    all_queries = gathered[:, :d]
    pos_digits = gathered[:, d:d + 2].astype(jnp.int32)
    all_positives = pos_digits[:, 0] * 32 + pos_digits[:, 1]
    digits = jnp.stack([slots // 16384, (slots // 128) % 128, slots % 128], axis=1)
    code = jnp.zeros((slots.shape[0], STAT), jnp.bfloat16).at[:, :3].set(digits.astype(jnp.bfloat16))
    fresh_ext = lax.all_gather(
        jnp.concatenate([fresh_keys, code], axis=1), ("dp", "queue"), axis=0, tiled=True
    )
    fresh_all = fresh_ext[:, :d]
    got = fresh_ext[:, d:d + 3].astype(jnp.int32)
    slots_all = got[:, 0] * 16384 + got[:, 1] * 128 + got[:, 2]

    device_index = _device_index()
    fresh_padded = jnp.zeros((STAT, d), fresh_keys.dtype).at[:fresh_keys.shape[0]].set(fresh_keys)
    local_pulled, stats = local_partials(gathered, queue_keys, fresh_padded, min(512, total_rows))
    fresh_scores = score_rows(all_queries, fresh_keys)
    fresh_ids = device_index * fresh_keys.shape[0] + jnp.arange(fresh_keys.shape[0], dtype=jnp.int32)
    is_positive = all_positives[:, None] == fresh_ids[None, :]
    positive_total = jnp.sum(jnp.where(is_positive, fresh_scores, 0.0))
    halves = (2, n // 2, own_rows)
    combined, loss_tile = combine(
        local_pulled.reshape(halves + (d,)),
        stats.reshape(halves + (STAT,)),
        jnp.full((8, 128), positive_total, jnp.float32),
        d,
        dp_size // 2,
    )
    sum_rows = combined[:, d + 1]
    pulled = combined[:, :d]
    queue_index = lax.axis_index("queue")
    local_start = queue_index * own_rows
    positive_rows = lax.dynamic_slice_in_dim(positives, local_start, own_rows, 0)
    positive_keys = jnp.take(fresh_all, positive_rows, axis=0).astype(jnp.float32)
    query_grad = pulled / sum_rows[:, None] - positive_keys
    mean_loss = loss_tile[0, 0] / total_rows
    held_rows = queue_keys.shape[0]
    local_slot = slots_all - device_index * held_rows
    picks = jnp.arange(held_rows, dtype=jnp.int32)[:, None] == local_slot[None, :]
    inserted = jnp.dot(picks.astype(jnp.bfloat16), fresh_all, preferred_element_type=jnp.float32)
    replaced = jnp.any(picks, axis=1)
    new_queue = jnp.where(replaced[:, None], inserted.astype(jnp.bfloat16), queue_keys)
    return (query_grad, mean_loss, new_queue)


def solution(mesh):
    placed = (
        P(("dp", "queue"), None),
        P(("dp", "queue"), None),
        P(("dp", "queue")),
        P("dp", None),
        P("dp"),
    )
    return jax.shard_map(
        shards,
        mesh=mesh,
        in_specs=placed,
        out_specs=(P(("dp", "queue"), None), P(), P(("dp", "queue"), None)),
        check_vma=False,
    )
```

```python
import functools

import jax
import jax.numpy as jnp
from jax import lax
from jax.experimental import pallas as pl
from jax.experimental.pallas import tpu as pltpu
from jax.sharding import PartitionSpec as P

MESH = pl.DeviceIdType.MESH
STAT = 128
FRESH_HELD = 8
KEY_CHUNK = 512


def score_rows(query_rows, key_rows):
    return lax.dot_general(
        query_rows, key_rows, (((1,), (1,)), ((), ())), preferred_element_type=jnp.float32
    )


def _device_index():
    return lax.axis_index("dp") * lax.axis_size("queue") + lax.axis_index("queue")


def _wait_bytes(src, dst, send_sem, recv_sem, device_id):
    total = pltpu.make_async_remote_copy(
        src_ref=src, dst_ref=dst, send_sem=send_sem, recv_sem=recv_sem,
        device_id=device_id, device_id_type=MESH,
    )
    total.wait_send()
    total.wait_recv()


def partial_kernel(q_ref, k_ref, f_ref, p_ref, s_ref):
    q = q_ref[:, :k_ref.shape[1]]
    dims = (((1,), (1,)), ((), ()))
    scores = lax.dot_general(q, k_ref[...], dims, preferred_element_type=jnp.float32)
    fresh = lax.dot_general(q, f_ref[...], dims, preferred_element_type=jnp.float32)
    held = lax.broadcasted_iota(jnp.int32, fresh.shape, 1) < FRESH_HELD
    fresh = jnp.where(held, fresh, -jnp.inf)
    top = jnp.maximum(jnp.max(scores, axis=1, keepdims=True), jnp.max(fresh, axis=1, keepdims=True))
    fresh_weights = jnp.exp(fresh - top)
    total = jnp.sum(fresh_weights, axis=1, keepdims=True)
    acc = jnp.dot(fresh_weights.astype(jnp.bfloat16), f_ref[...], preferred_element_type=jnp.float32)
    chunk = min(KEY_CHUNK, k_ref.shape[0])
    for j in range(k_ref.shape[0] // chunk):
        weights = jnp.exp(scores[:, j * chunk:(j + 1) * chunk] - top)
        total = total + jnp.sum(weights, axis=1, keepdims=True)
        acc = acc + jnp.dot(
            weights.astype(jnp.bfloat16), k_ref[j * chunk:(j + 1) * chunk, :],
            preferred_element_type=jnp.float32,
        )
    p_ref[...] = acc
    col = lax.broadcasted_iota(jnp.int32, s_ref.shape, 1)
    s_ref[...] = jnp.where(col == 0, top, jnp.where(col == 1, total, 0.0))


def local_partials(queries, keys, fresh_padded, block):
    rows, width = queries.shape
    d = keys.shape[1]
    return pl.pallas_call(
        partial_kernel,
        grid=(rows // block,),
        out_shape=(
            jax.ShapeDtypeStruct((rows, d), jnp.float32),
            jax.ShapeDtypeStruct((rows, STAT), jnp.float32),
        ),
        in_specs=[
            pl.BlockSpec((block, width), lambda i: (i, 0)),
            pl.BlockSpec(keys.shape, lambda i: (0, 0)),
            pl.BlockSpec(fresh_padded.shape, lambda i: (0, 0)),
        ],
        out_specs=(
            pl.BlockSpec((block, d), lambda i: (i, 0)),
            pl.BlockSpec((block, STAT), lambda i: (i, 0)),
        ),
        compiler_params=pltpu.CompilerParams(vmem_limit_bytes=60 * 1024 * 1024),
    )(queries, keys, fresh_padded)


def gather_kernel(x_ref, f_ref, o_ref, fo_ref, buf, fbuf, sems):
    dp = lax.axis_index("dp")
    y, c = dp // 2, lax.rem(dp, 2)
    ys = lax.axis_size("dp") // 2
    r = ys
    qi = lax.axis_index("queue")
    mine_at = {"y": y, "z": qi // r, "x": lax.rem(qi, r)}
    partner = (dp + 1 - 2 * c, qi)

    def along(axis, j):
        at = dict(mine_at)
        at[axis] = j
        return (at["y"] * 2 + c, at["z"] * r + at["x"])

    barrier = pltpu.get_barrier_semaphore()
    pl.semaphore_signal(barrier, inc=1, device_id=partner, device_id_type=MESH)
    for axis in ("y", "x", "z"):
        for k in range(1, r):
            pl.semaphore_signal(barrier, inc=1, device_id=along(axis, lax.rem(mine_at[axis] + k, r)),
                                device_id_type=MESH)
    pl.semaphore_wait(barrier, 1 + 3 * (r - 1))

    mine = pltpu.make_async_copy(x_ref, buf.at[c, y], sems.at[4])
    mine.start()
    first = [
        pltpu.make_async_remote_copy(
            src_ref=x_ref, dst_ref=buf.at[c, y], send_sem=sems.at[0], recv_sem=sems.at[1],
            device_id=dst, device_id_type=MESH,
        )
        for dst in [partner] + [along("y", lax.rem(y + k, ys)) for k in range(1, ys)]
    ]
    for copy in first:
        copy.start()

    yi, zi, xi = mine_at["y"], mine_at["z"], mine_at["x"]

    def fresh_round(i, axis, src, dst):
        for k in range(1, r):
            pltpu.make_async_remote_copy(
                src_ref=src, dst_ref=dst, send_sem=sems.at[6 + 2 * i], recv_sem=sems.at[7 + 2 * i],
                device_id=along(axis, lax.rem(mine_at[axis] + k, r)), device_id_type=MESH,
            ).start()

    own_fresh = pltpu.make_async_copy(f_ref, fbuf.at[yi, c, zi, xi], sems.at[5])
    own_fresh.start()
    fresh_round(0, "x", f_ref, fbuf.at[yi, c, zi, xi])
    own_fresh.wait()
    _wait_bytes(fbuf.at[0, 0, 0, pl.ds(0, r - 1)], fbuf.at[0, 0, 0, pl.ds(0, r - 1)],
                sems.at[6], sems.at[7], along("x", lax.rem(xi + 1, r)))
    fresh_round(1, "z", fbuf.at[yi, c, zi], fbuf.at[yi, c, zi])
    _wait_bytes(fbuf.at[0, 0, pl.ds(0, r - 1)], fbuf.at[0, 0, pl.ds(0, r - 1)],
                sems.at[8], sems.at[9], along("z", lax.rem(zi + 1, r)))
    fresh_round(2, "y", fbuf.at[yi, c], fbuf.at[yi, c])

    _wait_bytes(buf.at[0], buf.at[0], sems.at[0], sems.at[1], partner)
    mine.wait()
    second = [
        pltpu.make_async_remote_copy(
            src_ref=buf.at[c, lax.rem(y + k, ys)], dst_ref=buf.at[c, lax.rem(y + k, ys)],
            send_sem=sems.at[2], recv_sem=sems.at[3], device_id=partner, device_id_type=MESH,
        )
        for k in range(1, ys)
    ]
    for copy in second:
        copy.start()
    _wait_bytes(fbuf.at[pl.ds(0, r - 1), 0], fbuf.at[pl.ds(0, r - 1), 0],
                sems.at[10], sems.at[11], along("y", lax.rem(yi + 1, r)))
    for j in range(r):
        pltpu.make_async_remote_copy(
            src_ref=fbuf.at[j, c], dst_ref=fbuf.at[j, c], send_sem=sems.at[12], recv_sem=sems.at[13],
            device_id=partner, device_id_type=MESH,
        ).start()
    _wait_bytes(buf.at[0, pl.ds(0, ys - 1)], buf.at[0, pl.ds(0, ys - 1)], sems.at[2], sems.at[3], partner)
    _wait_bytes(fbuf.at[:, 0], fbuf.at[:, 0], sems.at[12], sems.at[13], partner)
    o_ref[...] = buf[...]
    fo_ref[...] = fbuf[...]


def gather_dp(x, fresh, ys):
    return pl.pallas_call(
        gather_kernel,
        out_shape=(
            jax.ShapeDtypeStruct((2, ys) + x.shape, x.dtype),
            jax.ShapeDtypeStruct((ys, 2, ys, ys) + fresh.shape, fresh.dtype),
        ),
        in_specs=[pl.BlockSpec(memory_space=pltpu.VMEM), pl.BlockSpec(memory_space=pltpu.VMEM)],
        out_specs=(pl.BlockSpec(memory_space=pltpu.VMEM), pl.BlockSpec(memory_space=pltpu.VMEM)),
        scratch_shapes=[
            pltpu.VMEM((2, ys) + x.shape, x.dtype),
            pltpu.VMEM((ys, 2, ys, ys) + fresh.shape, fresh.dtype),
            pltpu.SemaphoreType.DMA((14,)),
        ],
        compiler_params=pltpu.CompilerParams(collective_id=1, has_side_effects=True),
    )(x, fresh)


def _merge(blocks, at):
    top = blocks[0][:, at:at + 1]
    for b in blocks[1:]:
        top = jnp.maximum(top, b[:, at:at + 1])
    acc = blocks[0] * jnp.exp(blocks[0][:, at:at + 1] - top)
    for b in blocks[1:]:
        acc = acc + b * jnp.exp(b[:, at:at + 1] - top)
    col = lax.broadcasted_iota(jnp.int32, acc.shape, 1)
    return jnp.where(col == at, top, acc)


TREES = (("x", "z", "y"), ("z", "y", "x"), ("y", "x", "z"))


def combine_kernel(d, side, p_ref, s_ref, pos_ref, o_ref, loss_ref, own_p, own_s, pair_p, pair_s,
                   send1, recv1, send2, recv2, send3, recv3, loss_buf, loss_pair, sems):
    r = side
    part = d // len(TREES)
    g = p_ref.shape[1]
    dp = lax.axis_index("dp")
    y, c = dp // 2, lax.rem(dp, 2)
    qi = lax.axis_index("queue")
    mine_at = {"y": y, "z": qi // r, "x": lax.rem(qi, r)}
    partner = (dp + 1 - 2 * c, qi)

    def device(at):
        return (at["y"] * 2 + c, at["z"] * r + at["x"])

    def along(axis, j):
        at = dict(mine_at)
        at[axis] = j
        return device(at)

    barrier = pltpu.get_barrier_semaphore()
    pl.semaphore_signal(barrier, inc=1, device_id=partner, device_id_type=MESH)
    for axis in ("x", "z", "y"):
        for k in range(1, r):
            pl.semaphore_signal(barrier, inc=1, device_id=along(axis, lax.rem(mine_at[axis] + k, r)),
                                device_id_type=MESH)
    pl.semaphore_wait(barrier, 1 + 3 * (r - 1))

    pair_copies = [
        pltpu.make_async_remote_copy(
            src_ref=src.at[1 - c], dst_ref=dst, send_sem=sems.at[2 * i], recv_sem=sems.at[2 * i + 1],
            device_id=partner, device_id_type=MESH,
        )
        for i, (src, dst) in enumerate(((p_ref, pair_p), (s_ref, pair_s)))
    ]
    for copy in pair_copies:
        copy.start()
    mine = [pltpu.make_async_copy(src.at[c], dst, sems.at[4 + i])
            for i, (src, dst) in enumerate(((p_ref, own_p), (s_ref, own_s)))]
    for copy in mine:
        copy.start()
    for copy in mine + pair_copies:
        copy.wait()

    def merge_pair(k, carry):
        a, b = own_s[k], pair_s[k]
        top = jnp.maximum(a[:, 0:1], b[:, 0:1])
        wa, wb = jnp.exp(a[:, 0:1] - top), jnp.exp(b[:, 0:1] - top)
        pulled = own_p[k] * wa + pair_p[k] * wb
        col = lax.broadcasted_iota(jnp.int32, a.shape, 1)
        stats = jnp.where(col == 0, top, a * wa + b * wb)
        at = {"y": k // (r * r), "z": lax.rem(k // r, r), "x": lax.rem(k, r)}
        for t, (a1, a2, a3) in enumerate(TREES):
            slot = at[a2] * r + at[a3]
            send1[t, at[a1], slot, :, :part] = pulled[:, t * part:(t + 1) * part]
            send1[t, at[a1], slot, :, part:] = stats
        return carry

    lax.fori_loop(0, g, merge_pair, 0)

    def level(lvl, send, recv, blocks):
        sent = []
        for t, axes in enumerate(TREES):
            axis = axes[lvl]
            me_a = mine_at[axis]
            for k in range(1, r):
                dst = lax.rem(me_a + k, r)
                copy = pltpu.make_async_remote_copy(
                    src_ref=send.at[t, pl.ds(dst * blocks, blocks)], dst_ref=recv.at[t, me_a],
                    send_sem=sems.at[6 + 2 * (3 * lvl + t)], recv_sem=sems.at[7 + 2 * (3 * lvl + t)],
                    device_id=along(axis, dst), device_id_type=MESH,
                )
                copy.start()
            recv[t, me_a] = send[t, pl.ds(me_a * blocks, blocks)]
            sent.append(axis)
        for t, axis in enumerate(sent):
            _wait_bytes(recv.at[t, pl.ds(0, r - 1)], recv.at[t, pl.ds(0, r - 1)],
                        sems.at[6 + 2 * (3 * lvl + t)], sems.at[7 + 2 * (3 * lvl + t)],
                        along(axis, lax.rem(mine_at[axis] + 1, r)))

    def run_level1():
        sent_axes = []
        for t, axes in enumerate(TREES):
            axis = axes[0]
            me_a = mine_at[axis]
            for k in range(1, r):
                dst = lax.rem(me_a + k, r)
                pltpu.make_async_remote_copy(
                    src_ref=send1.at[t, dst], dst_ref=recv1.at[t, me_a],
                    send_sem=sems.at[6 + 2 * t], recv_sem=sems.at[7 + 2 * t],
                    device_id=along(axis, dst), device_id_type=MESH,
                ).start()
            recv1[t, me_a] = send1[t, me_a]
            sent_axes.append(axis)
        for t, axis in enumerate(sent_axes):
            _wait_bytes(send1.at[t, pl.ds(0, r - 1)], recv1.at[t, pl.ds(0, r - 1)],
                        sems.at[6 + 2 * t], sems.at[7 + 2 * t],
                        along(axis, lax.rem(mine_at[axis] + 1, r)))

    run_level1()

    def merge1(b, carry):
        for t in range(len(TREES)):
            send2[t, b] = _merge([recv1[t, i, b] for i in range(r)], part)
        return carry

    lax.fori_loop(0, r * r, merge1, 0)
    level(1, send2, recv2, r)

    for t in range(len(TREES)):
        for a3 in range(r):
            send3[t, a3] = _merge([recv2[t, i, a3] for i in range(r)], part)
    level(2, send3, recv3, 1)

    finals = [_merge([recv3[t, i, 0] for i in range(r)], part) for t in range(len(TREES))]
    stats = finals[0][:, part:]
    for t in range(len(TREES)):
        o_ref[:, t * part:(t + 1) * part] = finals[t][:, :part]
    o_ref[:, d:] = stats
    top = stats[:, 0:1]
    sums = stats[:, 1:2]

    total = jnp.broadcast_to(jnp.sum(top + jnp.log(sums)) - pos_ref[0:1, 0:1], loss_ref.shape)
    for n_axis, axis in enumerate(("x", "z", "y")):
        me_a = mine_at[axis]
        loss_buf[n_axis, me_a] = total
        for k in range(1, r):
            dst = lax.rem(me_a + k, r)
            pltpu.make_async_remote_copy(
                src_ref=loss_buf.at[n_axis, me_a], dst_ref=loss_buf.at[n_axis, me_a],
                send_sem=sems.at[24 + 2 * n_axis], recv_sem=sems.at[25 + 2 * n_axis],
                device_id=along(axis, dst), device_id_type=MESH,
            ).start()
        _wait_bytes(loss_buf.at[n_axis, pl.ds(0, r - 1)], loss_buf.at[n_axis, pl.ds(0, r - 1)],
                    sems.at[24 + 2 * n_axis], sems.at[25 + 2 * n_axis],
                    along(axis, lax.rem(me_a + 1, r)))
        total = loss_buf[n_axis, 0]
        for i in range(1, r):
            total = total + loss_buf[n_axis, i]
    loss_pair[c] = total
    to_pair_loss = pltpu.make_async_remote_copy(
        src_ref=loss_pair.at[c], dst_ref=loss_pair.at[c], send_sem=sems.at[30], recv_sem=sems.at[31],
        device_id=partner, device_id_type=MESH,
    )
    to_pair_loss.start()
    to_pair_loss.wait()
    loss_ref[...] = loss_pair[0] + loss_pair[1]


def combine(pulled, stats, pos, d, side):
    g, rows = pulled.shape[1:3]
    width = d + stats.shape[3]
    trees = len(TREES)
    block = (rows, d // trees + STAT)
    return pl.pallas_call(
        functools.partial(combine_kernel, d, side),
        out_shape=(
            jax.ShapeDtypeStruct((rows, width), jnp.float32),
            jax.ShapeDtypeStruct((8, 128), jnp.float32),
        ),
        in_specs=[
            pl.BlockSpec(memory_space=pl.ANY),
            pl.BlockSpec(memory_space=pl.ANY),
            pl.BlockSpec(memory_space=pltpu.VMEM),
        ],
        out_specs=(
            pl.BlockSpec(memory_space=pltpu.VMEM),
            pl.BlockSpec(memory_space=pltpu.VMEM),
        ),
        scratch_shapes=[
            pltpu.VMEM((g, rows, d), jnp.float32),
            pltpu.VMEM((g, rows, width - d), jnp.float32),
            pltpu.VMEM((g, rows, d), jnp.float32),
            pltpu.VMEM((g, rows, width - d), jnp.float32),
            pltpu.VMEM((trees, side, side * side) + block, jnp.float32),
            pltpu.VMEM((trees, side, side * side) + block, jnp.float32),
            pltpu.VMEM((trees, side * side) + block, jnp.float32),
            pltpu.VMEM((trees, side, side) + block, jnp.float32),
            pltpu.VMEM((trees, side) + block, jnp.float32),
            pltpu.VMEM((trees, side, 1) + block, jnp.float32),
            pltpu.VMEM((3, side, 8, 128), jnp.float32),
            pltpu.VMEM((2, 8, 128), jnp.float32),
            pltpu.SemaphoreType.DMA((32,)),
        ],
        compiler_params=pltpu.CompilerParams(collective_id=0, has_side_effects=True),
    )(pulled, stats, pos)


def shards(queue_keys, fresh_keys, slots, queries, positives):
    dp_size = lax.axis_size("dp")
    queue_size = lax.axis_size("queue")
    n = dp_size * queue_size
    assert fresh_keys.shape[0] == FRESH_HELD
    assert queue_size == (dp_size // 2) ** 2
    d = queries.shape[1]
    pos_code = jnp.zeros((queries.shape[0], STAT), jnp.bfloat16)
    pos_code = pos_code.at[:, 0].set((positives // 32).astype(jnp.bfloat16))
    pos_code = pos_code.at[:, 1].set((positives % 32).astype(jnp.bfloat16))
    digits = jnp.stack([slots // 16384, (slots // 128) % 128, slots % 128], axis=1)
    code = jnp.zeros((slots.shape[0], STAT), jnp.bfloat16).at[:, :3].set(digits.astype(jnp.bfloat16))
    gathered, fresh_ext = gather_dp(
        jnp.concatenate([queries, pos_code], axis=1),
        jnp.concatenate([fresh_keys, code], axis=1),
        dp_size // 2,
    )
    fresh_ext = fresh_ext.reshape(n * fresh_keys.shape[0], d + STAT)
    total_rows = dp_size * queries.shape[0]
    own_rows = total_rows // n
    gathered = gathered.reshape(total_rows, d + STAT)
    all_queries = gathered[:, :d]
    pos_digits = gathered[:, d:d + 2].astype(jnp.int32)
    all_positives = pos_digits[:, 0] * 32 + pos_digits[:, 1]
    fresh_all = fresh_ext[:, :d]
    got = fresh_ext[:, d:d + 3].astype(jnp.int32)
    slots_all = got[:, 0] * 16384 + got[:, 1] * 128 + got[:, 2]

    device_index = _device_index()
    fresh_padded = jnp.zeros((STAT, d), fresh_keys.dtype).at[:fresh_keys.shape[0]].set(fresh_keys)
    local_pulled, stats = local_partials(gathered, queue_keys, fresh_padded, min(256, total_rows))
    fresh_scores = score_rows(all_queries, fresh_keys)
    fresh_ids = device_index * fresh_keys.shape[0] + jnp.arange(fresh_keys.shape[0], dtype=jnp.int32)
    is_positive = all_positives[:, None] == fresh_ids[None, :]
    positive_total = jnp.sum(jnp.where(is_positive, fresh_scores, 0.0))
    halves = (2, n // 2, own_rows)
    combined, loss_tile = combine(
        local_pulled.reshape(halves + (d,)),
        stats.reshape(halves + (STAT,)),
        jnp.full((8, 128), positive_total, jnp.float32),
        d,
        dp_size // 2,
    )
    sum_rows = combined[:, d + 1]
    pulled = combined[:, :d]
    queue_index = lax.axis_index("queue")
    local_start = queue_index * own_rows
    positive_rows = lax.dynamic_slice_in_dim(positives, local_start, own_rows, 0)
    positive_keys = jnp.take(fresh_all, positive_rows, axis=0).astype(jnp.float32)
    query_grad = pulled / sum_rows[:, None] - positive_keys
    mean_loss = loss_tile[0, 0] / total_rows
    held_rows = queue_keys.shape[0]
    local_slot = slots_all - device_index * held_rows
    picks = jnp.arange(held_rows, dtype=jnp.int32)[:, None] == local_slot[None, :]
    inserted = jnp.dot(picks.astype(jnp.bfloat16), fresh_all, preferred_element_type=jnp.float32)
    replaced = jnp.any(picks, axis=1)
    new_queue = jnp.where(replaced[:, None], inserted.astype(jnp.bfloat16), queue_keys)
    return (query_grad, mean_loss, new_queue)


def solution(mesh):
    placed = (
        P(("dp", "queue"), None),
        P(("dp", "queue"), None),
        P(("dp", "queue")),
        P("dp", None),
        P("dp"),
    )
    return jax.shard_map(
        shards,
        mesh=mesh,
        in_specs=placed,
        out_specs=(P(("dp", "queue"), None), P(), P(("dp", "queue"), None)),
        check_vma=False,
    )
```

```python
import functools

import jax
import jax.numpy as jnp
from jax import lax
from jax.experimental import pallas as pl
from jax.experimental.pallas import tpu as pltpu
from jax.sharding import PartitionSpec as P

MESH = pl.DeviceIdType.MESH
STAT = 128
FRESH_HELD = 8
KEY_CHUNK = 512


def score_rows(query_rows, key_rows):
    return lax.dot_general(
        query_rows, key_rows, (((1,), (1,)), ((), ())), preferred_element_type=jnp.float32
    )


def _device_index():
    return lax.axis_index("dp") * lax.axis_size("queue") + lax.axis_index("queue")


def _wait_bytes(src, dst, send_sem, recv_sem, device_id):
    total = pltpu.make_async_remote_copy(
        src_ref=src, dst_ref=dst, send_sem=send_sem, recv_sem=recv_sem,
        device_id=device_id, device_id_type=MESH,
    )
    total.wait_send()
    total.wait_recv()


def partial_kernel(q_ref, k_ref, f_ref, p_ref, s_ref):
    q = q_ref[:, :k_ref.shape[1]]
    dims = (((1,), (1,)), ((), ()))
    scores = lax.dot_general(q, k_ref[...], dims, preferred_element_type=jnp.float32)
    fresh = lax.dot_general(q, f_ref[...], dims, preferred_element_type=jnp.float32)
    held = lax.broadcasted_iota(jnp.int32, fresh.shape, 1) < FRESH_HELD
    fresh = jnp.where(held, fresh, -jnp.inf)
    top = jnp.maximum(jnp.max(scores, axis=1, keepdims=True), jnp.max(fresh, axis=1, keepdims=True))
    fresh_weights = jnp.exp(fresh - top)
    total = jnp.sum(fresh_weights, axis=1, keepdims=True)
    acc = jnp.dot(fresh_weights.astype(jnp.bfloat16), f_ref[...], preferred_element_type=jnp.float32)
    chunk = min(KEY_CHUNK, k_ref.shape[0])
    for j in range(k_ref.shape[0] // chunk):
        weights = jnp.exp(scores[:, j * chunk:(j + 1) * chunk] - top)
        total = total + jnp.sum(weights, axis=1, keepdims=True)
        acc = acc + jnp.dot(
            weights.astype(jnp.bfloat16), k_ref[j * chunk:(j + 1) * chunk, :],
            preferred_element_type=jnp.float32,
        )
    p_ref[...] = acc
    col = lax.broadcasted_iota(jnp.int32, s_ref.shape, 1)
    s_ref[...] = jnp.where(col == 0, top, jnp.where(col == 1, total, 0.0))


def local_partials(queries, keys, fresh_padded, block):
    rows, width = queries.shape
    d = keys.shape[1]
    return pl.pallas_call(
        partial_kernel,
        grid=(rows // block,),
        out_shape=(
            jax.ShapeDtypeStruct((rows, d), jnp.float32),
            jax.ShapeDtypeStruct((rows, STAT), jnp.float32),
        ),
        in_specs=[
            pl.BlockSpec((block, width), lambda i: (i, 0)),
            pl.BlockSpec(keys.shape, lambda i: (0, 0)),
            pl.BlockSpec(fresh_padded.shape, lambda i: (0, 0)),
        ],
        out_specs=(
            pl.BlockSpec((block, d), lambda i: (i, 0)),
            pl.BlockSpec((block, STAT), lambda i: (i, 0)),
        ),
        compiler_params=pltpu.CompilerParams(vmem_limit_bytes=60 * 1024 * 1024),
    )(queries, keys, fresh_padded)


def gather_kernel(x_ref, f_ref, o_ref, fo_ref, buf, fbuf, sems):
    dp = lax.axis_index("dp")
    y, c = dp // 2, lax.rem(dp, 2)
    ys = lax.axis_size("dp") // 2
    r = ys
    qi = lax.axis_index("queue")
    mine_at = {"y": y, "z": qi // r, "x": lax.rem(qi, r)}
    partner = (dp + 1 - 2 * c, qi)

    def along(axis, j):
        at = dict(mine_at)
        at[axis] = j
        return (at["y"] * 2 + c, at["z"] * r + at["x"])

    barrier = pltpu.get_barrier_semaphore()
    pl.semaphore_signal(barrier, inc=1, device_id=partner, device_id_type=MESH)
    for axis in ("y", "x", "z"):
        for k in range(1, r):
            pl.semaphore_signal(barrier, inc=1, device_id=along(axis, lax.rem(mine_at[axis] + k, r)),
                                device_id_type=MESH)
    pl.semaphore_wait(barrier, 1 + 3 * (r - 1))

    mine = pltpu.make_async_copy(x_ref, buf.at[c, y], sems.at[4])
    mine.start()
    first = [
        pltpu.make_async_remote_copy(
            src_ref=x_ref, dst_ref=buf.at[c, y], send_sem=sems.at[0], recv_sem=sems.at[1],
            device_id=dst, device_id_type=MESH,
        )
        for dst in [partner] + [along("y", lax.rem(y + k, ys)) for k in range(1, ys)]
    ]
    for copy in first:
        copy.start()

    yi, zi, xi = mine_at["y"], mine_at["z"], mine_at["x"]

    def fresh_round(i, axis, src, dst):
        for k in range(1, r):
            pltpu.make_async_remote_copy(
                src_ref=src, dst_ref=dst, send_sem=sems.at[6 + 2 * i], recv_sem=sems.at[7 + 2 * i],
                device_id=along(axis, lax.rem(mine_at[axis] + k, r)), device_id_type=MESH,
            ).start()

    own_fresh = pltpu.make_async_copy(f_ref, fbuf.at[yi, c, zi, xi], sems.at[5])
    own_fresh.start()
    fresh_round(0, "x", f_ref, fbuf.at[yi, c, zi, xi])
    own_fresh.wait()
    _wait_bytes(fbuf.at[0, 0, 0, pl.ds(0, r - 1)], fbuf.at[0, 0, 0, pl.ds(0, r - 1)],
                sems.at[6], sems.at[7], along("x", lax.rem(xi + 1, r)))
    fresh_round(1, "z", fbuf.at[yi, c, zi], fbuf.at[yi, c, zi])
    _wait_bytes(fbuf.at[0, 0, pl.ds(0, r - 1)], fbuf.at[0, 0, pl.ds(0, r - 1)],
                sems.at[8], sems.at[9], along("z", lax.rem(zi + 1, r)))
    fresh_round(2, "y", fbuf.at[yi, c], fbuf.at[yi, c])

    _wait_bytes(buf.at[0], buf.at[0], sems.at[0], sems.at[1], partner)
    mine.wait()
    second = [
        pltpu.make_async_remote_copy(
            src_ref=buf.at[c, lax.rem(y + k, ys)], dst_ref=buf.at[c, lax.rem(y + k, ys)],
            send_sem=sems.at[2], recv_sem=sems.at[3], device_id=partner, device_id_type=MESH,
        )
        for k in range(1, ys)
    ]
    for copy in second:
        copy.start()
    _wait_bytes(fbuf.at[pl.ds(0, r - 1), 0], fbuf.at[pl.ds(0, r - 1), 0],
                sems.at[10], sems.at[11], along("y", lax.rem(yi + 1, r)))
    for j in range(r):
        pltpu.make_async_remote_copy(
            src_ref=fbuf.at[j, c], dst_ref=fbuf.at[j, c], send_sem=sems.at[12], recv_sem=sems.at[13],
            device_id=partner, device_id_type=MESH,
        ).start()
    _wait_bytes(buf.at[0, pl.ds(0, ys - 1)], buf.at[0, pl.ds(0, ys - 1)], sems.at[2], sems.at[3], partner)
    _wait_bytes(fbuf.at[:, 0], fbuf.at[:, 0], sems.at[12], sems.at[13], partner)
    o_ref[...] = buf[...]
    fo_ref[...] = fbuf[...]


def gather_dp(x, fresh, ys):
    return pl.pallas_call(
        gather_kernel,
        out_shape=(
            jax.ShapeDtypeStruct((2, ys) + x.shape, x.dtype),
            jax.ShapeDtypeStruct((ys, 2, ys, ys) + fresh.shape, fresh.dtype),
        ),
        in_specs=[pl.BlockSpec(memory_space=pltpu.VMEM), pl.BlockSpec(memory_space=pltpu.VMEM)],
        out_specs=(pl.BlockSpec(memory_space=pltpu.VMEM), pl.BlockSpec(memory_space=pltpu.VMEM)),
        scratch_shapes=[
            pltpu.VMEM((2, ys) + x.shape, x.dtype),
            pltpu.VMEM((ys, 2, ys, ys) + fresh.shape, fresh.dtype),
            pltpu.SemaphoreType.DMA((14,)),
        ],
        compiler_params=pltpu.CompilerParams(collective_id=1, has_side_effects=True),
    )(x, fresh)


def _merge(blocks, at):
    top = blocks[0][:, at:at + 1]
    for b in blocks[1:]:
        top = jnp.maximum(top, b[:, at:at + 1])
    acc = blocks[0] * jnp.exp(blocks[0][:, at:at + 1] - top)
    for b in blocks[1:]:
        acc = acc + b * jnp.exp(b[:, at:at + 1] - top)
    col = lax.broadcasted_iota(jnp.int32, acc.shape, 1)
    return jnp.where(col == at, top, acc)


TREES = (("x", "z", "y"), ("z", "y", "x"), ("y", "x", "z"))


def combine_kernel(d, side, p_ref, s_ref, pos_ref, o_ref, loss_ref, own_p, own_s, pair_p, pair_s,
                   send1, recv1, send2, recv2, send3, recv3, loss_buf, loss_pair, sems):
    r = side
    part = d // len(TREES)
    g = p_ref.shape[1]
    dp = lax.axis_index("dp")
    y, c = dp // 2, lax.rem(dp, 2)
    qi = lax.axis_index("queue")
    mine_at = {"y": y, "z": qi // r, "x": lax.rem(qi, r)}
    partner = (dp + 1 - 2 * c, qi)

    def device(at):
        return (at["y"] * 2 + c, at["z"] * r + at["x"])

    def along(axis, j):
        at = dict(mine_at)
        at[axis] = j
        return device(at)

    barrier = pltpu.get_barrier_semaphore()
    pl.semaphore_signal(barrier, inc=1, device_id=partner, device_id_type=MESH)
    for axis in ("x", "z", "y"):
        for k in range(1, r):
            pl.semaphore_signal(barrier, inc=1, device_id=along(axis, lax.rem(mine_at[axis] + k, r)),
                                device_id_type=MESH)
    pl.semaphore_wait(barrier, 1 + 3 * (r - 1))

    pair_copies = [
        pltpu.make_async_remote_copy(
            src_ref=src.at[1 - c], dst_ref=dst, send_sem=sems.at[2 * i], recv_sem=sems.at[2 * i + 1],
            device_id=partner, device_id_type=MESH,
        )
        for i, (src, dst) in enumerate(((p_ref, pair_p), (s_ref, pair_s)))
    ]
    for copy in pair_copies:
        copy.start()
    mine = [pltpu.make_async_copy(src.at[c], dst, sems.at[4 + i])
            for i, (src, dst) in enumerate(((p_ref, own_p), (s_ref, own_s)))]
    for copy in mine:
        copy.start()
    for copy in mine + pair_copies:
        copy.wait()

    def merge_pair(k, carry):
        a, b = own_s[k], pair_s[k]
        top = jnp.maximum(a[:, 0:1], b[:, 0:1])
        wa, wb = jnp.exp(a[:, 0:1] - top), jnp.exp(b[:, 0:1] - top)
        pulled = own_p[k] * wa + pair_p[k] * wb
        col = lax.broadcasted_iota(jnp.int32, a.shape, 1)
        stats = jnp.where(col == 0, top, a * wa + b * wb)
        at = {"y": k // (r * r), "z": lax.rem(k // r, r), "x": lax.rem(k, r)}
        for t, (a1, a2, a3) in enumerate(TREES):
            slot = at[a2] * r + at[a3]
            send1[t, at[a1], slot, :, :part] = pulled[:, t * part:(t + 1) * part]
            send1[t, at[a1], slot, :, part:] = stats
        return carry

    lax.fori_loop(0, g, merge_pair, 0)

    def level(lvl, send, recv, blocks):
        sent = []
        for t, axes in enumerate(TREES):
            axis = axes[lvl]
            me_a = mine_at[axis]
            for k in range(1, r):
                dst = lax.rem(me_a + k, r)
                copy = pltpu.make_async_remote_copy(
                    src_ref=send.at[t, pl.ds(dst * blocks, blocks)], dst_ref=recv.at[t, me_a],
                    send_sem=sems.at[6 + 2 * (3 * lvl + t)], recv_sem=sems.at[7 + 2 * (3 * lvl + t)],
                    device_id=along(axis, dst), device_id_type=MESH,
                )
                copy.start()
            recv[t, me_a] = send[t, pl.ds(me_a * blocks, blocks)]
            sent.append(axis)
        for t, axis in enumerate(sent):
            _wait_bytes(recv.at[t, pl.ds(0, r - 1)], recv.at[t, pl.ds(0, r - 1)],
                        sems.at[6 + 2 * (3 * lvl + t)], sems.at[7 + 2 * (3 * lvl + t)],
                        along(axis, lax.rem(mine_at[axis] + 1, r)))

    def run_level1():
        sent_axes = []
        for t, axes in enumerate(TREES):
            axis = axes[0]
            me_a = mine_at[axis]
            for k in range(1, r):
                dst = lax.rem(me_a + k, r)
                pltpu.make_async_remote_copy(
                    src_ref=send1.at[t, dst], dst_ref=recv1.at[t, me_a],
                    send_sem=sems.at[6 + 2 * t], recv_sem=sems.at[7 + 2 * t],
                    device_id=along(axis, dst), device_id_type=MESH,
                ).start()
            recv1[t, me_a] = send1[t, me_a]
            sent_axes.append(axis)
        for t, axis in enumerate(sent_axes):
            _wait_bytes(send1.at[t, pl.ds(0, r - 1)], recv1.at[t, pl.ds(0, r - 1)],
                        sems.at[6 + 2 * t], sems.at[7 + 2 * t],
                        along(axis, lax.rem(mine_at[axis] + 1, r)))

    run_level1()

    def merge1(b, carry):
        for t in range(len(TREES)):
            send2[t, b] = _merge([recv1[t, i, b] for i in range(r)], part)
        return carry

    lax.fori_loop(0, r * r, merge1, 0)
    level(1, send2, recv2, r)

    for t in range(len(TREES)):
        for a3 in range(r):
            send3[t, a3] = _merge([recv2[t, i, a3] for i in range(r)], part)
    level(2, send3, recv3, 1)

    finals = [_merge([recv3[t, i, 0] for i in range(r)], part) for t in range(len(TREES))]
    stats = finals[0][:, part:]
    for t in range(len(TREES)):
        o_ref[:, t * part:(t + 1) * part] = finals[t][:, :part]
    o_ref[:, d:] = stats
    top = stats[:, 0:1]
    sums = stats[:, 1:2]

    total = jnp.broadcast_to(jnp.sum(top + jnp.log(sums)) - pos_ref[0:1, 0:1], loss_ref.shape)
    for n_axis, axis in enumerate(("x", "z", "y")):
        me_a = mine_at[axis]
        loss_buf[n_axis, me_a] = total
        for k in range(1, r):
            dst = lax.rem(me_a + k, r)
            pltpu.make_async_remote_copy(
                src_ref=loss_buf.at[n_axis, me_a], dst_ref=loss_buf.at[n_axis, me_a],
                send_sem=sems.at[24 + 2 * n_axis], recv_sem=sems.at[25 + 2 * n_axis],
                device_id=along(axis, dst), device_id_type=MESH,
            ).start()
        _wait_bytes(loss_buf.at[n_axis, pl.ds(0, r - 1)], loss_buf.at[n_axis, pl.ds(0, r - 1)],
                    sems.at[24 + 2 * n_axis], sems.at[25 + 2 * n_axis],
                    along(axis, lax.rem(me_a + 1, r)))
        total = loss_buf[n_axis, 0]
        for i in range(1, r):
            total = total + loss_buf[n_axis, i]
    loss_pair[c] = total
    to_pair_loss = pltpu.make_async_remote_copy(
        src_ref=loss_pair.at[c], dst_ref=loss_pair.at[c], send_sem=sems.at[30], recv_sem=sems.at[31],
        device_id=partner, device_id_type=MESH,
    )
    to_pair_loss.start()
    to_pair_loss.wait()
    loss_ref[...] = loss_pair[0] + loss_pair[1]


def combine(pulled, stats, pos, d, side):
    g, rows = pulled.shape[1:3]
    width = d + stats.shape[3]
    trees = len(TREES)
    block = (rows, d // trees + STAT)
    return pl.pallas_call(
        functools.partial(combine_kernel, d, side),
        out_shape=(
            jax.ShapeDtypeStruct((rows, width), jnp.float32),
            jax.ShapeDtypeStruct((8, 128), jnp.float32),
        ),
        in_specs=[
            pl.BlockSpec(memory_space=pl.ANY),
            pl.BlockSpec(memory_space=pl.ANY),
            pl.BlockSpec(memory_space=pltpu.VMEM),
        ],
        out_specs=(
            pl.BlockSpec(memory_space=pltpu.VMEM),
            pl.BlockSpec(memory_space=pltpu.VMEM),
        ),
        scratch_shapes=[
            pltpu.VMEM((g, rows, d), jnp.float32),
            pltpu.VMEM((g, rows, width - d), jnp.float32),
            pltpu.VMEM((g, rows, d), jnp.float32),
            pltpu.VMEM((g, rows, width - d), jnp.float32),
            pltpu.VMEM((trees, side, side * side) + block, jnp.float32),
            pltpu.VMEM((trees, side, side * side) + block, jnp.float32),
            pltpu.VMEM((trees, side * side) + block, jnp.float32),
            pltpu.VMEM((trees, side, side) + block, jnp.float32),
            pltpu.VMEM((trees, side) + block, jnp.float32),
            pltpu.VMEM((trees, side, 1) + block, jnp.float32),
            pltpu.VMEM((3, side, 8, 128), jnp.float32),
            pltpu.VMEM((2, 8, 128), jnp.float32),
            pltpu.SemaphoreType.DMA((32,)),
        ],
        compiler_params=pltpu.CompilerParams(collective_id=0, has_side_effects=True),
    )(pulled, stats, pos)


def shards(queue_keys, fresh_keys, slots, queries, positives):
    dp_size = lax.axis_size("dp")
    queue_size = lax.axis_size("queue")
    n = dp_size * queue_size
    assert fresh_keys.shape[0] == FRESH_HELD
    assert queue_size == (dp_size // 2) ** 2
    d = queries.shape[1]
    pos_code = jnp.zeros((queries.shape[0], STAT), jnp.bfloat16)
    pos_code = pos_code.at[:, 0].set((positives // 32).astype(jnp.bfloat16))
    pos_code = pos_code.at[:, 1].set((positives % 32).astype(jnp.bfloat16))
    digits = jnp.stack([slots // 16384, (slots // 128) % 128, slots % 128], axis=1)
    code = jnp.zeros((slots.shape[0], STAT), jnp.bfloat16).at[:, :3].set(digits.astype(jnp.bfloat16))
    gathered, fresh_ext = gather_dp(
        jnp.concatenate([queries, pos_code], axis=1),
        jnp.concatenate([fresh_keys, code], axis=1).astype(jnp.float32),
        dp_size // 2,
    )
    fresh_ext = fresh_ext.reshape(n * fresh_keys.shape[0], d + STAT)
    total_rows = dp_size * queries.shape[0]
    own_rows = total_rows // n
    gathered = gathered.reshape(total_rows, d + STAT)
    all_queries = gathered[:, :d]
    pos_digits = gathered[:, d:d + 2].astype(jnp.int32)
    all_positives = pos_digits[:, 0] * 32 + pos_digits[:, 1]
    fresh_all = fresh_ext[:, :d].astype(jnp.bfloat16)
    got = fresh_ext[:, d:d + 3].astype(jnp.int32)
    slots_all = got[:, 0] * 16384 + got[:, 1] * 128 + got[:, 2]

    device_index = _device_index()
    fresh_padded = jnp.zeros((STAT, d), fresh_keys.dtype).at[:fresh_keys.shape[0]].set(fresh_keys)
    local_pulled, stats = local_partials(gathered, queue_keys, fresh_padded, min(256, total_rows))
    fresh_scores = score_rows(all_queries, fresh_keys)
    fresh_ids = device_index * fresh_keys.shape[0] + jnp.arange(fresh_keys.shape[0], dtype=jnp.int32)
    is_positive = all_positives[:, None] == fresh_ids[None, :]
    positive_total = jnp.sum(jnp.where(is_positive, fresh_scores, 0.0))
    halves = (2, n // 2, own_rows)
    combined, loss_tile = combine(
        local_pulled.reshape(halves + (d,)),
        stats.reshape(halves + (STAT,)),
        jnp.full((8, 128), positive_total, jnp.float32),
        d,
        dp_size // 2,
    )
    sum_rows = combined[:, d + 1]
    pulled = combined[:, :d]
    queue_index = lax.axis_index("queue")
    local_start = queue_index * own_rows
    positive_rows = lax.dynamic_slice_in_dim(positives, local_start, own_rows, 0)
    positive_keys = jnp.take(fresh_all, positive_rows, axis=0).astype(jnp.float32)
    query_grad = pulled / sum_rows[:, None] - positive_keys
    mean_loss = loss_tile[0, 0] / total_rows
    held_rows = queue_keys.shape[0]
    local_slot = slots_all - device_index * held_rows
    picks = jnp.arange(held_rows, dtype=jnp.int32)[:, None] == local_slot[None, :]
    inserted = jnp.dot(picks.astype(jnp.bfloat16), fresh_all, preferred_element_type=jnp.float32)
    replaced = jnp.any(picks, axis=1)
    new_queue = jnp.where(replaced[:, None], inserted.astype(jnp.bfloat16), queue_keys)
    return (query_grad, mean_loss, new_queue)


def solution(mesh):
    placed = (
        P(("dp", "queue"), None),
        P(("dp", "queue"), None),
        P(("dp", "queue")),
        P("dp", None),
        P("dp"),
    )
    return jax.shard_map(
        shards,
        mesh=mesh,
        in_specs=placed,
        out_specs=(P(("dp", "queue"), None), P(), P(("dp", "queue"), None)),
        check_vma=False,
    )
```

```python
import functools

import jax
import jax.numpy as jnp
from jax import lax
from jax.experimental import pallas as pl
from jax.experimental.pallas import tpu as pltpu
from jax.sharding import PartitionSpec as P

MESH = pl.DeviceIdType.MESH
STAT = 128
FRESH_HELD = 8
KEY_CHUNK = 512


def score_rows(query_rows, key_rows):
    return lax.dot_general(
        query_rows, key_rows, (((1,), (1,)), ((), ())), preferred_element_type=jnp.float32
    )


def _device_index():
    return lax.axis_index("dp") * lax.axis_size("queue") + lax.axis_index("queue")


def _wait_bytes(src, dst, send_sem, recv_sem, device_id):
    total = pltpu.make_async_remote_copy(
        src_ref=src, dst_ref=dst, send_sem=send_sem, recv_sem=recv_sem,
        device_id=device_id, device_id_type=MESH,
    )
    total.wait_send()
    total.wait_recv()


def partial_kernel(q_ref, k_ref, f_ref, p_ref, s_ref):
    q = q_ref[:, :k_ref.shape[1]]
    dims = (((1,), (1,)), ((), ()))
    scores = lax.dot_general(q, k_ref[...], dims, preferred_element_type=jnp.float32)
    fresh = lax.dot_general(q, f_ref[...], dims, preferred_element_type=jnp.float32)
    held = lax.broadcasted_iota(jnp.int32, fresh.shape, 1) < FRESH_HELD
    fresh = jnp.where(held, fresh, -jnp.inf)
    top = jnp.maximum(jnp.max(scores, axis=1, keepdims=True), jnp.max(fresh, axis=1, keepdims=True))
    fresh_weights = jnp.exp(fresh - top)
    total = jnp.sum(fresh_weights, axis=1, keepdims=True)
    acc = jnp.dot(fresh_weights.astype(jnp.bfloat16), f_ref[...], preferred_element_type=jnp.float32)
    chunk = min(KEY_CHUNK, k_ref.shape[0])
    for j in range(k_ref.shape[0] // chunk):
        weights = jnp.exp(scores[:, j * chunk:(j + 1) * chunk] - top)
        total = total + jnp.sum(weights, axis=1, keepdims=True)
        acc = acc + jnp.dot(
            weights.astype(jnp.bfloat16), k_ref[j * chunk:(j + 1) * chunk, :],
            preferred_element_type=jnp.float32,
        )
    p_ref[...] = acc
    col = lax.broadcasted_iota(jnp.int32, s_ref.shape, 1)
    s_ref[...] = jnp.where(col == 0, top, jnp.where(col == 1, total, 0.0))


def local_partials(queries, keys, fresh_padded, block):
    rows, width = queries.shape
    d = keys.shape[1]
    return pl.pallas_call(
        partial_kernel,
        grid=(rows // block,),
        out_shape=(
            jax.ShapeDtypeStruct((rows, d), jnp.float32),
            jax.ShapeDtypeStruct((rows, STAT), jnp.float32),
        ),
        in_specs=[
            pl.BlockSpec((block, width), lambda i: (i, 0)),
            pl.BlockSpec(keys.shape, lambda i: (0, 0)),
            pl.BlockSpec(fresh_padded.shape, lambda i: (0, 0)),
        ],
        out_specs=(
            pl.BlockSpec((block, d), lambda i: (i, 0)),
            pl.BlockSpec((block, STAT), lambda i: (i, 0)),
        ),
        compiler_params=pltpu.CompilerParams(vmem_limit_bytes=60 * 1024 * 1024),
    )(queries, keys, fresh_padded)


def gather_kernel(x_ref, f_ref, o_ref, fo_ref, buf, fbuf, sems):
    dp = lax.axis_index("dp")
    y, c = dp // 2, lax.rem(dp, 2)
    ys = lax.axis_size("dp") // 2
    r = ys
    qi = lax.axis_index("queue")
    mine_at = {"y": y, "z": qi // r, "x": lax.rem(qi, r)}
    partner = (dp + 1 - 2 * c, qi)

    def along(axis, j):
        at = dict(mine_at)
        at[axis] = j
        return (at["y"] * 2 + c, at["z"] * r + at["x"])

    barrier = pltpu.get_barrier_semaphore()
    pl.semaphore_signal(barrier, inc=1, device_id=partner, device_id_type=MESH)
    for axis in ("y", "x", "z"):
        for k in range(1, r):
            pl.semaphore_signal(barrier, inc=1, device_id=along(axis, lax.rem(mine_at[axis] + k, r)),
                                device_id_type=MESH)
    pl.semaphore_wait(barrier, 1 + 3 * (r - 1))

    mine = pltpu.make_async_copy(x_ref, buf.at[c, y], sems.at[4])
    mine.start()
    first = [
        pltpu.make_async_remote_copy(
            src_ref=x_ref, dst_ref=buf.at[c, y], send_sem=sems.at[0], recv_sem=sems.at[1],
            device_id=dst, device_id_type=MESH,
        )
        for dst in [partner] + [along("y", lax.rem(y + k, ys)) for k in range(1, ys)]
    ]
    for copy in first:
        copy.start()

    yi, zi, xi = mine_at["y"], mine_at["z"], mine_at["x"]

    def fresh_round(i, axis, src, dst):
        for k in range(1, r):
            pltpu.make_async_remote_copy(
                src_ref=src, dst_ref=dst, send_sem=sems.at[6 + 2 * i], recv_sem=sems.at[7 + 2 * i],
                device_id=along(axis, lax.rem(mine_at[axis] + k, r)), device_id_type=MESH,
            ).start()

    own_fresh = pltpu.make_async_copy(f_ref, fbuf.at[c, xi, zi, yi], sems.at[5])
    own_fresh.start()
    fresh_round(0, "y", f_ref, fbuf.at[c, xi, zi, yi])
    own_fresh.wait()
    _wait_bytes(fbuf.at[0, 0, 0, pl.ds(0, r - 1)], fbuf.at[0, 0, 0, pl.ds(0, r - 1)],
                sems.at[6], sems.at[7], along("y", lax.rem(yi + 1, r)))
    fresh_round(1, "z", fbuf.at[c, xi, zi], fbuf.at[c, xi, zi])
    _wait_bytes(fbuf.at[0, 0, pl.ds(0, r - 1)], fbuf.at[0, 0, pl.ds(0, r - 1)],
                sems.at[8], sems.at[9], along("z", lax.rem(zi + 1, r)))
    fresh_round(2, "x", fbuf.at[c, xi], fbuf.at[c, xi])

    _wait_bytes(buf.at[0], buf.at[0], sems.at[0], sems.at[1], partner)
    mine.wait()
    second = [
        pltpu.make_async_remote_copy(
            src_ref=buf.at[c, lax.rem(y + k, ys)], dst_ref=buf.at[c, lax.rem(y + k, ys)],
            send_sem=sems.at[2], recv_sem=sems.at[3], device_id=partner, device_id_type=MESH,
        )
        for k in range(1, ys)
    ]
    for copy in second:
        copy.start()
    _wait_bytes(fbuf.at[0, pl.ds(0, r - 1)], fbuf.at[0, pl.ds(0, r - 1)],
                sems.at[10], sems.at[11], along("x", lax.rem(xi + 1, r)))
    pltpu.make_async_remote_copy(
        src_ref=fbuf.at[c], dst_ref=fbuf.at[c], send_sem=sems.at[12], recv_sem=sems.at[13],
        device_id=partner, device_id_type=MESH,
    ).start()
    _wait_bytes(buf.at[0, pl.ds(0, ys - 1)], buf.at[0, pl.ds(0, ys - 1)], sems.at[2], sems.at[3], partner)
    _wait_bytes(fbuf.at[0], fbuf.at[0], sems.at[12], sems.at[13], partner)
    o_ref[...] = buf[...]
    fo_ref[...] = fbuf[...]


def gather_dp(x, fresh, ys):
    return pl.pallas_call(
        gather_kernel,
        out_shape=(
            jax.ShapeDtypeStruct((2, ys) + x.shape, x.dtype),
            jax.ShapeDtypeStruct((2, ys, ys, ys) + fresh.shape, fresh.dtype),
        ),
        in_specs=[pl.BlockSpec(memory_space=pltpu.VMEM), pl.BlockSpec(memory_space=pltpu.VMEM)],
        out_specs=(pl.BlockSpec(memory_space=pltpu.VMEM), pl.BlockSpec(memory_space=pltpu.VMEM)),
        scratch_shapes=[
            pltpu.VMEM((2, ys) + x.shape, x.dtype),
            pltpu.VMEM((2, ys, ys, ys) + fresh.shape, fresh.dtype),
            pltpu.SemaphoreType.DMA((14,)),
        ],
        compiler_params=pltpu.CompilerParams(collective_id=1, has_side_effects=True),
    )(x, fresh)


def _merge(blocks, at):
    top = blocks[0][:, at:at + 1]
    for b in blocks[1:]:
        top = jnp.maximum(top, b[:, at:at + 1])
    acc = blocks[0] * jnp.exp(blocks[0][:, at:at + 1] - top)
    for b in blocks[1:]:
        acc = acc + b * jnp.exp(b[:, at:at + 1] - top)
    col = lax.broadcasted_iota(jnp.int32, acc.shape, 1)
    return jnp.where(col == at, top, acc)


TREES = (("x", "z", "y"), ("z", "y", "x"), ("y", "x", "z"))


def combine_kernel(d, side, p_ref, s_ref, pos_ref, o_ref, loss_ref, own_p, own_s, pair_p, pair_s,
                   send1, recv1, send2, recv2, send3, recv3, loss_buf, loss_pair, sems):
    r = side
    part = d // len(TREES)
    g = p_ref.shape[1]
    dp = lax.axis_index("dp")
    y, c = dp // 2, lax.rem(dp, 2)
    qi = lax.axis_index("queue")
    mine_at = {"y": y, "z": qi // r, "x": lax.rem(qi, r)}
    partner = (dp + 1 - 2 * c, qi)

    def device(at):
        return (at["y"] * 2 + c, at["z"] * r + at["x"])

    def along(axis, j):
        at = dict(mine_at)
        at[axis] = j
        return device(at)

    barrier = pltpu.get_barrier_semaphore()
    pl.semaphore_signal(barrier, inc=1, device_id=partner, device_id_type=MESH)
    for axis in ("x", "z", "y"):
        for k in range(1, r):
            pl.semaphore_signal(barrier, inc=1, device_id=along(axis, lax.rem(mine_at[axis] + k, r)),
                                device_id_type=MESH)
    pl.semaphore_wait(barrier, 1 + 3 * (r - 1))

    pair_copies = [
        pltpu.make_async_remote_copy(
            src_ref=src.at[1 - c], dst_ref=dst, send_sem=sems.at[2 * i], recv_sem=sems.at[2 * i + 1],
            device_id=partner, device_id_type=MESH,
        )
        for i, (src, dst) in enumerate(((p_ref, pair_p), (s_ref, pair_s)))
    ]
    for copy in pair_copies:
        copy.start()
    mine = [pltpu.make_async_copy(src.at[c], dst, sems.at[4 + i])
            for i, (src, dst) in enumerate(((p_ref, own_p), (s_ref, own_s)))]
    for copy in mine:
        copy.start()
    for copy in mine + pair_copies:
        copy.wait()

    def merge_pair(k, carry):
        a, b = own_s[k], pair_s[k]
        top = jnp.maximum(a[:, 0:1], b[:, 0:1])
        wa, wb = jnp.exp(a[:, 0:1] - top), jnp.exp(b[:, 0:1] - top)
        pulled = own_p[k] * wa + pair_p[k] * wb
        col = lax.broadcasted_iota(jnp.int32, a.shape, 1)
        stats = jnp.where(col == 0, top, a * wa + b * wb)
        at = {"y": k // (r * r), "z": lax.rem(k // r, r), "x": lax.rem(k, r)}
        for t, (a1, a2, a3) in enumerate(TREES):
            slot = at[a2] * r + at[a3]
            send1[t, at[a1], slot, :, :part] = pulled[:, t * part:(t + 1) * part]
            send1[t, at[a1], slot, :, part:] = stats
        return carry

    lax.fori_loop(0, g, merge_pair, 0)

    def level(lvl, send, recv, blocks):
        sent = []
        for t, axes in enumerate(TREES):
            axis = axes[lvl]
            me_a = mine_at[axis]
            for k in range(1, r):
                dst = lax.rem(me_a + k, r)
                copy = pltpu.make_async_remote_copy(
                    src_ref=send.at[t, pl.ds(dst * blocks, blocks)], dst_ref=recv.at[t, me_a],
                    send_sem=sems.at[6 + 2 * (3 * lvl + t)], recv_sem=sems.at[7 + 2 * (3 * lvl + t)],
                    device_id=along(axis, dst), device_id_type=MESH,
                )
                copy.start()
            recv[t, me_a] = send[t, pl.ds(me_a * blocks, blocks)]
            sent.append(axis)
        for t, axis in enumerate(sent):
            _wait_bytes(recv.at[t, pl.ds(0, r - 1)], recv.at[t, pl.ds(0, r - 1)],
                        sems.at[6 + 2 * (3 * lvl + t)], sems.at[7 + 2 * (3 * lvl + t)],
                        along(axis, lax.rem(mine_at[axis] + 1, r)))

    def run_level1():
        sent_axes = []
        for t, axes in enumerate(TREES):
            axis = axes[0]
            me_a = mine_at[axis]
            for k in range(1, r):
                dst = lax.rem(me_a + k, r)
                pltpu.make_async_remote_copy(
                    src_ref=send1.at[t, dst], dst_ref=recv1.at[t, me_a],
                    send_sem=sems.at[6 + 2 * t], recv_sem=sems.at[7 + 2 * t],
                    device_id=along(axis, dst), device_id_type=MESH,
                ).start()
            recv1[t, me_a] = send1[t, me_a]
            sent_axes.append(axis)
        for t, axis in enumerate(sent_axes):
            _wait_bytes(send1.at[t, pl.ds(0, r - 1)], recv1.at[t, pl.ds(0, r - 1)],
                        sems.at[6 + 2 * t], sems.at[7 + 2 * t],
                        along(axis, lax.rem(mine_at[axis] + 1, r)))

    run_level1()

    def merge1(b, carry):
        for t in range(len(TREES)):
            send2[t, b] = _merge([recv1[t, i, b] for i in range(r)], part)
        return carry

    lax.fori_loop(0, r * r, merge1, 0)
    level(1, send2, recv2, r)

    for t in range(len(TREES)):
        for a3 in range(r):
            send3[t, a3] = _merge([recv2[t, i, a3] for i in range(r)], part)
    level(2, send3, recv3, 1)

    finals = [_merge([recv3[t, i, 0] for i in range(r)], part) for t in range(len(TREES))]
    stats = finals[0][:, part:]
    for t in range(len(TREES)):
        o_ref[:, t * part:(t + 1) * part] = finals[t][:, :part]
    o_ref[:, d:] = stats
    top = stats[:, 0:1]
    sums = stats[:, 1:2]

    total = jnp.broadcast_to(jnp.sum(top + jnp.log(sums)) - pos_ref[0:1, 0:1], loss_ref.shape)
    for n_axis, axis in enumerate(("x", "z", "y")):
        me_a = mine_at[axis]
        loss_buf[n_axis, me_a] = total
        for k in range(1, r):
            dst = lax.rem(me_a + k, r)
            pltpu.make_async_remote_copy(
                src_ref=loss_buf.at[n_axis, me_a], dst_ref=loss_buf.at[n_axis, me_a],
                send_sem=sems.at[24 + 2 * n_axis], recv_sem=sems.at[25 + 2 * n_axis],
                device_id=along(axis, dst), device_id_type=MESH,
            ).start()
        _wait_bytes(loss_buf.at[n_axis, pl.ds(0, r - 1)], loss_buf.at[n_axis, pl.ds(0, r - 1)],
                    sems.at[24 + 2 * n_axis], sems.at[25 + 2 * n_axis],
                    along(axis, lax.rem(me_a + 1, r)))
        total = loss_buf[n_axis, 0]
        for i in range(1, r):
            total = total + loss_buf[n_axis, i]
    loss_pair[c] = total
    to_pair_loss = pltpu.make_async_remote_copy(
        src_ref=loss_pair.at[c], dst_ref=loss_pair.at[c], send_sem=sems.at[30], recv_sem=sems.at[31],
        device_id=partner, device_id_type=MESH,
    )
    to_pair_loss.start()
    to_pair_loss.wait()
    loss_ref[...] = loss_pair[0] + loss_pair[1]


def combine(pulled, stats, pos, d, side):
    g, rows = pulled.shape[1:3]
    width = d + stats.shape[3]
    trees = len(TREES)
    block = (rows, d // trees + STAT)
    return pl.pallas_call(
        functools.partial(combine_kernel, d, side),
        out_shape=(
            jax.ShapeDtypeStruct((rows, width), jnp.float32),
            jax.ShapeDtypeStruct((8, 128), jnp.float32),
        ),
        in_specs=[
            pl.BlockSpec(memory_space=pl.ANY),
            pl.BlockSpec(memory_space=pl.ANY),
            pl.BlockSpec(memory_space=pltpu.VMEM),
        ],
        out_specs=(
            pl.BlockSpec(memory_space=pltpu.VMEM),
            pl.BlockSpec(memory_space=pltpu.VMEM),
        ),
        scratch_shapes=[
            pltpu.VMEM((g, rows, d), jnp.float32),
            pltpu.VMEM((g, rows, width - d), jnp.float32),
            pltpu.VMEM((g, rows, d), jnp.float32),
            pltpu.VMEM((g, rows, width - d), jnp.float32),
            pltpu.VMEM((trees, side, side * side) + block, jnp.float32),
            pltpu.VMEM((trees, side, side * side) + block, jnp.float32),
            pltpu.VMEM((trees, side * side) + block, jnp.float32),
            pltpu.VMEM((trees, side, side) + block, jnp.float32),
            pltpu.VMEM((trees, side) + block, jnp.float32),
            pltpu.VMEM((trees, side, 1) + block, jnp.float32),
            pltpu.VMEM((3, side, 8, 128), jnp.float32),
            pltpu.VMEM((2, 8, 128), jnp.float32),
            pltpu.SemaphoreType.DMA((32,)),
        ],
        compiler_params=pltpu.CompilerParams(collective_id=0, has_side_effects=True),
    )(pulled, stats, pos)


def shards(queue_keys, fresh_keys, slots, queries, positives):
    dp_size = lax.axis_size("dp")
    queue_size = lax.axis_size("queue")
    n = dp_size * queue_size
    assert fresh_keys.shape[0] == FRESH_HELD
    assert queue_size == (dp_size // 2) ** 2
    d = queries.shape[1]
    pos_code = jnp.zeros((queries.shape[0], STAT), jnp.bfloat16)
    pos_code = pos_code.at[:, 0].set((positives // 32).astype(jnp.bfloat16))
    pos_code = pos_code.at[:, 1].set((positives % 32).astype(jnp.bfloat16))
    digits = jnp.stack([slots // 16384, (slots // 128) % 128, slots % 128], axis=1)
    code = jnp.zeros((slots.shape[0], STAT), jnp.bfloat16).at[:, :3].set(digits.astype(jnp.bfloat16))
    gathered, fresh_ext = gather_dp(
        jnp.concatenate([queries, pos_code], axis=1),
        jnp.concatenate([fresh_keys, code], axis=1),
        dp_size // 2,
    )
    fresh_ext = fresh_ext.transpose(3, 0, 2, 1, 4, 5).reshape(n * fresh_keys.shape[0], d + STAT)
    total_rows = dp_size * queries.shape[0]
    own_rows = total_rows // n
    gathered = gathered.reshape(total_rows, d + STAT)
    all_queries = gathered[:, :d]
    pos_digits = gathered[:, d:d + 2].astype(jnp.int32)
    all_positives = pos_digits[:, 0] * 32 + pos_digits[:, 1]
    fresh_all = fresh_ext[:, :d]
    got = fresh_ext[:, d:d + 3].astype(jnp.int32)
    slots_all = got[:, 0] * 16384 + got[:, 1] * 128 + got[:, 2]

    device_index = _device_index()
    fresh_padded = jnp.zeros((STAT, d), fresh_keys.dtype).at[:fresh_keys.shape[0]].set(fresh_keys)
    local_pulled, stats = local_partials(gathered, queue_keys, fresh_padded, min(256, total_rows))
    fresh_scores = score_rows(all_queries, fresh_keys)
    fresh_ids = device_index * fresh_keys.shape[0] + jnp.arange(fresh_keys.shape[0], dtype=jnp.int32)
    is_positive = all_positives[:, None] == fresh_ids[None, :]
    positive_total = jnp.sum(jnp.where(is_positive, fresh_scores, 0.0))
    halves = (2, n // 2, own_rows)
    combined, loss_tile = combine(
        local_pulled.reshape(halves + (d,)),
        stats.reshape(halves + (STAT,)),
        jnp.full((8, 128), positive_total, jnp.float32),
        d,
        dp_size // 2,
    )
    sum_rows = combined[:, d + 1]
    pulled = combined[:, :d]
    queue_index = lax.axis_index("queue")
    local_start = queue_index * own_rows
    positive_rows = lax.dynamic_slice_in_dim(positives, local_start, own_rows, 0)
    positive_keys = jnp.take(fresh_all, positive_rows, axis=0).astype(jnp.float32)
    query_grad = pulled / sum_rows[:, None] - positive_keys
    mean_loss = loss_tile[0, 0] / total_rows
    held_rows = queue_keys.shape[0]
    local_slot = slots_all - device_index * held_rows
    picks = jnp.arange(held_rows, dtype=jnp.int32)[:, None] == local_slot[None, :]
    inserted = jnp.dot(picks.astype(jnp.bfloat16), fresh_all, preferred_element_type=jnp.float32)
    replaced = jnp.any(picks, axis=1)
    new_queue = jnp.where(replaced[:, None], inserted.astype(jnp.bfloat16), queue_keys)
    return (query_grad, mean_loss, new_queue)


def solution(mesh):
    placed = (
        P(("dp", "queue"), None),
        P(("dp", "queue"), None),
        P(("dp", "queue")),
        P("dp", None),
        P("dp"),
    )
    return jax.shard_map(
        shards,
        mesh=mesh,
        in_specs=placed,
        out_specs=(P(("dp", "queue"), None), P(), P(("dp", "queue"), None)),
        check_vma=False,
    )
```

```python
import functools

import jax
import jax.numpy as jnp
from jax import lax
from jax.experimental import pallas as pl
from jax.experimental.pallas import tpu as pltpu
from jax.sharding import PartitionSpec as P

MESH = pl.DeviceIdType.MESH
STAT = 128
FRESH_HELD = 8
KEY_CHUNK = 512


def score_rows(query_rows, key_rows):
    return lax.dot_general(
        query_rows, key_rows, (((1,), (1,)), ((), ())), preferred_element_type=jnp.float32
    )


def _device_index():
    return lax.axis_index("dp") * lax.axis_size("queue") + lax.axis_index("queue")


def _wait_bytes(src, dst, send_sem, recv_sem, device_id):
    total = pltpu.make_async_remote_copy(
        src_ref=src, dst_ref=dst, send_sem=send_sem, recv_sem=recv_sem,
        device_id=device_id, device_id_type=MESH,
    )
    total.wait_send()
    total.wait_recv()


def partial_kernel(q_ref, k_ref, f_ref, p_ref, s_ref):
    q = q_ref[:, :k_ref.shape[1]]
    dims = (((1,), (1,)), ((), ()))
    scores = lax.dot_general(q, k_ref[...], dims, preferred_element_type=jnp.float32)
    fresh = lax.dot_general(q, f_ref[...], dims, preferred_element_type=jnp.float32)
    held = lax.broadcasted_iota(jnp.int32, fresh.shape, 1) < FRESH_HELD
    fresh = jnp.where(held, fresh, -jnp.inf)
    top = jnp.maximum(jnp.max(scores, axis=1, keepdims=True), jnp.max(fresh, axis=1, keepdims=True))
    fresh_weights = jnp.exp(fresh - top)
    total = jnp.sum(fresh_weights, axis=1, keepdims=True)
    acc = jnp.dot(fresh_weights.astype(jnp.bfloat16), f_ref[...], preferred_element_type=jnp.float32)
    chunk = min(KEY_CHUNK, k_ref.shape[0])
    for j in range(k_ref.shape[0] // chunk):
        weights = jnp.exp(scores[:, j * chunk:(j + 1) * chunk] - top)
        total = total + jnp.sum(weights, axis=1, keepdims=True)
        acc = acc + jnp.dot(
            weights.astype(jnp.bfloat16), k_ref[j * chunk:(j + 1) * chunk, :],
            preferred_element_type=jnp.float32,
        )
    p_ref[...] = acc
    col = lax.broadcasted_iota(jnp.int32, s_ref.shape, 1)
    s_ref[...] = jnp.where(col == 0, top, jnp.where(col == 1, total, 0.0))


def local_partials(queries, keys, fresh_padded, block):
    rows, width = queries.shape
    d = keys.shape[1]
    return pl.pallas_call(
        partial_kernel,
        grid=(rows // block,),
        out_shape=(
            jax.ShapeDtypeStruct((rows, d), jnp.float32),
            jax.ShapeDtypeStruct((rows, STAT), jnp.float32),
        ),
        in_specs=[
            pl.BlockSpec((block, width), lambda i: (i, 0)),
            pl.BlockSpec(keys.shape, lambda i: (0, 0)),
            pl.BlockSpec(fresh_padded.shape, lambda i: (0, 0)),
        ],
        out_specs=(
            pl.BlockSpec((block, d), lambda i: (i, 0)),
            pl.BlockSpec((block, STAT), lambda i: (i, 0)),
        ),
        compiler_params=pltpu.CompilerParams(vmem_limit_bytes=60 * 1024 * 1024),
    )(queries, keys, fresh_padded)


def gather_kernel(x_ref, f_ref, o_ref, fo_ref, buf, fbuf, sems):
    dp = lax.axis_index("dp")
    y, c = dp // 2, lax.rem(dp, 2)
    ys = lax.axis_size("dp") // 2
    r = ys
    qi = lax.axis_index("queue")
    mine_at = {"y": y, "z": qi // r, "x": lax.rem(qi, r)}
    partner = (dp + 1 - 2 * c, qi)

    def along(axis, j):
        at = dict(mine_at)
        at[axis] = j
        return (at["y"] * 2 + c, at["z"] * r + at["x"])

    barrier = pltpu.get_barrier_semaphore()
    pl.semaphore_signal(barrier, inc=1, device_id=partner, device_id_type=MESH)
    for axis in ("y", "x", "z"):
        for k in range(1, r):
            pl.semaphore_signal(barrier, inc=1, device_id=along(axis, lax.rem(mine_at[axis] + k, r)),
                                device_id_type=MESH)
    pl.semaphore_wait(barrier, 1 + 3 * (r - 1))

    mine = pltpu.make_async_copy(x_ref, buf.at[c, y], sems.at[4])
    mine.start()
    first = [
        pltpu.make_async_remote_copy(
            src_ref=x_ref, dst_ref=buf.at[c, y], send_sem=sems.at[0], recv_sem=sems.at[1],
            device_id=dst, device_id_type=MESH,
        )
        for dst in [partner] + [along("y", lax.rem(y + k, ys)) for k in range(1, ys)]
    ]
    for copy in first:
        copy.start()

    yi, zi, xi = mine_at["y"], mine_at["z"], mine_at["x"]

    def fresh_round(i, axis, src, dst):
        for k in range(1, r):
            pltpu.make_async_remote_copy(
                src_ref=src, dst_ref=dst, send_sem=sems.at[6 + 2 * i], recv_sem=sems.at[7 + 2 * i],
                device_id=along(axis, lax.rem(mine_at[axis] + k, r)), device_id_type=MESH,
            ).start()

    own_fresh = pltpu.make_async_copy(f_ref, fbuf.at[yi, c, zi, xi], sems.at[5])
    own_fresh.start()
    fresh_round(0, "x", f_ref, fbuf.at[yi, c, zi, xi])
    own_fresh.wait()
    _wait_bytes(fbuf.at[0, 0, 0, pl.ds(0, r - 1)], fbuf.at[0, 0, 0, pl.ds(0, r - 1)],
                sems.at[6], sems.at[7], along("x", lax.rem(xi + 1, r)))
    fresh_round(1, "z", fbuf.at[yi, c, zi], fbuf.at[yi, c, zi])
    _wait_bytes(fbuf.at[0, 0, pl.ds(0, r - 1)], fbuf.at[0, 0, pl.ds(0, r - 1)],
                sems.at[8], sems.at[9], along("z", lax.rem(zi + 1, r)))
    fresh_round(2, "y", fbuf.at[yi, c], fbuf.at[yi, c])

    _wait_bytes(buf.at[0], buf.at[0], sems.at[0], sems.at[1], partner)
    mine.wait()
    second = [
        pltpu.make_async_remote_copy(
            src_ref=buf.at[c, lax.rem(y + k, ys)], dst_ref=buf.at[c, lax.rem(y + k, ys)],
            send_sem=sems.at[2], recv_sem=sems.at[3], device_id=partner, device_id_type=MESH,
        )
        for k in range(1, ys)
    ]
    for copy in second:
        copy.start()
    _wait_bytes(fbuf.at[pl.ds(0, r - 1), 0], fbuf.at[pl.ds(0, r - 1), 0],
                sems.at[10], sems.at[11], along("y", lax.rem(yi + 1, r)))
    for j in range(r):
        pltpu.make_async_remote_copy(
            src_ref=fbuf.at[j, c], dst_ref=fbuf.at[j, c], send_sem=sems.at[12], recv_sem=sems.at[13],
            device_id=partner, device_id_type=MESH,
        ).start()
    _wait_bytes(buf.at[0, pl.ds(0, ys - 1)], buf.at[0, pl.ds(0, ys - 1)], sems.at[2], sems.at[3], partner)
    _wait_bytes(fbuf.at[:, 0], fbuf.at[:, 0], sems.at[12], sems.at[13], partner)
    o_ref[...] = buf[...]
    fo_ref[...] = fbuf[...]


def gather_dp(x, fresh, ys):
    return pl.pallas_call(
        gather_kernel,
        out_shape=(
            jax.ShapeDtypeStruct((2, ys) + x.shape, x.dtype),
            jax.ShapeDtypeStruct((ys, 2, ys, ys) + fresh.shape, fresh.dtype),
        ),
        in_specs=[pl.BlockSpec(memory_space=pltpu.VMEM), pl.BlockSpec(memory_space=pltpu.VMEM)],
        out_specs=(pl.BlockSpec(memory_space=pltpu.VMEM), pl.BlockSpec(memory_space=pltpu.VMEM)),
        scratch_shapes=[
            pltpu.VMEM((2, ys) + x.shape, x.dtype),
            pltpu.VMEM((ys, 2, ys, ys) + fresh.shape, fresh.dtype),
            pltpu.SemaphoreType.DMA((14,)),
        ],
        compiler_params=pltpu.CompilerParams(collective_id=1, has_side_effects=True),
    )(x, fresh)


def _merge(blocks, at):
    top = blocks[0][:, at:at + 1]
    for b in blocks[1:]:
        top = jnp.maximum(top, b[:, at:at + 1])
    acc = blocks[0] * jnp.exp(blocks[0][:, at:at + 1] - top)
    for b in blocks[1:]:
        acc = acc + b * jnp.exp(b[:, at:at + 1] - top)
    col = lax.broadcasted_iota(jnp.int32, acc.shape, 1)
    return jnp.where(col == at, top, acc)


TREES = (("x", "z", "y"), ("z", "y", "x"), ("y", "x", "z"))


def combine_kernel(d, side, p_ref, s_ref, pos_ref, o_ref, loss_ref, own_p, own_s, pair_p, pair_s,
                   send1, recv1, send2, recv2, send3, recv3, loss_buf, loss_pair, sems):
    r = side
    part = d // len(TREES)
    g = p_ref.shape[1]
    dp = lax.axis_index("dp")
    y, c = dp // 2, lax.rem(dp, 2)
    qi = lax.axis_index("queue")
    mine_at = {"y": y, "z": qi // r, "x": lax.rem(qi, r)}
    partner = (dp + 1 - 2 * c, qi)

    def device(at):
        return (at["y"] * 2 + c, at["z"] * r + at["x"])

    def along(axis, j):
        at = dict(mine_at)
        at[axis] = j
        return device(at)

    barrier = pltpu.get_barrier_semaphore()
    pl.semaphore_signal(barrier, inc=1, device_id=partner, device_id_type=MESH)
    for axis in ("x", "z", "y"):
        for k in range(1, r):
            pl.semaphore_signal(barrier, inc=1, device_id=along(axis, lax.rem(mine_at[axis] + k, r)),
                                device_id_type=MESH)
    pl.semaphore_wait(barrier, 1 + 3 * (r - 1))

    pair_copies = [
        pltpu.make_async_remote_copy(
            src_ref=src.at[1 - c], dst_ref=dst, send_sem=sems.at[2 * i], recv_sem=sems.at[2 * i + 1],
            device_id=partner, device_id_type=MESH,
        )
        for i, (src, dst) in enumerate(((p_ref, pair_p), (s_ref, pair_s)))
    ]
    for copy in pair_copies:
        copy.start()
    mine = [pltpu.make_async_copy(src.at[c], dst, sems.at[4 + i])
            for i, (src, dst) in enumerate(((p_ref, own_p), (s_ref, own_s)))]
    for copy in mine:
        copy.start()
    for copy in mine + pair_copies:
        copy.wait()

    def merge_pair(k, carry):
        a, b = own_s[k], pair_s[k]
        top = jnp.maximum(a[:, 0:1], b[:, 0:1])
        wa, wb = jnp.exp(a[:, 0:1] - top), jnp.exp(b[:, 0:1] - top)
        pulled = own_p[k] * wa + pair_p[k] * wb
        col = lax.broadcasted_iota(jnp.int32, a.shape, 1)
        stats = jnp.where(col == 0, top, a * wa + b * wb)
        at = {"y": k // (r * r), "z": lax.rem(k // r, r), "x": lax.rem(k, r)}
        for t, (a1, a2, a3) in enumerate(TREES):
            slot = at[a2] * r + at[a3]
            send1[t, at[a1], slot, :, :part] = pulled[:, t * part:(t + 1) * part]
            send1[t, at[a1], slot, :, part:] = stats
        return carry

    lax.fori_loop(0, g, merge_pair, 0)

    def level(lvl, send, recv, blocks):
        sent = []
        for t, axes in enumerate(TREES):
            axis = axes[lvl]
            me_a = mine_at[axis]
            for k in range(1, r):
                dst = lax.rem(me_a + k, r)
                copy = pltpu.make_async_remote_copy(
                    src_ref=send.at[t, pl.ds(dst * blocks, blocks)], dst_ref=recv.at[t, me_a],
                    send_sem=sems.at[6 + 2 * (3 * lvl + t)], recv_sem=sems.at[7 + 2 * (3 * lvl + t)],
                    device_id=along(axis, dst), device_id_type=MESH,
                )
                copy.start()
            recv[t, me_a] = send[t, pl.ds(me_a * blocks, blocks)]
            sent.append(axis)
        for t, axis in enumerate(sent):
            _wait_bytes(recv.at[t, pl.ds(0, r - 1)], recv.at[t, pl.ds(0, r - 1)],
                        sems.at[6 + 2 * (3 * lvl + t)], sems.at[7 + 2 * (3 * lvl + t)],
                        along(axis, lax.rem(mine_at[axis] + 1, r)))

    def run_level1():
        sent_axes = []
        for t, axes in enumerate(TREES):
            axis = axes[0]
            me_a = mine_at[axis]
            for k in range(1, r):
                dst = lax.rem(me_a + k, r)
                pltpu.make_async_remote_copy(
                    src_ref=send1.at[t, dst], dst_ref=recv1.at[t, me_a],
                    send_sem=sems.at[6 + 2 * t], recv_sem=sems.at[7 + 2 * t],
                    device_id=along(axis, dst), device_id_type=MESH,
                ).start()
            recv1[t, me_a] = send1[t, me_a]
            sent_axes.append(axis)
        for t, axis in enumerate(sent_axes):
            _wait_bytes(send1.at[t, pl.ds(0, r - 1)], recv1.at[t, pl.ds(0, r - 1)],
                        sems.at[6 + 2 * t], sems.at[7 + 2 * t],
                        along(axis, lax.rem(mine_at[axis] + 1, r)))

    run_level1()

    def merge1(b, carry):
        for t in range(len(TREES)):
            send2[t, b] = _merge([recv1[t, i, b] for i in range(r)], part)
        return carry

    lax.fori_loop(0, r * r, merge1, 0)
    level(1, send2, recv2, r)

    for t in range(len(TREES)):
        for a3 in range(r):
            send3[t, a3] = _merge([recv2[t, i, a3] for i in range(r)], part)
    level(2, send3, recv3, 1)

    finals = [_merge([recv3[t, i, 0] for i in range(r)], part) for t in range(len(TREES))]
    stats = finals[0][:, part:]
    for t in range(len(TREES)):
        o_ref[:, t * part:(t + 1) * part] = finals[t][:, :part]
    o_ref[:, d:] = stats
    top = stats[:, 0:1]
    sums = stats[:, 1:2]

    total = jnp.broadcast_to(jnp.sum(top + jnp.log(sums)) - pos_ref[0:1, 0:1], loss_ref.shape)
    for n_axis, axis in enumerate(("x", "z", "y")):
        me_a = mine_at[axis]
        loss_buf[n_axis, me_a] = total
        for k in range(1, r):
            dst = lax.rem(me_a + k, r)
            pltpu.make_async_remote_copy(
                src_ref=loss_buf.at[n_axis, me_a], dst_ref=loss_buf.at[n_axis, me_a],
                send_sem=sems.at[24 + 2 * n_axis], recv_sem=sems.at[25 + 2 * n_axis],
                device_id=along(axis, dst), device_id_type=MESH,
            ).start()
        _wait_bytes(loss_buf.at[n_axis, pl.ds(0, r - 1)], loss_buf.at[n_axis, pl.ds(0, r - 1)],
                    sems.at[24 + 2 * n_axis], sems.at[25 + 2 * n_axis],
                    along(axis, lax.rem(me_a + 1, r)))
        total = loss_buf[n_axis, 0]
        for i in range(1, r):
            total = total + loss_buf[n_axis, i]
    loss_pair[c] = total
    to_pair_loss = pltpu.make_async_remote_copy(
        src_ref=loss_pair.at[c], dst_ref=loss_pair.at[c], send_sem=sems.at[30], recv_sem=sems.at[31],
        device_id=partner, device_id_type=MESH,
    )
    to_pair_loss.start()
    to_pair_loss.wait()
    loss_ref[...] = loss_pair[0] + loss_pair[1]


def combine(pulled, stats, pos, d, side):
    g, rows = pulled.shape[1:3]
    width = d + stats.shape[3]
    trees = len(TREES)
    block = (rows, d // trees + STAT)
    return pl.pallas_call(
        functools.partial(combine_kernel, d, side),
        out_shape=(
            jax.ShapeDtypeStruct((rows, width), jnp.float32),
            jax.ShapeDtypeStruct((8, 128), jnp.float32),
        ),
        in_specs=[
            pl.BlockSpec(memory_space=pl.ANY),
            pl.BlockSpec(memory_space=pl.ANY),
            pl.BlockSpec(memory_space=pltpu.VMEM),
        ],
        out_specs=(
            pl.BlockSpec(memory_space=pltpu.VMEM),
            pl.BlockSpec(memory_space=pltpu.VMEM),
        ),
        scratch_shapes=[
            pltpu.VMEM((g, rows, d), jnp.float32),
            pltpu.VMEM((g, rows, width - d), jnp.float32),
            pltpu.VMEM((g, rows, d), jnp.float32),
            pltpu.VMEM((g, rows, width - d), jnp.float32),
            pltpu.VMEM((trees, side, side * side) + block, jnp.float32),
            pltpu.VMEM((trees, side, side * side) + block, jnp.float32),
            pltpu.VMEM((trees, side * side) + block, jnp.float32),
            pltpu.VMEM((trees, side, side) + block, jnp.float32),
            pltpu.VMEM((trees, side) + block, jnp.float32),
            pltpu.VMEM((trees, side, 1) + block, jnp.float32),
            pltpu.VMEM((3, side, 8, 128), jnp.float32),
            pltpu.VMEM((2, 8, 128), jnp.float32),
            pltpu.SemaphoreType.DMA((32,)),
        ],
        compiler_params=pltpu.CompilerParams(collective_id=0, has_side_effects=True),
    )(pulled, stats, pos)


def shards(queue_keys, fresh_keys, slots, queries, positives):
    dp_size = lax.axis_size("dp")
    queue_size = lax.axis_size("queue")
    n = dp_size * queue_size
    assert fresh_keys.shape[0] == FRESH_HELD
    assert queue_size == (dp_size // 2) ** 2
    d = queries.shape[1]
    pos_code = jnp.zeros((queries.shape[0], STAT), jnp.bfloat16)
    pos_code = pos_code.at[:, 0].set((positives // 32).astype(jnp.bfloat16))
    pos_code = pos_code.at[:, 1].set((positives % 32).astype(jnp.bfloat16))
    digits = jnp.stack([slots // 16384, (slots // 128) % 128, slots % 128], axis=1)
    code = jnp.zeros((slots.shape[0], STAT), jnp.bfloat16).at[:, :3].set(digits.astype(jnp.bfloat16))
    gathered, fresh_ext = gather_dp(
        jnp.concatenate([queries, pos_code], axis=1),
        jnp.concatenate([fresh_keys, code], axis=1),
        dp_size // 2,
    )
    fresh_ext = fresh_ext.reshape(n * fresh_keys.shape[0], d + STAT)
    total_rows = dp_size * queries.shape[0]
    own_rows = total_rows // n
    gathered = gathered.reshape(total_rows, d + STAT)
    all_queries = gathered[:, :d]
    pos_digits = gathered[:, d:d + 2].astype(jnp.int32)
    all_positives = pos_digits[:, 0] * 32 + pos_digits[:, 1]
    fresh_all = fresh_ext[:, :d]
    got = fresh_ext[:, d:d + 3].astype(jnp.int32)
    slots_all = got[:, 0] * 16384 + got[:, 1] * 128 + got[:, 2]

    device_index = _device_index()
    fresh_padded = jnp.zeros((STAT, d), fresh_keys.dtype).at[:fresh_keys.shape[0]].set(fresh_keys)
    local_pulled, stats = local_partials(gathered, queue_keys, fresh_padded, min(256, total_rows))
    fresh_scores = score_rows(all_queries, fresh_keys)
    fresh_ids = device_index * fresh_keys.shape[0] + jnp.arange(fresh_keys.shape[0], dtype=jnp.int32)
    is_positive = all_positives[:, None] == fresh_ids[None, :]
    positive_total = jnp.sum(jnp.where(is_positive, fresh_scores, 0.0))
    halves = (2, n // 2, own_rows)
    combined, loss_tile = combine(
        local_pulled.reshape(halves + (d,)),
        stats.reshape(halves + (STAT,)),
        jnp.full((8, 128), positive_total, jnp.float32),
        d,
        dp_size // 2,
    )
    sum_rows = combined[:, d + 1]
    pulled = combined[:, :d]
    queue_index = lax.axis_index("queue")
    local_start = queue_index * own_rows
    positive_rows = lax.dynamic_slice_in_dim(positives, local_start, own_rows, 0)
    positive_keys = jnp.take(fresh_all, positive_rows, axis=0).astype(jnp.float32)
    query_grad = pulled / sum_rows[:, None] - positive_keys
    mean_loss = loss_tile[0, 0] / total_rows
    held_rows = queue_keys.shape[0]
    local_slot = slots_all - device_index * held_rows
    inside = (local_slot >= 0) & (local_slot < held_rows)
    spare = held_rows + jnp.arange(local_slot.shape[0], dtype=jnp.int32)
    target = jnp.where(inside, local_slot, spare)
    new_queue = queue_keys.at[target].set(fresh_all, mode="drop", unique_indices=True)
    return (query_grad, mean_loss, new_queue)


def solution(mesh):
    placed = (
        P(("dp", "queue"), None),
        P(("dp", "queue"), None),
        P(("dp", "queue")),
        P("dp", None),
        P("dp"),
    )
    return jax.shard_map(
        shards,
        mesh=mesh,
        in_specs=placed,
        out_specs=(P(("dp", "queue"), None), P(), P(("dp", "queue"), None)),
        check_vma=False,
    )
```

```python
import functools

import jax
import jax.numpy as jnp
from jax import lax
from jax.experimental import pallas as pl
from jax.experimental.pallas import tpu as pltpu
from jax.sharding import PartitionSpec as P

MESH = pl.DeviceIdType.MESH
STAT = 128
FRESH_HELD = 8
KEY_CHUNK = 1024


def score_rows(query_rows, key_rows):
    return lax.dot_general(
        query_rows, key_rows, (((1,), (1,)), ((), ())), preferred_element_type=jnp.float32
    )


def _device_index():
    return lax.axis_index("dp") * lax.axis_size("queue") + lax.axis_index("queue")


def _wait_bytes(src, dst, send_sem, recv_sem, device_id):
    total = pltpu.make_async_remote_copy(
        src_ref=src, dst_ref=dst, send_sem=send_sem, recv_sem=recv_sem,
        device_id=device_id, device_id_type=MESH,
    )
    total.wait_send()
    total.wait_recv()


def partial_kernel(q_ref, k_ref, f_ref, p_ref, s_ref):
    q = q_ref[:, :k_ref.shape[1]]
    dims = (((1,), (1,)), ((), ()))
    scores = lax.dot_general(q, k_ref[...], dims, preferred_element_type=jnp.float32)
    fresh = lax.dot_general(q, f_ref[...], dims, preferred_element_type=jnp.float32)
    held = lax.broadcasted_iota(jnp.int32, fresh.shape, 1) < FRESH_HELD
    fresh = jnp.where(held, fresh, -jnp.inf)
    top = jnp.maximum(jnp.max(scores, axis=1, keepdims=True), jnp.max(fresh, axis=1, keepdims=True))
    fresh_weights = jnp.exp(fresh - top)
    total = jnp.sum(fresh_weights, axis=1, keepdims=True)
    acc = jnp.dot(fresh_weights.astype(jnp.bfloat16), f_ref[...], preferred_element_type=jnp.float32)
    chunk = min(KEY_CHUNK, k_ref.shape[0])
    for j in range(k_ref.shape[0] // chunk):
        weights = jnp.exp(scores[:, j * chunk:(j + 1) * chunk] - top)
        total = total + jnp.sum(weights, axis=1, keepdims=True)
        acc = acc + jnp.dot(
            weights.astype(jnp.bfloat16), k_ref[j * chunk:(j + 1) * chunk, :],
            preferred_element_type=jnp.float32,
        )
    p_ref[...] = acc
    col = lax.broadcasted_iota(jnp.int32, s_ref.shape, 1)
    s_ref[...] = jnp.where(col == 0, top, jnp.where(col == 1, total, 0.0))


def local_partials(queries, keys, fresh_padded, block):
    rows, width = queries.shape
    d = keys.shape[1]
    return pl.pallas_call(
        partial_kernel,
        grid=(rows // block,),
        out_shape=(
            jax.ShapeDtypeStruct((rows, d), jnp.float32),
            jax.ShapeDtypeStruct((rows, STAT), jnp.float32),
        ),
        in_specs=[
            pl.BlockSpec((block, width), lambda i: (i, 0)),
            pl.BlockSpec(keys.shape, lambda i: (0, 0)),
            pl.BlockSpec(fresh_padded.shape, lambda i: (0, 0)),
        ],
        out_specs=(
            pl.BlockSpec((block, d), lambda i: (i, 0)),
            pl.BlockSpec((block, STAT), lambda i: (i, 0)),
        ),
        compiler_params=pltpu.CompilerParams(vmem_limit_bytes=60 * 1024 * 1024),
    )(queries, keys, fresh_padded)


def gather_kernel(x_ref, f_ref, o_ref, fo_ref, buf, fbuf, sems):
    dp = lax.axis_index("dp")
    y, c = dp // 2, lax.rem(dp, 2)
    ys = lax.axis_size("dp") // 2
    r = ys
    qi = lax.axis_index("queue")
    mine_at = {"y": y, "z": qi // r, "x": lax.rem(qi, r)}
    partner = (dp + 1 - 2 * c, qi)

    def along(axis, j):
        at = dict(mine_at)
        at[axis] = j
        return (at["y"] * 2 + c, at["z"] * r + at["x"])

    barrier = pltpu.get_barrier_semaphore()
    pl.semaphore_signal(barrier, inc=1, device_id=partner, device_id_type=MESH)
    for axis in ("y", "x", "z"):
        for k in range(1, r):
            pl.semaphore_signal(barrier, inc=1, device_id=along(axis, lax.rem(mine_at[axis] + k, r)),
                                device_id_type=MESH)
    pl.semaphore_wait(barrier, 1 + 3 * (r - 1))

    mine = pltpu.make_async_copy(x_ref, buf.at[c, y], sems.at[4])
    mine.start()
    first = [
        pltpu.make_async_remote_copy(
            src_ref=x_ref, dst_ref=buf.at[c, y], send_sem=sems.at[0], recv_sem=sems.at[1],
            device_id=dst, device_id_type=MESH,
        )
        for dst in [partner] + [along("y", lax.rem(y + k, ys)) for k in range(1, ys)]
    ]
    for copy in first:
        copy.start()

    yi, zi, xi = mine_at["y"], mine_at["z"], mine_at["x"]

    def fresh_round(i, axis, src, dst):
        for k in range(1, r):
            pltpu.make_async_remote_copy(
                src_ref=src, dst_ref=dst, send_sem=sems.at[6 + 2 * i], recv_sem=sems.at[7 + 2 * i],
                device_id=along(axis, lax.rem(mine_at[axis] + k, r)), device_id_type=MESH,
            ).start()

    own_fresh = pltpu.make_async_copy(f_ref, fbuf.at[yi, c, zi, xi], sems.at[5])
    own_fresh.start()
    fresh_round(0, "x", f_ref, fbuf.at[yi, c, zi, xi])
    own_fresh.wait()
    _wait_bytes(fbuf.at[0, 0, 0, pl.ds(0, r - 1)], fbuf.at[0, 0, 0, pl.ds(0, r - 1)],
                sems.at[6], sems.at[7], along("x", lax.rem(xi + 1, r)))
    fresh_round(1, "z", fbuf.at[yi, c, zi], fbuf.at[yi, c, zi])
    _wait_bytes(fbuf.at[0, 0, pl.ds(0, r - 1)], fbuf.at[0, 0, pl.ds(0, r - 1)],
                sems.at[8], sems.at[9], along("z", lax.rem(zi + 1, r)))
    fresh_round(2, "y", fbuf.at[yi, c], fbuf.at[yi, c])

    _wait_bytes(buf.at[0], buf.at[0], sems.at[0], sems.at[1], partner)
    mine.wait()
    second = [
        pltpu.make_async_remote_copy(
            src_ref=buf.at[c, lax.rem(y + k, ys)], dst_ref=buf.at[c, lax.rem(y + k, ys)],
            send_sem=sems.at[2], recv_sem=sems.at[3], device_id=partner, device_id_type=MESH,
        )
        for k in range(1, ys)
    ]
    for copy in second:
        copy.start()
    _wait_bytes(fbuf.at[pl.ds(0, r - 1), 0], fbuf.at[pl.ds(0, r - 1), 0],
                sems.at[10], sems.at[11], along("y", lax.rem(yi + 1, r)))
    for j in range(r):
        pltpu.make_async_remote_copy(
            src_ref=fbuf.at[j, c], dst_ref=fbuf.at[j, c], send_sem=sems.at[12], recv_sem=sems.at[13],
            device_id=partner, device_id_type=MESH,
        ).start()
    _wait_bytes(buf.at[0, pl.ds(0, ys - 1)], buf.at[0, pl.ds(0, ys - 1)], sems.at[2], sems.at[3], partner)
    _wait_bytes(fbuf.at[:, 0], fbuf.at[:, 0], sems.at[12], sems.at[13], partner)
    o_ref[...] = buf[...]
    fo_ref[...] = fbuf[...]


def gather_dp(x, fresh, ys):
    return pl.pallas_call(
        gather_kernel,
        out_shape=(
            jax.ShapeDtypeStruct((2, ys) + x.shape, x.dtype),
            jax.ShapeDtypeStruct((ys, 2, ys, ys) + fresh.shape, fresh.dtype),
        ),
        in_specs=[pl.BlockSpec(memory_space=pltpu.VMEM), pl.BlockSpec(memory_space=pltpu.VMEM)],
        out_specs=(pl.BlockSpec(memory_space=pltpu.VMEM), pl.BlockSpec(memory_space=pltpu.VMEM)),
        scratch_shapes=[
            pltpu.VMEM((2, ys) + x.shape, x.dtype),
            pltpu.VMEM((ys, 2, ys, ys) + fresh.shape, fresh.dtype),
            pltpu.SemaphoreType.DMA((14,)),
        ],
        compiler_params=pltpu.CompilerParams(collective_id=1, has_side_effects=True),
    )(x, fresh)


def _merge(blocks, at):
    top = blocks[0][:, at:at + 1]
    for b in blocks[1:]:
        top = jnp.maximum(top, b[:, at:at + 1])
    acc = blocks[0] * jnp.exp(blocks[0][:, at:at + 1] - top)
    for b in blocks[1:]:
        acc = acc + b * jnp.exp(b[:, at:at + 1] - top)
    col = lax.broadcasted_iota(jnp.int32, acc.shape, 1)
    return jnp.where(col == at, top, acc)


TREES = (("x", "z", "y"), ("z", "y", "x"), ("y", "x", "z"))


def combine_kernel(d, side, p_ref, s_ref, pos_ref, o_ref, loss_ref, own_p, own_s, pair_p, pair_s,
                   send1, recv1, send2, recv2, send3, recv3, loss_buf, loss_pair, sems):
    r = side
    part = d // len(TREES)
    g = p_ref.shape[1]
    dp = lax.axis_index("dp")
    y, c = dp // 2, lax.rem(dp, 2)
    qi = lax.axis_index("queue")
    mine_at = {"y": y, "z": qi // r, "x": lax.rem(qi, r)}
    partner = (dp + 1 - 2 * c, qi)

    def device(at):
        return (at["y"] * 2 + c, at["z"] * r + at["x"])

    def along(axis, j):
        at = dict(mine_at)
        at[axis] = j
        return device(at)

    barrier = pltpu.get_barrier_semaphore()
    pl.semaphore_signal(barrier, inc=1, device_id=partner, device_id_type=MESH)
    for axis in ("x", "z", "y"):
        for k in range(1, r):
            pl.semaphore_signal(barrier, inc=1, device_id=along(axis, lax.rem(mine_at[axis] + k, r)),
                                device_id_type=MESH)
    pl.semaphore_wait(barrier, 1 + 3 * (r - 1))

    pair_copies = [
        pltpu.make_async_remote_copy(
            src_ref=src.at[1 - c], dst_ref=dst, send_sem=sems.at[2 * i], recv_sem=sems.at[2 * i + 1],
            device_id=partner, device_id_type=MESH,
        )
        for i, (src, dst) in enumerate(((p_ref, pair_p), (s_ref, pair_s)))
    ]
    for copy in pair_copies:
        copy.start()
    mine = [pltpu.make_async_copy(src.at[c], dst, sems.at[4 + i])
            for i, (src, dst) in enumerate(((p_ref, own_p), (s_ref, own_s)))]
    for copy in mine:
        copy.start()
    for copy in mine + pair_copies:
        copy.wait()

    def merge_pair(k, carry):
        a, b = own_s[k], pair_s[k]
        top = jnp.maximum(a[:, 0:1], b[:, 0:1])
        wa, wb = jnp.exp(a[:, 0:1] - top), jnp.exp(b[:, 0:1] - top)
        pulled = own_p[k] * wa + pair_p[k] * wb
        col = lax.broadcasted_iota(jnp.int32, a.shape, 1)
        stats = jnp.where(col == 0, top, a * wa + b * wb)
        at = {"y": k // (r * r), "z": lax.rem(k // r, r), "x": lax.rem(k, r)}
        for t, (a1, a2, a3) in enumerate(TREES):
            slot = at[a2] * r + at[a3]
            send1[t, at[a1], slot, :, :part] = pulled[:, t * part:(t + 1) * part]
            send1[t, at[a1], slot, :, part:] = stats
        return carry

    lax.fori_loop(0, g, merge_pair, 0)

    def level(lvl, send, recv, blocks):
        sent = []
        for t, axes in enumerate(TREES):
            axis = axes[lvl]
            me_a = mine_at[axis]
            for k in range(1, r):
                dst = lax.rem(me_a + k, r)
                copy = pltpu.make_async_remote_copy(
                    src_ref=send.at[t, pl.ds(dst * blocks, blocks)], dst_ref=recv.at[t, me_a],
                    send_sem=sems.at[6 + 2 * (3 * lvl + t)], recv_sem=sems.at[7 + 2 * (3 * lvl + t)],
                    device_id=along(axis, dst), device_id_type=MESH,
                )
                copy.start()
            recv[t, me_a] = send[t, pl.ds(me_a * blocks, blocks)]
            sent.append(axis)
        for t, axis in enumerate(sent):
            _wait_bytes(recv.at[t, pl.ds(0, r - 1)], recv.at[t, pl.ds(0, r - 1)],
                        sems.at[6 + 2 * (3 * lvl + t)], sems.at[7 + 2 * (3 * lvl + t)],
                        along(axis, lax.rem(mine_at[axis] + 1, r)))

    def run_level1():
        sent_axes = []
        for t, axes in enumerate(TREES):
            axis = axes[0]
            me_a = mine_at[axis]
            for k in range(1, r):
                dst = lax.rem(me_a + k, r)
                pltpu.make_async_remote_copy(
                    src_ref=send1.at[t, dst], dst_ref=recv1.at[t, me_a],
                    send_sem=sems.at[6 + 2 * t], recv_sem=sems.at[7 + 2 * t],
                    device_id=along(axis, dst), device_id_type=MESH,
                ).start()
            recv1[t, me_a] = send1[t, me_a]
            sent_axes.append(axis)
        for t, axis in enumerate(sent_axes):
            _wait_bytes(send1.at[t, pl.ds(0, r - 1)], recv1.at[t, pl.ds(0, r - 1)],
                        sems.at[6 + 2 * t], sems.at[7 + 2 * t],
                        along(axis, lax.rem(mine_at[axis] + 1, r)))

    run_level1()

    def merge1(b, carry):
        for t in range(len(TREES)):
            send2[t, b] = _merge([recv1[t, i, b] for i in range(r)], part)
        return carry

    lax.fori_loop(0, r * r, merge1, 0)
    level(1, send2, recv2, r)

    for t in range(len(TREES)):
        for a3 in range(r):
            send3[t, a3] = _merge([recv2[t, i, a3] for i in range(r)], part)
    level(2, send3, recv3, 1)

    finals = [_merge([recv3[t, i, 0] for i in range(r)], part) for t in range(len(TREES))]
    stats = finals[0][:, part:]
    for t in range(len(TREES)):
        o_ref[:, t * part:(t + 1) * part] = finals[t][:, :part]
    o_ref[:, d:] = stats
    top = stats[:, 0:1]
    sums = stats[:, 1:2]

    total = jnp.broadcast_to(jnp.sum(top + jnp.log(sums)) - pos_ref[0:1, 0:1], loss_ref.shape)
    for n_axis, axis in enumerate(("x", "z", "y")):
        me_a = mine_at[axis]
        loss_buf[n_axis, me_a] = total
        for k in range(1, r):
            dst = lax.rem(me_a + k, r)
            pltpu.make_async_remote_copy(
                src_ref=loss_buf.at[n_axis, me_a], dst_ref=loss_buf.at[n_axis, me_a],
                send_sem=sems.at[24 + 2 * n_axis], recv_sem=sems.at[25 + 2 * n_axis],
                device_id=along(axis, dst), device_id_type=MESH,
            ).start()
        _wait_bytes(loss_buf.at[n_axis, pl.ds(0, r - 1)], loss_buf.at[n_axis, pl.ds(0, r - 1)],
                    sems.at[24 + 2 * n_axis], sems.at[25 + 2 * n_axis],
                    along(axis, lax.rem(me_a + 1, r)))
        total = loss_buf[n_axis, 0]
        for i in range(1, r):
            total = total + loss_buf[n_axis, i]
    loss_pair[c] = total
    to_pair_loss = pltpu.make_async_remote_copy(
        src_ref=loss_pair.at[c], dst_ref=loss_pair.at[c], send_sem=sems.at[30], recv_sem=sems.at[31],
        device_id=partner, device_id_type=MESH,
    )
    to_pair_loss.start()
    to_pair_loss.wait()
    loss_ref[...] = loss_pair[0] + loss_pair[1]


def combine(pulled, stats, pos, d, side):
    g, rows = pulled.shape[1:3]
    width = d + stats.shape[3]
    trees = len(TREES)
    block = (rows, d // trees + STAT)
    return pl.pallas_call(
        functools.partial(combine_kernel, d, side),
        out_shape=(
            jax.ShapeDtypeStruct((rows, width), jnp.float32),
            jax.ShapeDtypeStruct((8, 128), jnp.float32),
        ),
        in_specs=[
            pl.BlockSpec(memory_space=pl.ANY),
            pl.BlockSpec(memory_space=pl.ANY),
            pl.BlockSpec(memory_space=pltpu.VMEM),
        ],
        out_specs=(
            pl.BlockSpec(memory_space=pltpu.VMEM),
            pl.BlockSpec(memory_space=pltpu.VMEM),
        ),
        scratch_shapes=[
            pltpu.VMEM((g, rows, d), jnp.float32),
            pltpu.VMEM((g, rows, width - d), jnp.float32),
            pltpu.VMEM((g, rows, d), jnp.float32),
            pltpu.VMEM((g, rows, width - d), jnp.float32),
            pltpu.VMEM((trees, side, side * side) + block, jnp.float32),
            pltpu.VMEM((trees, side, side * side) + block, jnp.float32),
            pltpu.VMEM((trees, side * side) + block, jnp.float32),
            pltpu.VMEM((trees, side, side) + block, jnp.float32),
            pltpu.VMEM((trees, side) + block, jnp.float32),
            pltpu.VMEM((trees, side, 1) + block, jnp.float32),
            pltpu.VMEM((3, side, 8, 128), jnp.float32),
            pltpu.VMEM((2, 8, 128), jnp.float32),
            pltpu.SemaphoreType.DMA((32,)),
        ],
        compiler_params=pltpu.CompilerParams(collective_id=0, has_side_effects=True),
    )(pulled, stats, pos)


def shards(queue_keys, fresh_keys, slots, queries, positives):
    dp_size = lax.axis_size("dp")
    queue_size = lax.axis_size("queue")
    n = dp_size * queue_size
    assert fresh_keys.shape[0] == FRESH_HELD
    assert queue_size == (dp_size // 2) ** 2
    d = queries.shape[1]
    pos_code = jnp.zeros((queries.shape[0], STAT), jnp.bfloat16)
    pos_code = pos_code.at[:, 0].set((positives // 32).astype(jnp.bfloat16))
    pos_code = pos_code.at[:, 1].set((positives % 32).astype(jnp.bfloat16))
    digits = jnp.stack([slots // 16384, (slots // 128) % 128, slots % 128], axis=1)
    code = jnp.zeros((slots.shape[0], STAT), jnp.bfloat16).at[:, :3].set(digits.astype(jnp.bfloat16))
    gathered, fresh_ext = gather_dp(
        jnp.concatenate([queries, pos_code], axis=1),
        jnp.concatenate([fresh_keys, code], axis=1),
        dp_size // 2,
    )
    fresh_ext = fresh_ext.reshape(n * fresh_keys.shape[0], d + STAT)
    total_rows = dp_size * queries.shape[0]
    own_rows = total_rows // n
    gathered = gathered.reshape(total_rows, d + STAT)
    all_queries = gathered[:, :d]
    pos_digits = gathered[:, d:d + 2].astype(jnp.int32)
    all_positives = pos_digits[:, 0] * 32 + pos_digits[:, 1]
    fresh_all = fresh_ext[:, :d]
    got = fresh_ext[:, d:d + 3].astype(jnp.int32)
    slots_all = got[:, 0] * 16384 + got[:, 1] * 128 + got[:, 2]

    device_index = _device_index()
    fresh_padded = jnp.zeros((STAT, d), fresh_keys.dtype).at[:fresh_keys.shape[0]].set(fresh_keys)
    local_pulled, stats = local_partials(gathered, queue_keys, fresh_padded, min(256, total_rows))
    fresh_scores = score_rows(all_queries, fresh_keys)
    fresh_ids = device_index * fresh_keys.shape[0] + jnp.arange(fresh_keys.shape[0], dtype=jnp.int32)
    is_positive = all_positives[:, None] == fresh_ids[None, :]
    positive_total = jnp.sum(jnp.where(is_positive, fresh_scores, 0.0))
    halves = (2, n // 2, own_rows)
    combined, loss_tile = combine(
        local_pulled.reshape(halves + (d,)),
        stats.reshape(halves + (STAT,)),
        jnp.full((8, 128), positive_total, jnp.float32),
        d,
        dp_size // 2,
    )
    sum_rows = combined[:, d + 1]
    pulled = combined[:, :d]
    queue_index = lax.axis_index("queue")
    local_start = queue_index * own_rows
    positive_rows = lax.dynamic_slice_in_dim(positives, local_start, own_rows, 0)
    positive_keys = jnp.take(fresh_all, positive_rows, axis=0).astype(jnp.float32)
    query_grad = pulled / sum_rows[:, None] - positive_keys
    mean_loss = loss_tile[0, 0] / total_rows
    held_rows = queue_keys.shape[0]
    local_slot = slots_all - device_index * held_rows
    inside = (local_slot >= 0) & (local_slot < held_rows)
    spare = held_rows + jnp.arange(local_slot.shape[0], dtype=jnp.int32)
    target = jnp.where(inside, local_slot, spare)
    new_queue = queue_keys.at[target].set(fresh_all, mode="drop", unique_indices=True)
    return (query_grad, mean_loss, new_queue)


def solution(mesh):
    placed = (
        P(("dp", "queue"), None),
        P(("dp", "queue"), None),
        P(("dp", "queue")),
        P("dp", None),
        P("dp"),
    )
    return jax.shard_map(
        shards,
        mesh=mesh,
        in_specs=placed,
        out_specs=(P(("dp", "queue"), None), P(), P(("dp", "queue"), None)),
        check_vma=False,
    )
```

```python
import functools

import jax
import jax.numpy as jnp
from jax import lax
from jax.experimental import pallas as pl
from jax.experimental.pallas import tpu as pltpu
from jax.sharding import PartitionSpec as P

MESH = pl.DeviceIdType.MESH
STAT = 128
FRESH_HELD = 8
KEY_CHUNK = 256


def score_rows(query_rows, key_rows):
    return lax.dot_general(
        query_rows, key_rows, (((1,), (1,)), ((), ())), preferred_element_type=jnp.float32
    )


def _device_index():
    return lax.axis_index("dp") * lax.axis_size("queue") + lax.axis_index("queue")


def _wait_bytes(src, dst, send_sem, recv_sem, device_id):
    total = pltpu.make_async_remote_copy(
        src_ref=src, dst_ref=dst, send_sem=send_sem, recv_sem=recv_sem,
        device_id=device_id, device_id_type=MESH,
    )
    total.wait_send()
    total.wait_recv()


def partial_kernel(q_ref, k_ref, f_ref, p_ref, s_ref):
    q = q_ref[:, :k_ref.shape[1]]
    dims = (((1,), (1,)), ((), ()))
    scores = lax.dot_general(q, k_ref[...], dims, preferred_element_type=jnp.float32)
    fresh = lax.dot_general(q, f_ref[...], dims, preferred_element_type=jnp.float32)
    held = lax.broadcasted_iota(jnp.int32, fresh.shape, 1) < FRESH_HELD
    fresh = jnp.where(held, fresh, -jnp.inf)
    top = jnp.maximum(jnp.max(scores, axis=1, keepdims=True), jnp.max(fresh, axis=1, keepdims=True))
    fresh_weights = jnp.exp(fresh - top)
    total = jnp.sum(fresh_weights, axis=1, keepdims=True)
    acc = jnp.dot(fresh_weights.astype(jnp.bfloat16), f_ref[...], preferred_element_type=jnp.float32)
    chunk = min(KEY_CHUNK, k_ref.shape[0])
    for j in range(k_ref.shape[0] // chunk):
        weights = jnp.exp(scores[:, j * chunk:(j + 1) * chunk] - top)
        total = total + jnp.sum(weights, axis=1, keepdims=True)
        acc = acc + jnp.dot(
            weights.astype(jnp.bfloat16), k_ref[j * chunk:(j + 1) * chunk, :],
            preferred_element_type=jnp.float32,
        )
    p_ref[...] = acc
    col = lax.broadcasted_iota(jnp.int32, s_ref.shape, 1)
    s_ref[...] = jnp.where(col == 0, top, jnp.where(col == 1, total, 0.0))


def local_partials(queries, keys, fresh_padded, block):
    rows, width = queries.shape
    d = keys.shape[1]
    return pl.pallas_call(
        partial_kernel,
        grid=(rows // block,),
        out_shape=(
            jax.ShapeDtypeStruct((rows, d), jnp.float32),
            jax.ShapeDtypeStruct((rows, STAT), jnp.float32),
        ),
        in_specs=[
            pl.BlockSpec((block, width), lambda i: (i, 0)),
            pl.BlockSpec(keys.shape, lambda i: (0, 0)),
            pl.BlockSpec(fresh_padded.shape, lambda i: (0, 0)),
        ],
        out_specs=(
            pl.BlockSpec((block, d), lambda i: (i, 0)),
            pl.BlockSpec((block, STAT), lambda i: (i, 0)),
        ),
        compiler_params=pltpu.CompilerParams(vmem_limit_bytes=60 * 1024 * 1024),
    )(queries, keys, fresh_padded)


def gather_kernel(x_ref, f_ref, o_ref, fo_ref, buf, fbuf, sems):
    dp = lax.axis_index("dp")
    y, c = dp // 2, lax.rem(dp, 2)
    ys = lax.axis_size("dp") // 2
    r = ys
    qi = lax.axis_index("queue")
    mine_at = {"y": y, "z": qi // r, "x": lax.rem(qi, r)}
    partner = (dp + 1 - 2 * c, qi)

    def along(axis, j):
        at = dict(mine_at)
        at[axis] = j
        return (at["y"] * 2 + c, at["z"] * r + at["x"])

    barrier = pltpu.get_barrier_semaphore()
    pl.semaphore_signal(barrier, inc=1, device_id=partner, device_id_type=MESH)
    for axis in ("y", "x", "z"):
        for k in range(1, r):
            pl.semaphore_signal(barrier, inc=1, device_id=along(axis, lax.rem(mine_at[axis] + k, r)),
                                device_id_type=MESH)
    pl.semaphore_wait(barrier, 1 + 3 * (r - 1))

    mine = pltpu.make_async_copy(x_ref, buf.at[c, y], sems.at[4])
    mine.start()
    first = [
        pltpu.make_async_remote_copy(
            src_ref=x_ref, dst_ref=buf.at[c, y], send_sem=sems.at[0], recv_sem=sems.at[1],
            device_id=dst, device_id_type=MESH,
        )
        for dst in [partner] + [along("y", lax.rem(y + k, ys)) for k in range(1, ys)]
    ]
    for copy in first:
        copy.start()

    yi, zi, xi = mine_at["y"], mine_at["z"], mine_at["x"]

    def fresh_round(i, axis, src, dst):
        for k in range(1, r):
            pltpu.make_async_remote_copy(
                src_ref=src, dst_ref=dst, send_sem=sems.at[6 + 2 * i], recv_sem=sems.at[7 + 2 * i],
                device_id=along(axis, lax.rem(mine_at[axis] + k, r)), device_id_type=MESH,
            ).start()

    own_fresh = pltpu.make_async_copy(f_ref, fbuf.at[yi, c, zi, xi], sems.at[5])
    own_fresh.start()
    fresh_round(0, "x", f_ref, fbuf.at[yi, c, zi, xi])
    own_fresh.wait()
    _wait_bytes(fbuf.at[0, 0, 0, pl.ds(0, r - 1)], fbuf.at[0, 0, 0, pl.ds(0, r - 1)],
                sems.at[6], sems.at[7], along("x", lax.rem(xi + 1, r)))
    fresh_round(1, "z", fbuf.at[yi, c, zi], fbuf.at[yi, c, zi])
    _wait_bytes(fbuf.at[0, 0, pl.ds(0, r - 1)], fbuf.at[0, 0, pl.ds(0, r - 1)],
                sems.at[8], sems.at[9], along("z", lax.rem(zi + 1, r)))
    fresh_round(2, "y", fbuf.at[yi, c], fbuf.at[yi, c])

    _wait_bytes(buf.at[0], buf.at[0], sems.at[0], sems.at[1], partner)
    mine.wait()
    second = [
        pltpu.make_async_remote_copy(
            src_ref=buf.at[c, lax.rem(y + k, ys)], dst_ref=buf.at[c, lax.rem(y + k, ys)],
            send_sem=sems.at[2], recv_sem=sems.at[3], device_id=partner, device_id_type=MESH,
        )
        for k in range(1, ys)
    ]
    for copy in second:
        copy.start()
    _wait_bytes(fbuf.at[pl.ds(0, r - 1), 0], fbuf.at[pl.ds(0, r - 1), 0],
                sems.at[10], sems.at[11], along("y", lax.rem(yi + 1, r)))
    for j in range(r):
        pltpu.make_async_remote_copy(
            src_ref=fbuf.at[j, c], dst_ref=fbuf.at[j, c], send_sem=sems.at[12], recv_sem=sems.at[13],
            device_id=partner, device_id_type=MESH,
        ).start()
    _wait_bytes(buf.at[0, pl.ds(0, ys - 1)], buf.at[0, pl.ds(0, ys - 1)], sems.at[2], sems.at[3], partner)
    _wait_bytes(fbuf.at[:, 0], fbuf.at[:, 0], sems.at[12], sems.at[13], partner)
    o_ref[...] = buf[...]
    fo_ref[...] = fbuf[...]


def gather_dp(x, fresh, ys):
    return pl.pallas_call(
        gather_kernel,
        out_shape=(
            jax.ShapeDtypeStruct((2, ys) + x.shape, x.dtype),
            jax.ShapeDtypeStruct((ys, 2, ys, ys) + fresh.shape, fresh.dtype),
        ),
        in_specs=[pl.BlockSpec(memory_space=pltpu.VMEM), pl.BlockSpec(memory_space=pltpu.VMEM)],
        out_specs=(pl.BlockSpec(memory_space=pltpu.VMEM), pl.BlockSpec(memory_space=pltpu.VMEM)),
        scratch_shapes=[
            pltpu.VMEM((2, ys) + x.shape, x.dtype),
            pltpu.VMEM((ys, 2, ys, ys) + fresh.shape, fresh.dtype),
            pltpu.SemaphoreType.DMA((14,)),
        ],
        compiler_params=pltpu.CompilerParams(collective_id=1, has_side_effects=True),
    )(x, fresh)


def _merge(blocks, at):
    top = blocks[0][:, at:at + 1]
    for b in blocks[1:]:
        top = jnp.maximum(top, b[:, at:at + 1])
    acc = blocks[0] * jnp.exp(blocks[0][:, at:at + 1] - top)
    for b in blocks[1:]:
        acc = acc + b * jnp.exp(b[:, at:at + 1] - top)
    col = lax.broadcasted_iota(jnp.int32, acc.shape, 1)
    return jnp.where(col == at, top, acc)


TREES = (("x", "z", "y"), ("z", "y", "x"), ("y", "x", "z"))


def combine_kernel(d, side, p_ref, s_ref, pos_ref, o_ref, loss_ref, own_p, own_s, pair_p, pair_s,
                   send1, recv1, send2, recv2, send3, recv3, loss_buf, loss_pair, sems):
    r = side
    part = d // len(TREES)
    g = p_ref.shape[1]
    dp = lax.axis_index("dp")
    y, c = dp // 2, lax.rem(dp, 2)
    qi = lax.axis_index("queue")
    mine_at = {"y": y, "z": qi // r, "x": lax.rem(qi, r)}
    partner = (dp + 1 - 2 * c, qi)

    def device(at):
        return (at["y"] * 2 + c, at["z"] * r + at["x"])

    def along(axis, j):
        at = dict(mine_at)
        at[axis] = j
        return device(at)

    barrier = pltpu.get_barrier_semaphore()
    pl.semaphore_signal(barrier, inc=1, device_id=partner, device_id_type=MESH)
    for axis in ("x", "z", "y"):
        for k in range(1, r):
            pl.semaphore_signal(barrier, inc=1, device_id=along(axis, lax.rem(mine_at[axis] + k, r)),
                                device_id_type=MESH)
    pl.semaphore_wait(barrier, 1 + 3 * (r - 1))

    pair_copies = [
        pltpu.make_async_remote_copy(
            src_ref=src.at[1 - c], dst_ref=dst, send_sem=sems.at[2 * i], recv_sem=sems.at[2 * i + 1],
            device_id=partner, device_id_type=MESH,
        )
        for i, (src, dst) in enumerate(((p_ref, pair_p), (s_ref, pair_s)))
    ]
    for copy in pair_copies:
        copy.start()
    mine = [pltpu.make_async_copy(src.at[c], dst, sems.at[4 + i])
            for i, (src, dst) in enumerate(((p_ref, own_p), (s_ref, own_s)))]
    for copy in mine:
        copy.start()
    for copy in mine + pair_copies:
        copy.wait()

    def merge_pair(k, carry):
        a, b = own_s[k], pair_s[k]
        top = jnp.maximum(a[:, 0:1], b[:, 0:1])
        wa, wb = jnp.exp(a[:, 0:1] - top), jnp.exp(b[:, 0:1] - top)
        pulled = own_p[k] * wa + pair_p[k] * wb
        col = lax.broadcasted_iota(jnp.int32, a.shape, 1)
        stats = jnp.where(col == 0, top, a * wa + b * wb)
        at = {"y": k // (r * r), "z": lax.rem(k // r, r), "x": lax.rem(k, r)}
        for t, (a1, a2, a3) in enumerate(TREES):
            slot = at[a2] * r + at[a3]
            send1[t, at[a1], slot, :, :part] = pulled[:, t * part:(t + 1) * part]
            send1[t, at[a1], slot, :, part:] = stats
        return carry

    lax.fori_loop(0, g, merge_pair, 0)

    def level(lvl, send, recv, blocks):
        sent = []
        for t, axes in enumerate(TREES):
            axis = axes[lvl]
            me_a = mine_at[axis]
            for k in range(1, r):
                dst = lax.rem(me_a + k, r)
                copy = pltpu.make_async_remote_copy(
                    src_ref=send.at[t, pl.ds(dst * blocks, blocks)], dst_ref=recv.at[t, me_a],
                    send_sem=sems.at[6 + 2 * (3 * lvl + t)], recv_sem=sems.at[7 + 2 * (3 * lvl + t)],
                    device_id=along(axis, dst), device_id_type=MESH,
                )
                copy.start()
            recv[t, me_a] = send[t, pl.ds(me_a * blocks, blocks)]
            sent.append(axis)
        for t, axis in enumerate(sent):
            _wait_bytes(recv.at[t, pl.ds(0, r - 1)], recv.at[t, pl.ds(0, r - 1)],
                        sems.at[6 + 2 * (3 * lvl + t)], sems.at[7 + 2 * (3 * lvl + t)],
                        along(axis, lax.rem(mine_at[axis] + 1, r)))

    def run_level1():
        sent_axes = []
        for t, axes in enumerate(TREES):
            axis = axes[0]
            me_a = mine_at[axis]
            for k in range(1, r):
                dst = lax.rem(me_a + k, r)
                pltpu.make_async_remote_copy(
                    src_ref=send1.at[t, dst], dst_ref=recv1.at[t, me_a],
                    send_sem=sems.at[6 + 2 * t], recv_sem=sems.at[7 + 2 * t],
                    device_id=along(axis, dst), device_id_type=MESH,
                ).start()
            recv1[t, me_a] = send1[t, me_a]
            sent_axes.append(axis)
        for t, axis in enumerate(sent_axes):
            _wait_bytes(send1.at[t, pl.ds(0, r - 1)], recv1.at[t, pl.ds(0, r - 1)],
                        sems.at[6 + 2 * t], sems.at[7 + 2 * t],
                        along(axis, lax.rem(mine_at[axis] + 1, r)))

    run_level1()

    def merge1(b, carry):
        for t in range(len(TREES)):
            send2[t, b] = _merge([recv1[t, i, b] for i in range(r)], part)
        return carry

    lax.fori_loop(0, r * r, merge1, 0)
    level(1, send2, recv2, r)

    for t in range(len(TREES)):
        for a3 in range(r):
            send3[t, a3] = _merge([recv2[t, i, a3] for i in range(r)], part)
    level(2, send3, recv3, 1)

    finals = [_merge([recv3[t, i, 0] for i in range(r)], part) for t in range(len(TREES))]
    stats = finals[0][:, part:]
    for t in range(len(TREES)):
        o_ref[:, t * part:(t + 1) * part] = finals[t][:, :part]
    o_ref[:, d:] = stats
    top = stats[:, 0:1]
    sums = stats[:, 1:2]

    total = jnp.broadcast_to(jnp.sum(top + jnp.log(sums)) - pos_ref[0:1, 0:1], loss_ref.shape)
    for n_axis, axis in enumerate(("x", "z", "y")):
        me_a = mine_at[axis]
        loss_buf[n_axis, me_a] = total
        for k in range(1, r):
            dst = lax.rem(me_a + k, r)
            pltpu.make_async_remote_copy(
                src_ref=loss_buf.at[n_axis, me_a], dst_ref=loss_buf.at[n_axis, me_a],
                send_sem=sems.at[24 + 2 * n_axis], recv_sem=sems.at[25 + 2 * n_axis],
                device_id=along(axis, dst), device_id_type=MESH,
            ).start()
        _wait_bytes(loss_buf.at[n_axis, pl.ds(0, r - 1)], loss_buf.at[n_axis, pl.ds(0, r - 1)],
                    sems.at[24 + 2 * n_axis], sems.at[25 + 2 * n_axis],
                    along(axis, lax.rem(me_a + 1, r)))
        total = loss_buf[n_axis, 0]
        for i in range(1, r):
            total = total + loss_buf[n_axis, i]
    loss_pair[c] = total
    to_pair_loss = pltpu.make_async_remote_copy(
        src_ref=loss_pair.at[c], dst_ref=loss_pair.at[c], send_sem=sems.at[30], recv_sem=sems.at[31],
        device_id=partner, device_id_type=MESH,
    )
    to_pair_loss.start()
    to_pair_loss.wait()
    loss_ref[...] = loss_pair[0] + loss_pair[1]


def combine(pulled, stats, pos, d, side):
    g, rows = pulled.shape[1:3]
    width = d + stats.shape[3]
    trees = len(TREES)
    block = (rows, d // trees + STAT)
    return pl.pallas_call(
        functools.partial(combine_kernel, d, side),
        out_shape=(
            jax.ShapeDtypeStruct((rows, width), jnp.float32),
            jax.ShapeDtypeStruct((8, 128), jnp.float32),
        ),
        in_specs=[
            pl.BlockSpec(memory_space=pl.ANY),
            pl.BlockSpec(memory_space=pl.ANY),
            pl.BlockSpec(memory_space=pltpu.VMEM),
        ],
        out_specs=(
            pl.BlockSpec(memory_space=pltpu.VMEM),
            pl.BlockSpec(memory_space=pltpu.VMEM),
        ),
        scratch_shapes=[
            pltpu.VMEM((g, rows, d), jnp.float32),
            pltpu.VMEM((g, rows, width - d), jnp.float32),
            pltpu.VMEM((g, rows, d), jnp.float32),
            pltpu.VMEM((g, rows, width - d), jnp.float32),
            pltpu.VMEM((trees, side, side * side) + block, jnp.float32),
            pltpu.VMEM((trees, side, side * side) + block, jnp.float32),
            pltpu.VMEM((trees, side * side) + block, jnp.float32),
            pltpu.VMEM((trees, side, side) + block, jnp.float32),
            pltpu.VMEM((trees, side) + block, jnp.float32),
            pltpu.VMEM((trees, side, 1) + block, jnp.float32),
            pltpu.VMEM((3, side, 8, 128), jnp.float32),
            pltpu.VMEM((2, 8, 128), jnp.float32),
            pltpu.SemaphoreType.DMA((32,)),
        ],
        compiler_params=pltpu.CompilerParams(collective_id=0, has_side_effects=True),
    )(pulled, stats, pos)


def shards(queue_keys, fresh_keys, slots, queries, positives):
    dp_size = lax.axis_size("dp")
    queue_size = lax.axis_size("queue")
    n = dp_size * queue_size
    assert fresh_keys.shape[0] == FRESH_HELD
    assert queue_size == (dp_size // 2) ** 2
    d = queries.shape[1]
    pos_code = jnp.zeros((queries.shape[0], STAT), jnp.bfloat16)
    pos_code = pos_code.at[:, 0].set((positives // 32).astype(jnp.bfloat16))
    pos_code = pos_code.at[:, 1].set((positives % 32).astype(jnp.bfloat16))
    digits = jnp.stack([slots // 16384, (slots // 128) % 128, slots % 128], axis=1)
    code = jnp.zeros((slots.shape[0], STAT), jnp.bfloat16).at[:, :3].set(digits.astype(jnp.bfloat16))
    gathered, fresh_ext = gather_dp(
        jnp.concatenate([queries, pos_code], axis=1),
        jnp.concatenate([fresh_keys, code], axis=1),
        dp_size // 2,
    )
    fresh_ext = fresh_ext.reshape(n * fresh_keys.shape[0], d + STAT)
    total_rows = dp_size * queries.shape[0]
    own_rows = total_rows // n
    gathered = gathered.reshape(total_rows, d + STAT)
    all_queries = gathered[:, :d]
    pos_digits = gathered[:, d:d + 2].astype(jnp.int32)
    all_positives = pos_digits[:, 0] * 32 + pos_digits[:, 1]
    fresh_all = fresh_ext[:, :d]
    got = fresh_ext[:, d:d + 3].astype(jnp.int32)
    slots_all = got[:, 0] * 16384 + got[:, 1] * 128 + got[:, 2]

    device_index = _device_index()
    fresh_padded = jnp.zeros((STAT, d), fresh_keys.dtype).at[:fresh_keys.shape[0]].set(fresh_keys)
    local_pulled, stats = local_partials(gathered, queue_keys, fresh_padded, min(256, total_rows))
    fresh_scores = score_rows(all_queries, fresh_keys)
    fresh_ids = device_index * fresh_keys.shape[0] + jnp.arange(fresh_keys.shape[0], dtype=jnp.int32)
    is_positive = all_positives[:, None] == fresh_ids[None, :]
    positive_total = jnp.sum(jnp.where(is_positive, fresh_scores, 0.0))
    halves = (2, n // 2, own_rows)
    combined, loss_tile = combine(
        local_pulled.reshape(halves + (d,)),
        stats.reshape(halves + (STAT,)),
        jnp.full((8, 128), positive_total, jnp.float32),
        d,
        dp_size // 2,
    )
    sum_rows = combined[:, d + 1]
    pulled = combined[:, :d]
    queue_index = lax.axis_index("queue")
    local_start = queue_index * own_rows
    positive_rows = lax.dynamic_slice_in_dim(positives, local_start, own_rows, 0)
    positive_keys = jnp.take(fresh_all, positive_rows, axis=0).astype(jnp.float32)
    query_grad = pulled / sum_rows[:, None] - positive_keys
    mean_loss = loss_tile[0, 0] / total_rows
    held_rows = queue_keys.shape[0]
    local_slot = slots_all - device_index * held_rows
    inside = (local_slot >= 0) & (local_slot < held_rows)
    spare = held_rows + jnp.arange(local_slot.shape[0], dtype=jnp.int32)
    target = jnp.where(inside, local_slot, spare)
    new_queue = queue_keys.at[target].set(fresh_all, mode="drop", unique_indices=True)
    return (query_grad, mean_loss, new_queue)


def solution(mesh):
    placed = (
        P(("dp", "queue"), None),
        P(("dp", "queue"), None),
        P(("dp", "queue")),
        P("dp", None),
        P("dp"),
    )
    return jax.shard_map(
        shards,
        mesh=mesh,
        in_specs=placed,
        out_specs=(P(("dp", "queue"), None), P(), P(("dp", "queue"), None)),
        check_vma=False,
    )
```

```python
import functools

import jax
import jax.numpy as jnp
from jax import lax
from jax.experimental import pallas as pl
from jax.experimental.pallas import tpu as pltpu
from jax.sharding import PartitionSpec as P

MESH = pl.DeviceIdType.MESH
STAT = 128
FRESH_HELD = 8
KEY_CHUNK = 512


def score_rows(query_rows, key_rows):
    return lax.dot_general(
        query_rows, key_rows, (((1,), (1,)), ((), ())), preferred_element_type=jnp.float32
    )


def _device_index():
    return lax.axis_index("dp") * lax.axis_size("queue") + lax.axis_index("queue")


def _wait_bytes(src, dst, send_sem, recv_sem, device_id):
    total = pltpu.make_async_remote_copy(
        src_ref=src, dst_ref=dst, send_sem=send_sem, recv_sem=recv_sem,
        device_id=device_id, device_id_type=MESH,
    )
    total.wait_send()
    total.wait_recv()


def partial_kernel(q_ref, k_ref, f_ref, p_ref, s_ref):
    q = q_ref[:, :k_ref.shape[1]]
    dims = (((1,), (1,)), ((), ()))
    scores = lax.dot_general(q, k_ref[...], dims, preferred_element_type=jnp.float32)
    fresh = lax.dot_general(q, f_ref[...], dims, preferred_element_type=jnp.float32)
    held = lax.broadcasted_iota(jnp.int32, fresh.shape, 1) < FRESH_HELD
    fresh = jnp.where(held, fresh, -jnp.inf)
    top = jnp.maximum(jnp.max(scores, axis=1, keepdims=True), jnp.max(fresh, axis=1, keepdims=True))
    fresh_weights = jnp.exp(fresh - top)
    total = jnp.sum(fresh_weights, axis=1, keepdims=True)
    acc = jnp.dot(fresh_weights.astype(jnp.bfloat16), f_ref[...], preferred_element_type=jnp.float32)
    chunk = min(KEY_CHUNK, k_ref.shape[0])
    for j in range(k_ref.shape[0] // chunk):
        weights = jnp.exp(scores[:, j * chunk:(j + 1) * chunk] - top)
        total = total + jnp.sum(weights, axis=1, keepdims=True)
        acc = acc + jnp.dot(
            weights.astype(jnp.bfloat16), k_ref[j * chunk:(j + 1) * chunk, :],
            preferred_element_type=jnp.float32,
        )
    p_ref[...] = acc
    col = lax.broadcasted_iota(jnp.int32, s_ref.shape, 1)
    s_ref[...] = jnp.where(col == 0, top, jnp.where(col == 1, total, 0.0))


def local_partials(queries, keys, fresh_padded, block):
    rows, width = queries.shape
    d = keys.shape[1]
    return pl.pallas_call(
        partial_kernel,
        grid=(rows // block,),
        out_shape=(
            jax.ShapeDtypeStruct((rows, d), jnp.float32),
            jax.ShapeDtypeStruct((rows, STAT), jnp.float32),
        ),
        in_specs=[
            pl.BlockSpec((block, width), lambda i: (i, 0)),
            pl.BlockSpec(keys.shape, lambda i: (0, 0)),
            pl.BlockSpec(fresh_padded.shape, lambda i: (0, 0)),
        ],
        out_specs=(
            pl.BlockSpec((block, d), lambda i: (i, 0)),
            pl.BlockSpec((block, STAT), lambda i: (i, 0)),
        ),
        compiler_params=pltpu.CompilerParams(vmem_limit_bytes=60 * 1024 * 1024),
    )(queries, keys, fresh_padded)


def gather_kernel(x_ref, f_ref, o_ref, fo_ref, buf, fbuf, sems):
    dp = lax.axis_index("dp")
    y, c = dp // 2, lax.rem(dp, 2)
    ys = lax.axis_size("dp") // 2
    r = ys
    qi = lax.axis_index("queue")
    mine_at = {"y": y, "z": qi // r, "x": lax.rem(qi, r)}
    partner = (dp + 1 - 2 * c, qi)

    def along(axis, j):
        at = dict(mine_at)
        at[axis] = j
        return (at["y"] * 2 + c, at["z"] * r + at["x"])

    barrier = pltpu.get_barrier_semaphore()
    pl.semaphore_signal(barrier, inc=1, device_id=partner, device_id_type=MESH)
    for axis in ("y", "x", "z"):
        for k in range(1, r):
            pl.semaphore_signal(barrier, inc=1, device_id=along(axis, lax.rem(mine_at[axis] + k, r)),
                                device_id_type=MESH)
    pl.semaphore_wait(barrier, 1 + 3 * (r - 1))

    mine = pltpu.make_async_copy(x_ref, buf.at[c, y], sems.at[4])
    mine.start()
    first = [
        pltpu.make_async_remote_copy(
            src_ref=x_ref, dst_ref=buf.at[c, y], send_sem=sems.at[0], recv_sem=sems.at[1],
            device_id=dst, device_id_type=MESH,
        )
        for dst in [partner] + [along("y", lax.rem(y + k, ys)) for k in range(1, ys)]
    ]
    for copy in first:
        copy.start()

    yi, zi, xi = mine_at["y"], mine_at["z"], mine_at["x"]

    def fresh_round(i, axis, src, dst):
        for k in range(1, r):
            pltpu.make_async_remote_copy(
                src_ref=src, dst_ref=dst, send_sem=sems.at[6 + 2 * i], recv_sem=sems.at[7 + 2 * i],
                device_id=along(axis, lax.rem(mine_at[axis] + k, r)), device_id_type=MESH,
            ).start()

    own_fresh = pltpu.make_async_copy(f_ref, fbuf.at[yi, c, zi, xi], sems.at[5])
    own_fresh.start()
    fresh_round(0, "x", f_ref, fbuf.at[yi, c, zi, xi])
    own_fresh.wait()
    _wait_bytes(fbuf.at[0, 0, 0, pl.ds(0, r - 1)], fbuf.at[0, 0, 0, pl.ds(0, r - 1)],
                sems.at[6], sems.at[7], along("x", lax.rem(xi + 1, r)))
    fresh_round(1, "z", fbuf.at[yi, c, zi], fbuf.at[yi, c, zi])
    _wait_bytes(fbuf.at[0, 0, pl.ds(0, r - 1)], fbuf.at[0, 0, pl.ds(0, r - 1)],
                sems.at[8], sems.at[9], along("z", lax.rem(zi + 1, r)))
    fresh_round(2, "y", fbuf.at[yi, c], fbuf.at[yi, c])

    _wait_bytes(buf.at[0], buf.at[0], sems.at[0], sems.at[1], partner)
    mine.wait()
    second = [
        pltpu.make_async_remote_copy(
            src_ref=buf.at[c, lax.rem(y + k, ys)], dst_ref=buf.at[c, lax.rem(y + k, ys)],
            send_sem=sems.at[2], recv_sem=sems.at[3], device_id=partner, device_id_type=MESH,
        )
        for k in range(1, ys)
    ]
    for copy in second:
        copy.start()
    _wait_bytes(fbuf.at[pl.ds(0, r - 1), 0], fbuf.at[pl.ds(0, r - 1), 0],
                sems.at[10], sems.at[11], along("y", lax.rem(yi + 1, r)))
    for j in range(r):
        pltpu.make_async_remote_copy(
            src_ref=fbuf.at[j, c], dst_ref=fbuf.at[j, c], send_sem=sems.at[12], recv_sem=sems.at[13],
            device_id=partner, device_id_type=MESH,
        ).start()
    _wait_bytes(buf.at[0, pl.ds(0, ys - 1)], buf.at[0, pl.ds(0, ys - 1)], sems.at[2], sems.at[3], partner)
    _wait_bytes(fbuf.at[:, 0], fbuf.at[:, 0], sems.at[12], sems.at[13], partner)
    o_ref[...] = buf[...]
    fo_ref[...] = fbuf[...]


def gather_dp(x, fresh, ys):
    return pl.pallas_call(
        gather_kernel,
        out_shape=(
            jax.ShapeDtypeStruct((2, ys) + x.shape, x.dtype),
            jax.ShapeDtypeStruct((ys, 2, ys, ys) + fresh.shape, fresh.dtype),
        ),
        in_specs=[pl.BlockSpec(memory_space=pltpu.VMEM), pl.BlockSpec(memory_space=pltpu.VMEM)],
        out_specs=(pl.BlockSpec(memory_space=pltpu.VMEM), pl.BlockSpec(memory_space=pltpu.VMEM)),
        scratch_shapes=[
            pltpu.VMEM((2, ys) + x.shape, x.dtype),
            pltpu.VMEM((ys, 2, ys, ys) + fresh.shape, fresh.dtype),
            pltpu.SemaphoreType.DMA((14,)),
        ],
        compiler_params=pltpu.CompilerParams(collective_id=1, has_side_effects=True),
    )(x, fresh)


def _merge(blocks, at):
    top = blocks[0][:, at:at + 1]
    for b in blocks[1:]:
        top = jnp.maximum(top, b[:, at:at + 1])
    acc = blocks[0] * jnp.exp(blocks[0][:, at:at + 1] - top)
    for b in blocks[1:]:
        acc = acc + b * jnp.exp(b[:, at:at + 1] - top)
    col = lax.broadcasted_iota(jnp.int32, acc.shape, 1)
    return jnp.where(col == at, top, acc)


TREES = (("x", "z", "y"), ("z", "y", "x"), ("y", "x", "z"))


def combine_kernel(d, side, p_ref, s_ref, pos_ref, o_ref, loss_ref, own_p, own_s, pair_p, pair_s,
                   send1, recv1, send2, recv2, send3, recv3, loss_buf, loss_pair, sems):
    r = side
    part = d // len(TREES)
    g = p_ref.shape[1]
    dp = lax.axis_index("dp")
    y, c = dp // 2, lax.rem(dp, 2)
    qi = lax.axis_index("queue")
    mine_at = {"y": y, "z": qi // r, "x": lax.rem(qi, r)}
    partner = (dp + 1 - 2 * c, qi)

    def device(at):
        return (at["y"] * 2 + c, at["z"] * r + at["x"])

    def along(axis, j):
        at = dict(mine_at)
        at[axis] = j
        return device(at)

    barrier = pltpu.get_barrier_semaphore()
    pl.semaphore_signal(barrier, inc=1, device_id=partner, device_id_type=MESH)
    for axis in ("x", "z", "y"):
        for k in range(1, r):
            pl.semaphore_signal(barrier, inc=1, device_id=along(axis, lax.rem(mine_at[axis] + k, r)),
                                device_id_type=MESH)
    pl.semaphore_wait(barrier, 1 + 3 * (r - 1))

    pair_copies = [
        pltpu.make_async_remote_copy(
            src_ref=src.at[1 - c], dst_ref=dst, send_sem=sems.at[2 * i], recv_sem=sems.at[2 * i + 1],
            device_id=partner, device_id_type=MESH,
        )
        for i, (src, dst) in enumerate(((p_ref, pair_p), (s_ref, pair_s)))
    ]
    for copy in pair_copies:
        copy.start()
    mine = [pltpu.make_async_copy(src.at[c], dst, sems.at[4 + i])
            for i, (src, dst) in enumerate(((p_ref, own_p), (s_ref, own_s)))]
    for copy in mine:
        copy.start()
    for copy in mine + pair_copies:
        copy.wait()

    def merge_pair(k, carry):
        a, b = own_s[k], pair_s[k]
        top = jnp.maximum(a[:, 0:1], b[:, 0:1])
        wa, wb = jnp.exp(a[:, 0:1] - top), jnp.exp(b[:, 0:1] - top)
        pulled = own_p[k] * wa + pair_p[k] * wb
        col = lax.broadcasted_iota(jnp.int32, a.shape, 1)
        stats = jnp.where(col == 0, top, a * wa + b * wb)
        at = {"y": k // (r * r), "z": lax.rem(k // r, r), "x": lax.rem(k, r)}
        for t, (a1, a2, a3) in enumerate(TREES):
            slot = at[a2] * r + at[a3]
            send1[t, at[a1], slot, :, :part] = pulled[:, t * part:(t + 1) * part]
            send1[t, at[a1], slot, :, part:] = stats
        return carry

    lax.fori_loop(0, g, merge_pair, 0)

    def level(lvl, send, recv, blocks):
        sent = []
        for t, axes in enumerate(TREES):
            axis = axes[lvl]
            me_a = mine_at[axis]
            for k in range(1, r):
                dst = lax.rem(me_a + k, r)
                copy = pltpu.make_async_remote_copy(
                    src_ref=send.at[t, pl.ds(dst * blocks, blocks)], dst_ref=recv.at[t, me_a],
                    send_sem=sems.at[6 + 2 * (3 * lvl + t)], recv_sem=sems.at[7 + 2 * (3 * lvl + t)],
                    device_id=along(axis, dst), device_id_type=MESH,
                )
                copy.start()
            recv[t, me_a] = send[t, pl.ds(me_a * blocks, blocks)]
            sent.append(axis)
        for t, axis in enumerate(sent):
            _wait_bytes(recv.at[t, pl.ds(0, r - 1)], recv.at[t, pl.ds(0, r - 1)],
                        sems.at[6 + 2 * (3 * lvl + t)], sems.at[7 + 2 * (3 * lvl + t)],
                        along(axis, lax.rem(mine_at[axis] + 1, r)))

    def run_level1():
        sent_axes = []
        for t, axes in enumerate(TREES):
            axis = axes[0]
            me_a = mine_at[axis]
            for k in range(1, r):
                dst = lax.rem(me_a + k, r)
                pltpu.make_async_remote_copy(
                    src_ref=send1.at[t, dst], dst_ref=recv1.at[t, me_a],
                    send_sem=sems.at[6 + 2 * t], recv_sem=sems.at[7 + 2 * t],
                    device_id=along(axis, dst), device_id_type=MESH,
                ).start()
            recv1[t, me_a] = send1[t, me_a]
            sent_axes.append(axis)
        for t, axis in enumerate(sent_axes):
            _wait_bytes(send1.at[t, pl.ds(0, r - 1)], recv1.at[t, pl.ds(0, r - 1)],
                        sems.at[6 + 2 * t], sems.at[7 + 2 * t],
                        along(axis, lax.rem(mine_at[axis] + 1, r)))

    run_level1()

    def merge1(b, carry):
        for t in range(len(TREES)):
            send2[t, b] = _merge([recv1[t, i, b] for i in range(r)], part)
        return carry

    lax.fori_loop(0, r * r, merge1, 0)
    level(1, send2, recv2, r)

    for t in range(len(TREES)):
        for a3 in range(r):
            send3[t, a3] = _merge([recv2[t, i, a3] for i in range(r)], part)
    level(2, send3, recv3, 1)

    finals = [_merge([recv3[t, i, 0] for i in range(r)], part) for t in range(len(TREES))]
    stats = finals[0][:, part:]
    for t in range(len(TREES)):
        o_ref[:, t * part:(t + 1) * part] = finals[t][:, :part]
    o_ref[:, d:] = stats
    top = stats[:, 0:1]
    sums = stats[:, 1:2]

    total = jnp.broadcast_to(jnp.sum(top + jnp.log(sums)) - pos_ref[0:1, 0:1], loss_ref.shape)
    for n_axis, axis in enumerate(("x", "z", "y")):
        me_a = mine_at[axis]
        loss_buf[n_axis, me_a] = total
        for k in range(1, r):
            dst = lax.rem(me_a + k, r)
            pltpu.make_async_remote_copy(
                src_ref=loss_buf.at[n_axis, me_a], dst_ref=loss_buf.at[n_axis, me_a],
                send_sem=sems.at[24 + 2 * n_axis], recv_sem=sems.at[25 + 2 * n_axis],
                device_id=along(axis, dst), device_id_type=MESH,
            ).start()
        _wait_bytes(loss_buf.at[n_axis, pl.ds(0, r - 1)], loss_buf.at[n_axis, pl.ds(0, r - 1)],
                    sems.at[24 + 2 * n_axis], sems.at[25 + 2 * n_axis],
                    along(axis, lax.rem(me_a + 1, r)))
        total = loss_buf[n_axis, 0]
        for i in range(1, r):
            total = total + loss_buf[n_axis, i]
    loss_pair[c] = total
    to_pair_loss = pltpu.make_async_remote_copy(
        src_ref=loss_pair.at[c], dst_ref=loss_pair.at[c], send_sem=sems.at[30], recv_sem=sems.at[31],
        device_id=partner, device_id_type=MESH,
    )
    to_pair_loss.start()
    to_pair_loss.wait()
    loss_ref[...] = loss_pair[0] + loss_pair[1]


def combine(pulled, stats, pos, d, side):
    g, rows = pulled.shape[1:3]
    width = d + stats.shape[3]
    trees = len(TREES)
    block = (rows, d // trees + STAT)
    return pl.pallas_call(
        functools.partial(combine_kernel, d, side),
        out_shape=(
            jax.ShapeDtypeStruct((rows, width), jnp.float32),
            jax.ShapeDtypeStruct((8, 128), jnp.float32),
        ),
        in_specs=[
            pl.BlockSpec(memory_space=pl.ANY),
            pl.BlockSpec(memory_space=pl.ANY),
            pl.BlockSpec(memory_space=pltpu.VMEM),
        ],
        out_specs=(
            pl.BlockSpec(memory_space=pltpu.VMEM),
            pl.BlockSpec(memory_space=pltpu.VMEM),
        ),
        scratch_shapes=[
            pltpu.VMEM((g, rows, d), jnp.float32),
            pltpu.VMEM((g, rows, width - d), jnp.float32),
            pltpu.VMEM((g, rows, d), jnp.float32),
            pltpu.VMEM((g, rows, width - d), jnp.float32),
            pltpu.VMEM((trees, side, side * side) + block, jnp.float32),
            pltpu.VMEM((trees, side, side * side) + block, jnp.float32),
            pltpu.VMEM((trees, side * side) + block, jnp.float32),
            pltpu.VMEM((trees, side, side) + block, jnp.float32),
            pltpu.VMEM((trees, side) + block, jnp.float32),
            pltpu.VMEM((trees, side, 1) + block, jnp.float32),
            pltpu.VMEM((3, side, 8, 128), jnp.float32),
            pltpu.VMEM((2, 8, 128), jnp.float32),
            pltpu.SemaphoreType.DMA((32,)),
        ],
        compiler_params=pltpu.CompilerParams(collective_id=0, has_side_effects=True),
    )(pulled, stats, pos)


def shards(queue_keys, fresh_keys, slots, queries, positives):
    dp_size = lax.axis_size("dp")
    queue_size = lax.axis_size("queue")
    n = dp_size * queue_size
    assert fresh_keys.shape[0] == FRESH_HELD
    assert queue_size == (dp_size // 2) ** 2
    d = queries.shape[1]
    pos_code = jnp.stack([positives // 32, positives % 32], axis=1).astype(jnp.bfloat16)
    pos_code = jnp.pad(pos_code, ((0, 0), (0, STAT - 2)))
    digits = jnp.stack([slots // 16384, (slots // 128) % 128, slots % 128], axis=1)
    code = jnp.pad(digits.astype(jnp.bfloat16), ((0, 0), (0, STAT - 3)))
    gathered, fresh_ext = gather_dp(
        jnp.concatenate([queries, pos_code], axis=1),
        jnp.concatenate([fresh_keys, code], axis=1),
        dp_size // 2,
    )
    fresh_ext = fresh_ext.reshape(n * fresh_keys.shape[0], d + STAT)
    total_rows = dp_size * queries.shape[0]
    own_rows = total_rows // n
    gathered = gathered.reshape(total_rows, d + STAT)
    all_queries = gathered[:, :d]
    pos_digits = gathered[:, d:d + 2].astype(jnp.int32)
    all_positives = pos_digits[:, 0] * 32 + pos_digits[:, 1]
    fresh_all = fresh_ext[:, :d]
    got = fresh_ext[:, d:d + 3].astype(jnp.int32)
    slots_all = got[:, 0] * 16384 + got[:, 1] * 128 + got[:, 2]

    device_index = _device_index()
    fresh_padded = jnp.pad(fresh_keys, ((0, STAT - fresh_keys.shape[0]), (0, 0)))
    local_pulled, stats = local_partials(gathered, queue_keys, fresh_padded, min(256, total_rows))
    fresh_scores = score_rows(all_queries, fresh_keys)
    fresh_ids = device_index * fresh_keys.shape[0] + jnp.arange(fresh_keys.shape[0], dtype=jnp.int32)
    is_positive = all_positives[:, None] == fresh_ids[None, :]
    positive_total = jnp.sum(jnp.where(is_positive, fresh_scores, 0.0))
    halves = (2, n // 2, own_rows)
    combined, loss_tile = combine(
        local_pulled.reshape(halves + (d,)),
        stats.reshape(halves + (STAT,)),
        jnp.full((8, 128), positive_total, jnp.float32),
        d,
        dp_size // 2,
    )
    sum_rows = combined[:, d + 1]
    pulled = combined[:, :d]
    queue_index = lax.axis_index("queue")
    local_start = queue_index * own_rows
    positive_rows = lax.dynamic_slice_in_dim(positives, local_start, own_rows, 0)
    positive_keys = jnp.take(fresh_all, positive_rows, axis=0).astype(jnp.float32)
    query_grad = pulled / sum_rows[:, None] - positive_keys
    mean_loss = loss_tile[0, 0] / total_rows
    held_rows = queue_keys.shape[0]
    local_slot = slots_all - device_index * held_rows
    inside = (local_slot >= 0) & (local_slot < held_rows)
    spare = held_rows + jnp.arange(local_slot.shape[0], dtype=jnp.int32)
    target = jnp.where(inside, local_slot, spare)
    new_queue = queue_keys.at[target].set(fresh_all, mode="drop", unique_indices=True)
    return (query_grad, mean_loss, new_queue)


def solution(mesh):
    placed = (
        P(("dp", "queue"), None),
        P(("dp", "queue"), None),
        P(("dp", "queue")),
        P("dp", None),
        P("dp"),
    )
    return jax.shard_map(
        shards,
        mesh=mesh,
        in_specs=placed,
        out_specs=(P(("dp", "queue"), None), P(), P(("dp", "queue"), None)),
        check_vma=False,
    )
```

```python
import functools

import jax
import jax.numpy as jnp
from jax import lax
from jax.experimental import pallas as pl
from jax.experimental.pallas import tpu as pltpu
from jax.sharding import PartitionSpec as P

MESH = pl.DeviceIdType.MESH
STAT = 128
FRESH_HELD = 8
KEY_CHUNK = 512


def score_rows(query_rows, key_rows):
    return lax.dot_general(
        query_rows, key_rows, (((1,), (1,)), ((), ())), preferred_element_type=jnp.float32
    )


def _device_index():
    return lax.axis_index("dp") * lax.axis_size("queue") + lax.axis_index("queue")


def _wait_bytes(src, dst, send_sem, recv_sem, device_id):
    total = pltpu.make_async_remote_copy(
        src_ref=src, dst_ref=dst, send_sem=send_sem, recv_sem=recv_sem,
        device_id=device_id, device_id_type=MESH,
    )
    total.wait_send()
    total.wait_recv()


def partial_kernel(q_ref, k_ref, f_ref, p_ref, s_ref):
    q = q_ref[:, :k_ref.shape[1]]
    dims = (((1,), (1,)), ((), ()))
    scores = lax.dot_general(q, k_ref[...], dims, preferred_element_type=jnp.float32)
    fresh = lax.dot_general(q, f_ref[...], dims, preferred_element_type=jnp.float32)
    held = lax.broadcasted_iota(jnp.int32, fresh.shape, 1) < FRESH_HELD
    fresh = jnp.where(held, fresh, -jnp.inf)
    top = jnp.maximum(jnp.max(scores, axis=1, keepdims=True), jnp.max(fresh, axis=1, keepdims=True))
    fresh_weights = jnp.exp(fresh - top)
    total = jnp.sum(fresh_weights, axis=1, keepdims=True)
    acc = jnp.dot(fresh_weights.astype(jnp.bfloat16), f_ref[...], preferred_element_type=jnp.float32)
    chunk = min(KEY_CHUNK, k_ref.shape[0])
    for j in range(k_ref.shape[0] // chunk):
        weights = jnp.exp(scores[:, j * chunk:(j + 1) * chunk] - top)
        total = total + jnp.sum(weights, axis=1, keepdims=True)
        acc = acc + jnp.dot(
            weights.astype(jnp.bfloat16), k_ref[j * chunk:(j + 1) * chunk, :],
            preferred_element_type=jnp.float32,
        )
    p_ref[...] = acc
    col = lax.broadcasted_iota(jnp.int32, s_ref.shape, 1)
    s_ref[...] = jnp.where(col == 0, top, jnp.where(col == 1, total, 0.0))


def local_partials(queries, keys, fresh_padded, block):
    rows, width = queries.shape
    d = keys.shape[1]
    return pl.pallas_call(
        partial_kernel,
        grid=(rows // block,),
        out_shape=(
            jax.ShapeDtypeStruct((rows, d), jnp.float32),
            jax.ShapeDtypeStruct((rows, STAT), jnp.float32),
        ),
        in_specs=[
            pl.BlockSpec((block, width), lambda i: (i, 0)),
            pl.BlockSpec(keys.shape, lambda i: (0, 0)),
            pl.BlockSpec(fresh_padded.shape, lambda i: (0, 0)),
        ],
        out_specs=(
            pl.BlockSpec((block, d), lambda i: (i, 0)),
            pl.BlockSpec((block, STAT), lambda i: (i, 0)),
        ),
        compiler_params=pltpu.CompilerParams(vmem_limit_bytes=60 * 1024 * 1024),
    )(queries, keys, fresh_padded)


def gather_kernel(x_ref, f_ref, o_ref, fo_ref, buf, fbuf, sems):
    dp = lax.axis_index("dp")
    y, c = dp // 2, lax.rem(dp, 2)
    ys = lax.axis_size("dp") // 2
    r = ys
    qi = lax.axis_index("queue")
    mine_at = {"y": y, "z": qi // r, "x": lax.rem(qi, r)}
    partner = (dp + 1 - 2 * c, qi)

    def along(axis, j):
        at = dict(mine_at)
        at[axis] = j
        return (at["y"] * 2 + c, at["z"] * r + at["x"])

    barrier = pltpu.get_barrier_semaphore()
    pl.semaphore_signal(barrier, inc=1, device_id=partner, device_id_type=MESH)
    for axis in ("y", "x", "z"):
        for k in range(1, r):
            pl.semaphore_signal(barrier, inc=1, device_id=along(axis, lax.rem(mine_at[axis] + k, r)),
                                device_id_type=MESH)
    pl.semaphore_wait(barrier, 1 + 3 * (r - 1))

    mine = pltpu.make_async_copy(x_ref, buf.at[c, y], sems.at[4])
    mine.start()
    first = [
        pltpu.make_async_remote_copy(
            src_ref=x_ref, dst_ref=buf.at[c, y], send_sem=sems.at[0], recv_sem=sems.at[1],
            device_id=dst, device_id_type=MESH,
        )
        for dst in [partner] + [along("y", lax.rem(y + k, ys)) for k in range(1, ys)]
    ]
    for copy in first:
        copy.start()

    yi, zi, xi = mine_at["y"], mine_at["z"], mine_at["x"]

    def fresh_round(i, axis, src, dst):
        for k in range(1, r):
            pltpu.make_async_remote_copy(
                src_ref=src, dst_ref=dst, send_sem=sems.at[6 + 2 * i], recv_sem=sems.at[7 + 2 * i],
                device_id=along(axis, lax.rem(mine_at[axis] + k, r)), device_id_type=MESH,
            ).start()

    own_fresh = pltpu.make_async_copy(f_ref, fbuf.at[yi, c, zi, xi], sems.at[5])
    own_fresh.start()
    fresh_round(0, "x", f_ref, fbuf.at[yi, c, zi, xi])
    own_fresh.wait()
    _wait_bytes(fbuf.at[0, 0, 0, pl.ds(0, r - 1)], fbuf.at[0, 0, 0, pl.ds(0, r - 1)],
                sems.at[6], sems.at[7], along("x", lax.rem(xi + 1, r)))
    fresh_round(1, "z", fbuf.at[yi, c, zi], fbuf.at[yi, c, zi])
    _wait_bytes(fbuf.at[0, 0, pl.ds(0, r - 1)], fbuf.at[0, 0, pl.ds(0, r - 1)],
                sems.at[8], sems.at[9], along("z", lax.rem(zi + 1, r)))
    fresh_round(2, "y", fbuf.at[yi, c], fbuf.at[yi, c])

    _wait_bytes(buf.at[0], buf.at[0], sems.at[0], sems.at[1], partner)
    mine.wait()
    second = [
        pltpu.make_async_remote_copy(
            src_ref=buf.at[c, lax.rem(y + k, ys)], dst_ref=buf.at[c, lax.rem(y + k, ys)],
            send_sem=sems.at[2], recv_sem=sems.at[3], device_id=partner, device_id_type=MESH,
        )
        for k in range(1, ys)
    ]
    for copy in second:
        copy.start()
    _wait_bytes(fbuf.at[pl.ds(0, r - 1), 0], fbuf.at[pl.ds(0, r - 1), 0],
                sems.at[10], sems.at[11], along("y", lax.rem(yi + 1, r)))
    for j in range(r):
        pltpu.make_async_remote_copy(
            src_ref=fbuf.at[j, c], dst_ref=fbuf.at[j, c], send_sem=sems.at[12], recv_sem=sems.at[13],
            device_id=partner, device_id_type=MESH,
        ).start()
    _wait_bytes(buf.at[0, pl.ds(0, ys - 1)], buf.at[0, pl.ds(0, ys - 1)], sems.at[2], sems.at[3], partner)
    _wait_bytes(fbuf.at[:, 0], fbuf.at[:, 0], sems.at[12], sems.at[13], partner)
    o_ref[...] = buf[...]
    fo_ref[...] = fbuf[...]


def gather_dp(x, fresh, ys):
    return pl.pallas_call(
        gather_kernel,
        out_shape=(
            jax.ShapeDtypeStruct((2, ys) + x.shape, x.dtype),
            jax.ShapeDtypeStruct((ys, 2, ys, ys) + fresh.shape, fresh.dtype),
        ),
        in_specs=[pl.BlockSpec(memory_space=pltpu.VMEM), pl.BlockSpec(memory_space=pltpu.VMEM)],
        out_specs=(pl.BlockSpec(memory_space=pltpu.VMEM), pl.BlockSpec(memory_space=pltpu.VMEM)),
        scratch_shapes=[
            pltpu.VMEM((2, ys) + x.shape, x.dtype),
            pltpu.VMEM((ys, 2, ys, ys) + fresh.shape, fresh.dtype),
            pltpu.SemaphoreType.DMA((14,)),
        ],
        compiler_params=pltpu.CompilerParams(collective_id=1, has_side_effects=True),
    )(x, fresh)


def _merge(blocks, at):
    top = blocks[0][:, at:at + 1]
    for b in blocks[1:]:
        top = jnp.maximum(top, b[:, at:at + 1])
    acc = blocks[0] * jnp.exp(blocks[0][:, at:at + 1] - top)
    for b in blocks[1:]:
        acc = acc + b * jnp.exp(b[:, at:at + 1] - top)
    col = lax.broadcasted_iota(jnp.int32, acc.shape, 1)
    return jnp.where(col == at, top, acc)


TREES = (("x", "z", "y"), ("z", "y", "x"), ("y", "x", "z"))


def combine_kernel(d, side, p_ref, s_ref, pos_ref, o_ref, loss_ref, own_p, own_s, pair_p, pair_s,
                   send1, recv1, send2, recv2, send3, recv3, loss_buf, loss_pair, sems):
    r = side
    part = d // len(TREES)
    g = p_ref.shape[1]
    dp = lax.axis_index("dp")
    y, c = dp // 2, lax.rem(dp, 2)
    qi = lax.axis_index("queue")
    mine_at = {"y": y, "z": qi // r, "x": lax.rem(qi, r)}
    partner = (dp + 1 - 2 * c, qi)

    def device(at):
        return (at["y"] * 2 + c, at["z"] * r + at["x"])

    def along(axis, j):
        at = dict(mine_at)
        at[axis] = j
        return device(at)

    barrier = pltpu.get_barrier_semaphore()
    pl.semaphore_signal(barrier, inc=1, device_id=partner, device_id_type=MESH)
    for axis in ("x", "z", "y"):
        for k in range(1, r):
            pl.semaphore_signal(barrier, inc=1, device_id=along(axis, lax.rem(mine_at[axis] + k, r)),
                                device_id_type=MESH)
    pl.semaphore_wait(barrier, 1 + 3 * (r - 1))

    pair_copies = [
        pltpu.make_async_remote_copy(
            src_ref=src.at[1 - c], dst_ref=dst, send_sem=sems.at[2 * i], recv_sem=sems.at[2 * i + 1],
            device_id=partner, device_id_type=MESH,
        )
        for i, (src, dst) in enumerate(((p_ref, pair_p), (s_ref, pair_s)))
    ]
    for copy in pair_copies:
        copy.start()
    mine = [pltpu.make_async_copy(src.at[c], dst, sems.at[4 + i])
            for i, (src, dst) in enumerate(((p_ref, own_p), (s_ref, own_s)))]
    for copy in mine:
        copy.start()
    for copy in mine + pair_copies:
        copy.wait()

    def merge_pair(k, carry):
        a, b = own_s[k], pair_s[k]
        top = jnp.maximum(a[:, 0:1], b[:, 0:1])
        wa, wb = jnp.exp(a[:, 0:1] - top), jnp.exp(b[:, 0:1] - top)
        pulled = own_p[k] * wa + pair_p[k] * wb
        col = lax.broadcasted_iota(jnp.int32, a.shape, 1)
        stats = jnp.where(col == 0, top, a * wa + b * wb)
        at = {"y": k // (r * r), "z": lax.rem(k // r, r), "x": lax.rem(k, r)}
        for t, (a1, a2, a3) in enumerate(TREES):
            slot = at[a2] * r + at[a3]
            send1[t, at[a1], slot, :, :part] = pulled[:, t * part:(t + 1) * part]
            send1[t, at[a1], slot, :, part:] = stats
        return carry

    lax.fori_loop(0, g, merge_pair, 0)

    def level(lvl, send, recv, blocks):
        sent = []
        for t, axes in enumerate(TREES):
            axis = axes[lvl]
            me_a = mine_at[axis]
            for k in range(1, r):
                dst = lax.rem(me_a + k, r)
                copy = pltpu.make_async_remote_copy(
                    src_ref=send.at[t, pl.ds(dst * blocks, blocks)], dst_ref=recv.at[t, me_a],
                    send_sem=sems.at[6 + 2 * (3 * lvl + t)], recv_sem=sems.at[7 + 2 * (3 * lvl + t)],
                    device_id=along(axis, dst), device_id_type=MESH,
                )
                copy.start()
            recv[t, me_a] = send[t, pl.ds(me_a * blocks, blocks)]
            sent.append(axis)
        for t, axis in enumerate(sent):
            _wait_bytes(recv.at[t, pl.ds(0, r - 1)], recv.at[t, pl.ds(0, r - 1)],
                        sems.at[6 + 2 * (3 * lvl + t)], sems.at[7 + 2 * (3 * lvl + t)],
                        along(axis, lax.rem(mine_at[axis] + 1, r)))

    def run_level1():
        sent_axes = []
        for t, axes in enumerate(TREES):
            axis = axes[0]
            me_a = mine_at[axis]
            for k in range(1, r):
                dst = lax.rem(me_a + k, r)
                pltpu.make_async_remote_copy(
                    src_ref=send1.at[t, dst], dst_ref=recv1.at[t, me_a],
                    send_sem=sems.at[6 + 2 * t], recv_sem=sems.at[7 + 2 * t],
                    device_id=along(axis, dst), device_id_type=MESH,
                ).start()
            recv1[t, me_a] = send1[t, me_a]
            sent_axes.append(axis)
        for t, axis in enumerate(sent_axes):
            _wait_bytes(send1.at[t, pl.ds(0, r - 1)], recv1.at[t, pl.ds(0, r - 1)],
                        sems.at[6 + 2 * t], sems.at[7 + 2 * t],
                        along(axis, lax.rem(mine_at[axis] + 1, r)))

    run_level1()

    def merge1(b, carry):
        for t in range(len(TREES)):
            send2[t, b] = _merge([recv1[t, i, b] for i in range(r)], part)
        return carry

    lax.fori_loop(0, r * r, merge1, 0)
    level(1, send2, recv2, r)

    for t in range(len(TREES)):
        for a3 in range(r):
            send3[t, a3] = _merge([recv2[t, i, a3] for i in range(r)], part)
    level(2, send3, recv3, 1)

    finals = [_merge([recv3[t, i, 0] for i in range(r)], part) for t in range(len(TREES))]
    stats = finals[0][:, part:]
    for t in range(len(TREES)):
        o_ref[:, t * part:(t + 1) * part] = finals[t][:, :part]
    o_ref[:, d:] = stats
    top = stats[:, 0:1]
    sums = stats[:, 1:2]

    total = jnp.broadcast_to(jnp.sum(top + jnp.log(sums)) - pos_ref[0:1, 0:1], loss_ref.shape)
    for n_axis, axis in enumerate(("x", "z", "y")):
        me_a = mine_at[axis]
        loss_buf[n_axis, me_a] = total
        for k in range(1, r):
            dst = lax.rem(me_a + k, r)
            pltpu.make_async_remote_copy(
                src_ref=loss_buf.at[n_axis, me_a], dst_ref=loss_buf.at[n_axis, me_a],
                send_sem=sems.at[24 + 2 * n_axis], recv_sem=sems.at[25 + 2 * n_axis],
                device_id=along(axis, dst), device_id_type=MESH,
            ).start()
        _wait_bytes(loss_buf.at[n_axis, pl.ds(0, r - 1)], loss_buf.at[n_axis, pl.ds(0, r - 1)],
                    sems.at[24 + 2 * n_axis], sems.at[25 + 2 * n_axis],
                    along(axis, lax.rem(me_a + 1, r)))
        total = loss_buf[n_axis, 0]
        for i in range(1, r):
            total = total + loss_buf[n_axis, i]
    loss_pair[c] = total
    to_pair_loss = pltpu.make_async_remote_copy(
        src_ref=loss_pair.at[c], dst_ref=loss_pair.at[c], send_sem=sems.at[30], recv_sem=sems.at[31],
        device_id=partner, device_id_type=MESH,
    )
    to_pair_loss.start()
    to_pair_loss.wait()
    loss_ref[...] = loss_pair[0] + loss_pair[1]


def combine(pulled, stats, pos, d, side):
    g, rows = pulled.shape[1:3]
    width = d + stats.shape[3]
    trees = len(TREES)
    block = (rows, d // trees + STAT)
    return pl.pallas_call(
        functools.partial(combine_kernel, d, side),
        out_shape=(
            jax.ShapeDtypeStruct((rows, width), jnp.float32),
            jax.ShapeDtypeStruct((8, 128), jnp.float32),
        ),
        in_specs=[
            pl.BlockSpec(memory_space=pl.ANY),
            pl.BlockSpec(memory_space=pl.ANY),
            pl.BlockSpec(memory_space=pltpu.VMEM),
        ],
        out_specs=(
            pl.BlockSpec(memory_space=pltpu.VMEM),
            pl.BlockSpec(memory_space=pltpu.VMEM),
        ),
        scratch_shapes=[
            pltpu.VMEM((g, rows, d), jnp.float32),
            pltpu.VMEM((g, rows, width - d), jnp.float32),
            pltpu.VMEM((g, rows, d), jnp.float32),
            pltpu.VMEM((g, rows, width - d), jnp.float32),
            pltpu.VMEM((trees, side, side * side) + block, jnp.float32),
            pltpu.VMEM((trees, side, side * side) + block, jnp.float32),
            pltpu.VMEM((trees, side * side) + block, jnp.float32),
            pltpu.VMEM((trees, side, side) + block, jnp.float32),
            pltpu.VMEM((trees, side) + block, jnp.float32),
            pltpu.VMEM((trees, side, 1) + block, jnp.float32),
            pltpu.VMEM((3, side, 8, 128), jnp.float32),
            pltpu.VMEM((2, 8, 128), jnp.float32),
            pltpu.SemaphoreType.DMA((32,)),
        ],
        compiler_params=pltpu.CompilerParams(collective_id=0, has_side_effects=True),
    )(pulled, stats, pos)


def shards(queue_keys, fresh_keys, slots, queries, positives):
    dp_size = lax.axis_size("dp")
    queue_size = lax.axis_size("queue")
    n = dp_size * queue_size
    assert fresh_keys.shape[0] == FRESH_HELD
    assert queue_size == (dp_size // 2) ** 2
    d = queries.shape[1]
    pos_code = jnp.stack([positives // 32, positives % 32], axis=1).astype(jnp.bfloat16)
    pos_code = jnp.pad(pos_code, ((0, 0), (0, STAT - 2)))
    digits = jnp.stack([slots // 16384, (slots // 128) % 128, slots % 128], axis=1)
    code = jnp.pad(digits.astype(jnp.bfloat16), ((0, 0), (0, STAT - 3)))
    gathered, fresh_ext = gather_dp(
        jnp.concatenate([queries, pos_code], axis=1),
        jnp.concatenate([fresh_keys, code], axis=1),
        dp_size // 2,
    )
    fresh_ext = fresh_ext.reshape(n * fresh_keys.shape[0], d + STAT)
    total_rows = dp_size * queries.shape[0]
    own_rows = total_rows // n
    gathered = gathered.reshape(total_rows, d + STAT)
    all_queries = gathered[:, :d]
    pos_digits = gathered[:, d:d + 2].astype(jnp.int32)
    all_positives = pos_digits[:, 0] * 32 + pos_digits[:, 1]
    fresh_all = fresh_ext[:, :d]
    got = fresh_ext[:, d:d + 3].astype(jnp.int32)
    slots_all = got[:, 0] * 16384 + got[:, 1] * 128 + got[:, 2]

    device_index = _device_index()
    fresh_padded = jnp.pad(fresh_keys, ((0, STAT - fresh_keys.shape[0]), (0, 0)))
    local_pulled, stats = local_partials(gathered, queue_keys, fresh_padded, min(256, total_rows))
    fresh_scores = score_rows(all_queries, fresh_keys)
    fresh_ids = device_index * fresh_keys.shape[0] + jnp.arange(fresh_keys.shape[0], dtype=jnp.int32)
    is_positive = all_positives[:, None] == fresh_ids[None, :]
    positive_total = jnp.sum(jnp.where(is_positive, fresh_scores, 0.0))
    halves = (2, n // 2, own_rows)
    combined, loss_tile = combine(
        local_pulled.reshape(halves + (d,)),
        stats.reshape(halves + (STAT,)),
        positive_total.reshape(1, 1),
        d,
        dp_size // 2,
    )
    sum_rows = combined[:, d + 1]
    pulled = combined[:, :d]
    queue_index = lax.axis_index("queue")
    local_start = queue_index * own_rows
    positive_rows = lax.dynamic_slice_in_dim(positives, local_start, own_rows, 0)
    positive_keys = jnp.take(fresh_all, positive_rows, axis=0).astype(jnp.float32)
    query_grad = pulled / sum_rows[:, None] - positive_keys
    mean_loss = loss_tile[0, 0] / total_rows
    held_rows = queue_keys.shape[0]
    local_slot = slots_all - device_index * held_rows
    inside = (local_slot >= 0) & (local_slot < held_rows)
    spare = held_rows + jnp.arange(local_slot.shape[0], dtype=jnp.int32)
    target = jnp.where(inside, local_slot, spare)
    new_queue = queue_keys.at[target].set(fresh_all, mode="drop", unique_indices=True)
    return (query_grad, mean_loss, new_queue)


def solution(mesh):
    placed = (
        P(("dp", "queue"), None),
        P(("dp", "queue"), None),
        P(("dp", "queue")),
        P("dp", None),
        P("dp"),
    )
    return jax.shard_map(
        shards,
        mesh=mesh,
        in_specs=placed,
        out_specs=(P(("dp", "queue"), None), P(), P(("dp", "queue"), None)),
        check_vma=False,
    )
```
